32 devices in a mesh: rep: 2 (over x), grp: 16 (over z, y, core).
Axes of the slice: x: 2, y: 2, z: 4, core: 2. Of those that a mesh axis runs over, the one named last changes fastest.
Arguments:
- tokens: bfloat16 [4096, 1280], P(('rep', 'grp')), may hold values from -6 to 6
- segments: int32 [32, 128], P(('rep', 'grp')), may hold values from 0 to 3, never falling along the last dimension, each value on 1 to 64 neighbouring positions
- routes: int32 [4096, 7], P(('rep', 'grp')), may hold values from 0 to 15, all different within a row
- gates: float32 [4096, 7], P(('rep', 'grp')), may hold values from 0.08 to 0.22
- gain_attn: bfloat16 [1280], P('grp'), may hold values from 0.5 to 1.5
- w_qkv: bfloat16 [1280, 3840], P('grp'), may hold values from -0.15625 to 0.15625
- w_out: bfloat16 [1280, 1280], P(None, 'grp'), may hold values from -0.625 to 0.625
- gain_ffn: bfloat16 [1280], P('grp'), may hold values from 0.5 to 1.5
- shared_gate: bfloat16 [1280, 896], P('grp'), may hold values from -0.15625 to 0.15625
- shared_up: bfloat16 [1280, 896], P('grp'), may hold values from -0.15625 to 0.15625
- shared_down: bfloat16 [896, 1280], P(None, 'grp'), may hold values from -0.375 to 0.375
- route_gate: bfloat16 [16, 1280, 896], P('grp'), may hold values from -0.15625 to 0.15625
- route_up: bfloat16 [16, 1280, 896], P('grp'), may hold values from -0.15625 to 0.15625
- route_down: bfloat16 [16, 896, 1280], P('grp'), may hold values from -0.5 to 0.5
- cotangent: bfloat16 [4096, 1280], P(('rep', 'grp')), may hold values from -6 to 6
Outputs:
- mixed: bfloat16 [4096, 1280], P(('rep', 'grp'))
- grad_tokens: bfloat16 [4096, 1280], P(('rep', 'grp'))
- grad_gain_attn: float32 [1280], P('grp')
- grad_w_qkv: float32 [1280, 3840], P('grp')
- grad_w_out: float32 [1280, 1280], P(None, 'grp')
- grad_gain_ffn: float32 [1280], P('grp')
- grad_shared_gate: float32 [1280, 896], P('grp')
- grad_shared_up: float32 [1280, 896], P('grp')
- grad_shared_down: float32 [896, 1280], P(None, 'grp')
- grad_route_gate: float32 [16, 1280, 896], P('grp')
- grad_route_up: float32 [16, 1280, 896], P('grp')
- grad_route_down: float32 [16, 896, 1280], P('grp')
The draws below stay inside these ranges and needn't reach their ends.
Inputs may be any that keep to these rules, and one draw needn't show every extreme that they name: `routes`: each token names 7 different experts. `segments`: document numbers never fall along a sequence; a document holds 1 to 64 positions.
All inputs are finite; a program needn't handle non-finite values.
Results may differ from the reference program's by a relative error of at most 0.023.
Values may be sent and summed in bfloat16 or wider, within the bound.
No kernel may reach another device: no remote copies, remote signals or barrier semaphores. Data moves between devices by JAX's collectives and lax.ppermute only.
A program may use at most 192 MiB of HBM per device.

```python
import math
import jax
import jax.numpy as jnp
import numpy as np
from jax import lax

D = 1280
H = 10
HD = 128
FFE = 896
TOPK = 7
TOK_DEV = 128
LENGTH = 128
SEQS = 32
TOKENS = 4096
EXPERTS = 16
CAP = 63
DOCS = 4


def shard_levels(stream_key, extent, pieces, low, top_value):
    def one(dim, blocks):
        draws = jax.random.uniform(jax.random.fold_in(jax.random.fold_in(stream_key, 6), dim), (blocks,), jnp.float32, low / len(pieces), top_value / len(pieces))
        return jnp.repeat(jnp.exp(draws), extent[dim] // blocks).reshape((-1,) + (1,) * (len(extent) - dim - 1))

    factor_of = one(*pieces[0])
    for cut in pieces[1:]:
        factor_of = factor_of * one(*cut)
    return factor_of


def distinct(own_key, rows, number_of, top, lift):
    sequence = jax.random.permutation(jax.random.fold_in(own_key, 1), number_of)
    boost = sequence
    for power in range(3):
        boost = boost * boost // number_of
    boost = boost * lift // number_of
    lots = jax.random.randint(jax.random.fold_in(own_key, 2), (rows, number_of), 0, 4096) + boost
    holders = jax.random.permutation(jax.random.fold_in(own_key, 3), rows)[jnp.arange(number_of) % rows]
    lots = jnp.where(jnp.arange(rows)[:, None] == holders[None, :], 1 << 14, lots)
    priority = lots * number_of + jnp.arange(number_of)
    return lax.top_k(priority.astype(jnp.int32), top)[1].astype(jnp.int32)


def length_profile(number_of, total, bound, lean):
    loads = [(1 << 20) // math.isqrt(grade ** lean) + 1 for grade in range(2, number_of + 1)]
    surplus, holding = total - bound - (number_of - 1), [1] * (number_of - 1)
    while surplus > 0:
        movable = [i for i in range(number_of - 1) if holding[i] < bound]
        pool, budget = sum([loads[i] for i in movable]), surplus
        for i in movable:
            extra = min(bound - holding[i], max(1, budget * loads[i] // pool), surplus)
            holding[i] = holding[i] + extra
            surplus = surplus - extra
    return np.array([bound] + holding)


def ragged_sizes(stream_key, number_of, total, limit, slope):
    if number_of == 2:
        one = jax.random.randint(stream_key, (), max(1, total - limit), min(limit, total - 1) + 1)
        return jnp.stack([one, total - one])
    lengths = jnp.asarray(length_profile(number_of, total, limit, slope), jnp.int32)
    twos = (number_of - 1) // 2
    source_of, receiver = lengths[1:1 + 2 * twos:2], lengths[2:2 + 2 * twos:2]
    room = jnp.minimum(source_of - 1, limit - receiver)
    passed = jax.random.randint(jax.random.fold_in(stream_key, 1), (twos,), 0, 1 << 20) % (room + 1)
    lengths = lengths.at[1:1 + 2 * twos:2].set(source_of - passed).at[2:2 + 2 * twos:2].set(receiver + passed)
    return lengths[jax.random.permutation(jax.random.fold_in(stream_key, 2), number_of)]


def normal_values(rng, extent, scale, bound, shards=(), kind=jnp.bfloat16):
    values = jax.random.normal(rng, extent, jnp.float32) * scale
    if len(shards) > 0:
        values = shard_levels(rng, extent, shards, -0.22, 0.18) * values
    return jnp.clip(values, min=-bound, max=bound).astype(kind)


def setup_inputs(seed: int = 0) -> dict:
    keys = jax.random.split(jax.random.key(seed), 16)
    return {
        "tokens": normal_values(keys[0], (TOKENS, D), 1.0, 6.0, ((0, 32),)),
        "segments": jax.vmap(lambda own: jnp.searchsorted(jnp.cumsum(ragged_sizes(own, DOCS, LENGTH, TOK_DEV // 2, 2)), jnp.arange(LENGTH), side="right"))(jax.random.split(keys[1], SEQS)).reshape((SEQS, LENGTH)).astype(jnp.int32),
        "routes": distinct(keys[2], TOKENS, EXPERTS, TOPK, 3584),
        "gates": jnp.clip(0.08 + 0.14 * jax.random.uniform(keys[3], (TOKENS, TOPK), jnp.float32) ** shard_levels(keys[3], (TOKENS, TOPK), ((0, 32),), -0.2, 0.2), 0.08, 0.22),
        "gain_attn": jnp.clip(1.0 + 0.1 * jax.random.normal(keys[4], (D,), jnp.float32), 0.5, 1.5).astype(jnp.bfloat16),
        "w_qkv": normal_values(keys[5], (D, 3 * H * HD), D ** -0.5, 0.15625, ((0, 16),)),
        "w_out": normal_values(keys[6], (H * HD, D), (H * HD // 16) ** -0.5, 0.625, ((1, 16),)),
        "gain_ffn": jnp.clip(1.0 + 0.1 * jax.random.normal(keys[7], (D,), jnp.float32), 0.5, 1.5).astype(jnp.bfloat16),
        "shared_gate": normal_values(keys[8], (D, FFE), D ** -0.5, 0.15625, ((0, 16),)),
        "shared_up": normal_values(keys[9], (D, FFE), D ** -0.5, 0.15625, ((0, 16),)),
        "shared_down": normal_values(keys[10], (FFE, D), (FFE // 4) ** -0.5, 0.375, ((1, 16),)),
        "route_gate": normal_values(keys[11], (EXPERTS, D, FFE), D ** -0.5, 0.15625, ((0, 16),)),
        "route_up": normal_values(keys[12], (EXPERTS, D, FFE), D ** -0.5, 0.15625, ((0, 16),)),
        "route_down": normal_values(keys[13], (EXPERTS, FFE, D), (FFE // 8) ** -0.5, 0.5, ((0, 16),)),
        "cotangent": normal_values(keys[14], (TOKENS, D), 1.0, 6.0, ((0, 32),)),
    }


EPSILON = 1e-06
MASKED_SCORE = -1000000000.0
HIGHEST = lax.Precision.HIGHEST

@jax.custom_vjp
def low(v):
    return lax.optimization_barrier(v.astype(jnp.bfloat16)).astype(jnp.float32)

@jax.custom_vjp
def low_back(v):
    return v

def low_keep(v):
    return (low(v), None)

def low_pass(kept, grad):
    return (grad,)

def back_keep(v):
    return (v, None)

def back_low(kept, grad):
    return (low(grad),)
low.defvjp(low_keep, low_pass)
low_back.defvjp(back_keep, back_low)

def matmul(left, right):
    return jnp.dot(left, right, precision=HIGHEST, preferred_element_type=jnp.float32)

def rms_scale(values):
    return lax.rsqrt(lax.optimization_barrier(jnp.mean(values * values, axis=-1, keepdims=True)) + EPSILON)

def rotary_tables(seq_len, head_size):
    half = head_size // 2
    frequency = jnp.power(jnp.float32(10000.0), -2.0 * jnp.arange(half, dtype=jnp.float32) / head_size)
    angle = jnp.arange(seq_len, dtype=jnp.float32)[:, None] * frequency[None, :]
    return (jnp.cos(angle)[:, None, :], jnp.sin(angle)[:, None, :])

def rotate(values, cosine, sine):
    half = values.shape[-1] // 2
    first, second = (values[..., :half], values[..., half:])
    return jnp.concatenate([first * cosine - second * sine, second * cosine + first * sine], axis=-1)

def slot_table(route_rows):
    flat_ids = route_rows.reshape(-1).astype(jnp.int32)
    pair_count = flat_ids.shape[0]
    one_hot = (flat_ids[:, None] == jnp.arange(EXPERTS, dtype=jnp.int32)[None, :]).astype(jnp.int32)
    position = lax.optimization_barrier(jnp.sum((jnp.cumsum(one_hot, axis=0) - 1) * one_hot, axis=1))
    slot_index = jnp.where(position < CAP, flat_ids * CAP + position, EXPERTS * CAP).astype(jnp.int32)
    source_pair = jnp.full((EXPERTS * CAP,), pair_count, jnp.int32).at[slot_index].set(jnp.arange(pair_count, dtype=jnp.int32), mode='drop')
    return (slot_index, source_pair)

def block(params, rows, segment_ids, route_rows, gate_rows):
    gain_attn, w_qkv, w_out, gain_ffn, shared_gate, shared_up, shared_down, route_gate, route_up, route_down = params
    seq_len = rows.shape[0]
    inner = H * HD
    attn_in = low(rows * rms_scale(rows) * gain_attn)
    projected = low_back(matmul(attn_in, w_qkv))
    cosine, sine = rotary_tables(seq_len, HD)
    query_rows = low(rotate(projected[:, :inner].reshape(seq_len, H, HD), cosine, sine))
    key_rows = low(rotate(projected[:, inner:2 * inner].reshape(seq_len, H, HD), cosine, sine))
    value_rows = low(projected[:, 2 * inner:].reshape(seq_len, H, HD))
    places = jnp.arange(seq_len, dtype=jnp.int32)
    allowed = (places[:, None] >= places[None, :]) & (segment_ids[:, None] == segment_ids[None, :])
    scores = jnp.einsum('shd,thd->hst', query_rows, key_rows, precision=HIGHEST) / math.sqrt(HD)
    scores = low_back(jnp.where(allowed[None], scores, MASKED_SCORE))
    weights = low(jax.nn.softmax(scores, axis=-1))
    heads_out = jnp.einsum('hst,thd->shd', weights, value_rows, precision=HIGHEST).reshape(seq_len, inner)
    attn_rows = low(low_back(heads_out))
    residual = rows + low_back(matmul(attn_rows, w_out))
    ffn_in = low(residual * rms_scale(residual) * gain_ffn)
    gate_pre = low_back(matmul(ffn_in, shared_gate))
    up_pre = low_back(matmul(ffn_in, shared_up))
    shared_out = low_back(matmul(low(jax.nn.silu(gate_pre) * up_pre), shared_down))
    slot_index, source_pair = slot_table(route_rows)
    pair_count = seq_len * TOPK
    filled = source_pair < pair_count
    token_of = jnp.minimum(source_pair, pair_count - 1) // TOPK
    expert_in = low_back(jnp.where(filled[:, None], ffn_in[token_of], 0.0)).reshape(EXPERTS, CAP, D)
    expert_gate = low_back(jnp.einsum('ecd,edf->ecf', expert_in, route_gate, precision=HIGHEST))
    expert_up = low_back(jnp.einsum('ecd,edf->ecf', expert_in, route_up, precision=HIGHEST))
    expert_hidden = low(jax.nn.silu(expert_gate) * expert_up)
    expert_out = low(low_back(jnp.einsum('ecf,efd->ecd', expert_hidden, route_down, precision=HIGHEST)))
    padded = jnp.concatenate([expert_out.reshape(EXPERTS * CAP, D), jnp.zeros((1, D), jnp.float32)], axis=0)
    routed = (padded[slot_index] * gate_rows.reshape(-1)[:, None]).reshape(seq_len, TOPK, D).sum(axis=1)
    return residual + shared_out + routed

def reference(tokens, segments, routes, gates, gain_attn, w_qkv, w_out, gain_ffn, shared_gate, shared_up, shared_down, route_gate, route_up, route_down, cotangent):
    params = tuple((item.astype(jnp.float32) for item in (gain_attn, w_qkv, w_out, gain_ffn, shared_gate, shared_up, shared_down, route_gate, route_up, route_down)))
    rows_in = tokens.astype(jnp.float32)
    route_blocks = routes.reshape(SEQS, TOK_DEV, TOPK)
    gate_blocks = gates.astype(jnp.float32).reshape(SEQS, TOK_DEV, TOPK)

    def forward(rows_all, weights_all):

        def one_block(item):
            return jax.checkpoint(block)(weights_all, item[0], item[1], item[2], item[3])
        result = lax.map(one_block, (rows_all.reshape(SEQS, TOK_DEV, D), segments, route_blocks, gate_blocks))
        return result.reshape(TOKENS, D)
    output, pull = jax.vjp(forward, rows_in, params)
    grad_rows, grad_params = pull(cotangent.astype(jnp.float32))
    return (output.astype(jnp.bfloat16), grad_rows.astype(jnp.bfloat16), grad_params[0], grad_params[1], grad_params[2], grad_params[3], grad_params[4], grad_params[5], grad_params[6], grad_params[7], grad_params[8], grad_params[9])
```

```python
import math

import jax
import jax.numpy as jnp
from jax import lax
from jax.sharding import PartitionSpec as P

H = 10
HD = 128

EPSILON = 1e-06
MASKED_SCORE = -1000000000.0
BF = jnp.bfloat16
F32 = jnp.float32


def rms_scale(values):
    return lax.rsqrt(jnp.mean(values * values, axis=-1, keepdims=True) + EPSILON)


def rotary_tables(seq_len, head_size):
    half = head_size // 2
    frequency = jnp.power(
        jnp.float32(10000.0), -2.0 * jnp.arange(half, dtype=jnp.float32) / head_size
    )
    angle = jnp.arange(seq_len, dtype=jnp.float32)[:, None] * frequency[None, :]
    return (jnp.cos(angle)[:, None, :], jnp.sin(angle)[:, None, :])


def rotate(values, cosine, sine):
    half = values.shape[-1] // 2
    first, second = (values[..., :half], values[..., half:])
    return jnp.concatenate(
        [first * cosine - second * sine, second * cosine + first * sine], axis=-1
    )


def unrotate(grads, cosine, sine):
    half = grads.shape[-1] // 2
    first, second = (grads[..., :half], grads[..., half:])
    return jnp.concatenate(
        [first * cosine + second * sine, second * cosine - first * sine], axis=-1
    )


def contract(left, right, left_dim, right_dim):
    return lax.dot_general(
        left, right, (((left_dim,), (right_dim,)), ((), ())), preferred_element_type=F32
    )


def silu_slope(values):
    sigma = jax.nn.sigmoid(values)
    return sigma * (1.0 + values * (1.0 - sigma))


def norm_backward(grad_scaled, normed, inverse, gain):
    grad_normed = grad_scaled * gain
    grad_gain = jnp.sum(grad_scaled * normed, axis=0)
    grad_rows = inverse * (
        grad_normed - normed * jnp.mean(grad_normed * normed, axis=-1, keepdims=True)
    )
    return (grad_rows, grad_gain)


class Grid:
    def __init__(self):
        self.size = lax.axis_size("grp")
        self.reps = lax.axis_size("rep")
        self.c = 2 if self.size % 2 == 0 else 1
        self.z = 4 if self.size % (4 * self.c) == 0 else 1
        self.y = self.size // (self.c * self.z)
        me = lax.axis_index("grp")
        self.my_c = me % self.c
        self.my_y = me // self.c % self.y
        self.my_z = me // (self.c * self.y)

    def flat(self, z, y, c):
        return (z % self.z * self.y + y % self.y) * self.c + c % self.c

    def shift(self, value, dz, dy, dc):
        pairs = [
            (self.flat(z, y, c), self.flat(z + dz, y + dy, c + dc))
            for z in range(self.z)
            for y in range(self.y)
            for c in range(self.c)
        ]
        return lax.ppermute(value, "grp", pairs)

    def order(self):
        return [(i, j, k) for i in range(self.z) for j in range(self.y) for k in range(self.c)]

    def source(self, step):
        return self.flat(
            self.my_z - step[0] + self.z, self.my_y - step[1] + self.y, self.my_c - step[2] + self.c
        )

    def gather(self, block):
        held = {(0, 0, 0): block}
        for i in range(1, self.z):
            held[(i, 0, 0)] = self.shift(held[(i - 1, 0, 0)], 1, 0, 0)
        for i in range(self.z):
            for j in range(1, self.y):
                held[(i, j, 0)] = self.shift(held[(i, j - 1, 0)], 0, 1, 0)
        for i in range(self.z):
            for j in range(self.y):
                for k in range(1, self.c):
                    held[(i, j, k)] = self.shift(held[(i, j, k - 1)], 0, 0, 1)
        return held

    def ring(self, terms, dim):
        count = len(terms)
        if count == 1:
            return terms[0]
        move = [0, 0, 0]
        move[dim] = 1
        total = terms[1]
        for s in range(2, count + 1):
            arrived = self.shift(total, *move)
            total = (arrived.astype(F32) + terms[s % count].astype(F32)).astype(BF)
        return total

    def scatter_relative(self, parts):
        by_core = {
            (i, j): self.ring([parts[(i, j, k)] for k in range(self.c)], 2)
            for i in list(range(1, self.z)) + [0]
            for j in range(self.y)
        }
        by_y = {
            i: self.ring([by_core[(i, j)] for j in range(self.y)], 1)
            for i in list(range(1, self.z)) + [0]
        }
        return self.ring([by_y[i] for i in range(self.z)], 0)

    def scatter_rows(self, whole):
        rows = whole.shape[0] // self.size
        cut = whole.reshape(self.z, self.y, self.c, rows, whole.shape[1])

        def pick(i, j, k):
            start = (
                (self.my_z - i + self.z) % self.z,
                (self.my_y - j + self.y) % self.y,
                (self.my_c - k + self.c) % self.c,
                0,
                0,
            )
            return lax.dynamic_slice(cut, start, (1, 1, 1) + cut.shape[3:]).reshape(cut.shape[3:])

        return self.scatter_relative({step: pick(*step) for step in self.order()})

    def gather_rows(self, block):
        held = self.gather(block)
        rows = block.shape[0]
        whole = jnp.zeros((rows * self.size, block.shape[1]), block.dtype)
        for step in self.order():
            whole = lax.dynamic_update_slice(whole, held[step], (self.source(step) * rows, 0))
        return whole

    def over_reps(self, value):
        if self.reps == 2:
            return value.astype(F32) + lax.ppermute(value, "rep", [(0, 1), (1, 0)]).astype(F32)
        return lax.psum(value, "rep").astype(F32)


def local(
    tokens,
    segments,
    routes,
    gates,
    gain_attn,
    w_qkv,
    w_out,
    gain_ffn,
    shared_gate,
    shared_up,
    shared_down,
    route_gate,
    route_up,
    route_down,
    cotangent,
):
    grid = Grid()
    seq_len, model_width = tokens.shape
    top_count = routes.shape[1]
    groups = grid.size
    expert_count = groups * route_gate.shape[0]
    capacity = 9 * seq_len * top_count // (8 * expert_count)
    slots = -(-capacity // 16) * 16
    inner = H * HD
    head_scale = math.sqrt(HD)
    hidden = shared_gate.shape[1] // groups
    width = gain_attn.shape[0]

    chosen = routes[:, :, None] == jnp.arange(expert_count, dtype=jnp.int32)[None, None, :]
    gate_table = jnp.sum(jnp.where(chosen, gates[:, :, None], 0.0), axis=1)
    gate_table = jnp.where(jnp.any(chosen, axis=1), gate_table, -1.0).T
    both_gains = jnp.concatenate([gain_attn, gain_ffn]).astype(F32)
    small = jnp.concatenate(
        [gate_table, jnp.broadcast_to(both_gains, (groups, 2 * width))], axis=1
    )
    small = lax.all_to_all(small, "grp", split_axis=0, concat_axis=0, tiled=True)
    attn_gain = small[:, seq_len : seq_len + width].reshape(-1)
    ffn_gain = small[:, seq_len + width :].reshape(-1)

    qkv_weight = grid.gather_rows(w_qkv)
    out_weight_t = grid.gather_rows(w_out.T)
    rows = tokens.astype(F32)
    inverse_one = rms_scale(rows)
    normed_one = rows * inverse_one
    attn_in = (normed_one * attn_gain).astype(BF)
    projected = jnp.dot(attn_in, qkv_weight, preferred_element_type=F32)
    cosine, sine = rotary_tables(seq_len, HD)
    query_rows = rotate(projected[:, :inner].reshape(seq_len, H, HD), cosine, sine).astype(BF)
    key_rows = rotate(projected[:, inner : 2 * inner].reshape(seq_len, H, HD), cosine, sine).astype(
        BF
    )
    value_rows = projected[:, 2 * inner :].reshape(seq_len, H, HD).astype(BF)
    places = jnp.arange(seq_len, dtype=jnp.int32)
    doc_ids = segments[0]
    allowed = ((places[:, None] >= places[None, :]) & (doc_ids[:, None] == doc_ids[None, :]))[None]
    scores = jnp.einsum("shd,thd->hst", query_rows, key_rows, preferred_element_type=F32) / head_scale
    scores = jnp.where(allowed, scores, MASKED_SCORE)
    top_score = jnp.max(scores, axis=-1, keepdims=True)
    raised = jnp.exp(scores - top_score)
    row_total = jnp.sum(raised, axis=-1, keepdims=True)
    probs = raised / row_total
    probs_low = probs.astype(BF)
    attn_rows = (
        jnp.einsum("hst,thd->shd", probs_low, value_rows, preferred_element_type=F32)
        .reshape(seq_len, inner)
        .astype(BF)
    )
    residual = rows + contract(attn_rows, out_weight_t, 1, 1)
    inverse_two = rms_scale(residual)
    normed_two = residual * inverse_two
    ffn_in = (normed_two * ffn_gain).astype(BF)

    order = grid.order()
    dy_held = grid.gather(cotangent)
    dy_rows = jnp.stack([dy_held[step] for step in order])
    pieces = jnp.concatenate(
        [
            shared_gate.reshape(width, groups, hidden).transpose(1, 0, 2),
            shared_up.reshape(width, groups, hidden).transpose(1, 0, 2),
            shared_down.reshape(groups, hidden, width).transpose(0, 2, 1),
        ],
        axis=2,
    )
    pieces = lax.all_to_all(pieces, "grp", split_axis=0, concat_axis=0, tiled=True)
    pieces = pieces.reshape(model_width, 3 * hidden)
    shared_in, shared_back = pieces[:, : 2 * hidden], pieces[:, 2 * hidden :]
    ffn_held = grid.gather(ffn_in)
    ffn_rows = jnp.stack([ffn_held[step] for step in order])

    sources = jnp.stack([grid.source(step) for step in order])
    gate_rows = small[:, :seq_len][sources]
    routed_here = gate_rows >= 0.0
    earlier = (places[:, None] < places[None, :]).astype(BF)
    position = jnp.dot(routed_here.astype(BF), earlier, preferred_element_type=F32)
    kept = routed_here & (position < capacity)
    gate_kept = jnp.where(kept, gate_rows, 0.0)
    hit = kept[:, None, :] & (
        position[:, None, :] == jnp.arange(slots, dtype=F32)[None, :, None]
    )
    slot_gate = jnp.sum(jnp.where(hit, gate_rows[:, None, :], 0.0), axis=-1)
    select = hit.astype(BF)

    expert_gate_w, expert_up_w, expert_down_w = route_gate[0], route_up[0], route_down[0]
    flat = (groups * slots, model_width)
    expert_in = (
        jnp.einsum("sct,std->scd", select, ffn_rows, preferred_element_type=F32)
        .astype(BF)
        .reshape(flat)
    )
    grad_expert_out = (
        (
            jnp.einsum("sct,std->scd", select, dy_rows, preferred_element_type=F32)
            * slot_gate[:, :, None]
        )
        .astype(BF)
        .reshape(flat)
    )
    gate_part = jnp.dot(expert_in, expert_gate_w, preferred_element_type=F32)
    up_part = jnp.dot(expert_in, expert_up_w, preferred_element_type=F32)
    expert_silu = jax.nn.silu(gate_part)
    expert_hidden = (expert_silu * up_part).astype(BF)
    grad_hidden = contract(grad_expert_out, expert_down_w, 1, 1)
    grad_expert_gate = (grad_hidden * up_part * silu_slope(gate_part)).astype(BF)
    grad_expert_up = (grad_hidden * expert_silu).astype(BF)
    grad_expert_in = (
        contract(grad_expert_gate, expert_gate_w, 1, 1)
        + contract(grad_expert_up, expert_up_w, 1, 1)
    ).astype(BF)
    expert_out = jnp.dot(expert_hidden, expert_down_w, preferred_element_type=F32).astype(BF)

    all_ffn = ffn_rows.reshape(-1, model_width)
    all_dy = dy_rows.reshape(-1, model_width)
    shared_pre = jnp.dot(all_ffn, shared_in, preferred_element_type=F32)
    gate_pre, up_pre = shared_pre[:, :hidden], shared_pre[:, hidden:]
    shared_silu = jax.nn.silu(gate_pre)
    shared_hidden = (shared_silu * up_pre).astype(BF)
    grad_shared_hidden = jnp.dot(all_dy, shared_back, preferred_element_type=F32)
    grad_shared_pre = jnp.concatenate(
        [
            (grad_shared_hidden * up_pre * silu_slope(gate_pre)).astype(BF),
            (grad_shared_hidden * shared_silu).astype(BF),
        ],
        axis=1,
    )

    back_shape = (groups, slots, model_width)
    grad_back = jnp.einsum(
        "sct,scd->std", select, grad_expert_in.reshape(back_shape), preferred_element_type=F32
    ) + contract(grad_shared_pre, shared_in, 1, 1).reshape(ffn_rows.shape)
    grad_back = grad_back.astype(BF)
    grad_ffn_in = grid.scatter_relative({s: grad_back[i] for i, s in enumerate(order)}).astype(F32)
    out_back = jnp.einsum(
        "sct,scd->std", select, expert_out.reshape(back_shape), preferred_element_type=F32
    ) * gate_kept[:, :, None] + contract(shared_hidden, shared_back, 1, 1).reshape(ffn_rows.shape)
    out_back = out_back.astype(BF)
    ffn_out = grid.scatter_relative({s: out_back[i] for i, s in enumerate(order)}).astype(F32)
    mixed = (residual + ffn_out).astype(BF)

    grad_route_down = grid.over_reps(contract(expert_hidden, grad_expert_out, 0, 0).astype(BF))[None]
    grad_route_gate = grid.over_reps(contract(expert_in, grad_expert_gate, 0, 0).astype(BF))[None]
    grad_route_up = grid.over_reps(contract(expert_in, grad_expert_up, 0, 0).astype(BF))[None]
    grad_pieces = jnp.concatenate(
        [contract(all_ffn, grad_shared_pre, 0, 0), contract(all_dy, shared_hidden, 0, 0)], axis=1
    ).astype(BF)
    grad_pieces = lax.all_to_all(
        grad_pieces.reshape(groups, width, 3 * hidden), "grp", split_axis=0, concat_axis=0, tiled=True
    )
    grad_pieces = grid.over_reps(grad_pieces)

    def join(part):
        return part.transpose(1, 0, 2).reshape(width, groups * hidden)

    grad_shared_gate = join(grad_pieces[:, :, :hidden])
    grad_shared_up = join(grad_pieces[:, :, hidden : 2 * hidden])
    grad_shared_down = join(grad_pieces[:, :, 2 * hidden :]).T

    grad_out = cotangent.astype(F32)
    grad_norm_two, grad_ffn_gain = norm_backward(grad_ffn_in, normed_two, inverse_two, ffn_gain)
    grad_residual = grad_out + grad_norm_two
    grad_attn_low = grad_residual.astype(BF)
    grad_heads = jnp.dot(grad_attn_low, out_weight_t, preferred_element_type=F32)
    grad_heads = grad_heads.astype(BF).reshape(seq_len, H, HD)
    grad_probs = jnp.einsum("shd,thd->hst", grad_heads, value_rows, preferred_element_type=F32)
    grad_values = jnp.einsum("hst,shd->thd", probs_low, grad_heads, preferred_element_type=F32)
    grad_scores = (
        probs * (grad_probs - jnp.sum(grad_probs * probs, axis=-1, keepdims=True))
    ).astype(BF)
    grad_queries = (
        jnp.einsum("hst,thd->shd", grad_scores, key_rows, preferred_element_type=F32) / head_scale
    )
    grad_keys = (
        jnp.einsum("hst,shd->thd", grad_scores, query_rows, preferred_element_type=F32)
        / head_scale
    )
    grad_projected = jnp.concatenate(
        [
            unrotate(grad_queries, cosine, sine).reshape(seq_len, inner),
            unrotate(grad_keys, cosine, sine).reshape(seq_len, inner),
            grad_values.reshape(seq_len, inner),
        ],
        axis=-1,
    ).astype(BF)
    grad_out_t = contract(grad_attn_low, attn_rows, 0, 0).astype(BF)
    grad_w_out = grid.over_reps(grid.scatter_rows(grad_out_t)).T
    grad_qkv = contract(attn_in, grad_projected, 0, 0).astype(BF)
    grad_w_qkv = grid.over_reps(grid.scatter_rows(grad_qkv))
    grad_attn_in = contract(grad_projected, qkv_weight, 1, 1)
    grad_norm_one, grad_attn_gain = norm_backward(grad_attn_in, normed_one, inverse_one, attn_gain)
    grad_tokens = (grad_residual + grad_norm_one).astype(BF)

    gain_grads = jnp.concatenate(
        [grad_attn_gain.reshape(groups, width), grad_ffn_gain.reshape(groups, width)], axis=1
    )
    gain_grads = jnp.tile(gain_grads, (grid.reps, 1))
    gain_grads = lax.all_to_all(
        gain_grads, ("rep", "grp"), split_axis=0, concat_axis=0, tiled=True
    ).sum(axis=0)
    return (
        mixed,
        grad_tokens,
        gain_grads[:width],
        grad_w_qkv,
        grad_w_out,
        gain_grads[width:],
        grad_shared_gate,
        grad_shared_up,
        grad_shared_down,
        grad_route_gate,
        grad_route_up,
        grad_route_down,
    )


def solution(mesh):
    in_specs = (
        P(("rep", "grp"), None),
        P(("rep", "grp"), None),
        P(("rep", "grp"), None),
        P(("rep", "grp"), None),
        P("grp"),
        P("grp", None),
        P(None, "grp"),
        P("grp"),
        P("grp", None),
        P("grp", None),
        P(None, "grp"),
        P("grp", None, None),
        P("grp", None, None),
        P("grp", None, None),
        P(("rep", "grp"), None),
    )
    out_specs = (
        P(("rep", "grp"), None),
        P(("rep", "grp"), None),
        P("grp"),
        P("grp", None),
        P(None, "grp"),
        P("grp"),
        P("grp", None),
        P("grp", None),
        P(None, "grp"),
        P("grp", None, None),
        P("grp", None, None),
        P("grp", None, None),
    )
    return jax.shard_map(local, mesh=mesh, in_specs=in_specs, out_specs=out_specs, check_vma=False)
```

```python
import math

import jax
import jax.numpy as jnp
import numpy as np
from jax import lax
from jax.experimental import pallas as pl
from jax.experimental.pallas import tpu as pltpu
from jax.sharding import PartitionSpec as P

H = 10
HD = 128

EPSILON = 1e-06
MASKED_SCORE = -1000000000.0
BF = jnp.bfloat16
F32 = jnp.float32
BRIEF = pl.CostEstimate(flops=1, bytes_accessed=1, transcendentals=0)


def rms_scale(values):
    return lax.rsqrt(jnp.mean(values * values, axis=-1, keepdims=True) + EPSILON)


def rotary_tables(seq_len):
    half = HD // 2
    frequency = np.power(np.float32(10000.0), -2.0 * np.arange(half, dtype=np.float32) / HD)
    angle = np.arange(seq_len, dtype=np.float32)[:, None] * frequency.astype(np.float32)[None, :]
    cosine, sine = np.cos(angle), np.sin(angle)
    return np.stack(
        [np.concatenate([cosine, cosine], axis=1), np.concatenate([-sine, sine], axis=1)]
    ).astype(np.float32)


def contract(left, right, left_dim, right_dim):
    return lax.dot_general(
        left, right, (((left_dim,), (right_dim,)), ((), ())), preferred_element_type=F32
    )


def silu_slope(values):
    sigma = jax.nn.sigmoid(values)
    return sigma * (1.0 + values * (1.0 - sigma))


def norm_backward(grad_scaled, normed, inverse, gain):
    grad_normed = grad_scaled * gain
    grad_gain = jnp.sum(grad_scaled * normed, axis=0)
    grad_rows = inverse * (
        grad_normed - normed * jnp.mean(grad_normed * normed, axis=-1, keepdims=True)
    )
    return (grad_rows, grad_gain)


def after(value, *others):
    return lax.optimization_barrier((value,) + others)[0]


def attention_forward_kernel(q_in, k_in, v_in, table, doc_col, doc_row, q_ref, k_ref, v_ref, p_ref, o_ref):
    def turned(values):
        return (values * table[0] + pltpu.roll(values, HD // 2, 1) * table[1]).astype(BF)

    query, key, value = turned(q_in[...]), turned(k_in[...]), v_in[...].astype(BF)
    q_ref[...], k_ref[...], v_ref[...] = query, key, value
    scores = contract(query, key, 1, 1) / math.sqrt(HD)
    at = lax.broadcasted_iota(jnp.int32, scores.shape, 0)
    to = lax.broadcasted_iota(jnp.int32, scores.shape, 1)
    scores = jnp.where((at >= to) & (doc_col[...] == doc_row[...]), scores, MASKED_SCORE)
    raised = jnp.exp(scores - jnp.max(scores, axis=-1, keepdims=True))
    probs = raised / jnp.sum(raised, axis=-1, keepdims=True)
    p_ref[0] = probs
    o_ref[...] = contract(probs.astype(BF), value, 1, 0).astype(BF)


def attention_backward_kernel(g_ref, q_ref, k_ref, v_ref, p_ref, table, dq_ref, dk_ref, dv_ref):
    def turned_back(values):
        return (values * table[0] - pltpu.roll(values, HD // 2, 1) * table[1]).astype(BF)

    grad, probs = g_ref[...], p_ref[0]
    grad_probs = contract(grad, v_ref[...], 1, 1)
    dv_ref[...] = contract(probs.astype(BF), grad, 0, 0).astype(BF)
    mean = jnp.sum(grad_probs * probs, axis=-1, keepdims=True)
    grad_scores = (probs * (grad_probs - mean)).astype(BF)
    dq_ref[...] = turned_back(contract(grad_scores, k_ref[...], 1, 0) / math.sqrt(HD))
    dk_ref[...] = turned_back(contract(grad_scores, q_ref[...], 0, 0) / math.sqrt(HD))


def head_block(seq_len, offset=0):
    return pl.BlockSpec((seq_len, HD), lambda h: (0, offset + h))


def attention_forward(projected, table, documents):
    seq_len = projected.shape[0]
    row = jax.ShapeDtypeStruct((seq_len, H * HD), BF)
    probs_block = pl.BlockSpec((1, seq_len, seq_len), lambda h: (h, 0, 0))
    return pl.pallas_call(
        attention_forward_kernel,
        grid=(H,),
        in_specs=[
            head_block(seq_len),
            head_block(seq_len, H),
            head_block(seq_len, 2 * H),
            pl.BlockSpec((2, seq_len, HD), lambda h: (0, 0, 0)),
            pl.BlockSpec((seq_len, 1), lambda h: (0, 0)),
            pl.BlockSpec((1, seq_len), lambda h: (0, 0)),
        ],
        out_specs=[head_block(seq_len)] * 3 + [probs_block, head_block(seq_len)],
        out_shape=[row] * 3 + [jax.ShapeDtypeStruct((H, seq_len, seq_len), F32), row],
        cost_estimate=BRIEF,
        name="attention_forward",
    )(projected, projected, projected, table, documents.reshape(seq_len, 1), documents.reshape(1, seq_len))


def attention_backward(grad_heads, query, key, value, probs, table):
    seq_len = grad_heads.shape[0]
    row = jax.ShapeDtypeStruct((seq_len, H * HD), BF)
    return pl.pallas_call(
        attention_backward_kernel,
        grid=(H,),
        in_specs=[head_block(seq_len)] * 4
        + [
            pl.BlockSpec((1, seq_len, seq_len), lambda h: (h, 0, 0)),
            pl.BlockSpec((2, seq_len, HD), lambda h: (0, 0, 0)),
        ],
        out_specs=[head_block(seq_len)] * 3,
        out_shape=[row] * 3,
        cost_estimate=BRIEF,
        name="attention_backward",
    )(grad_heads, query, key, value, probs, table)


def tile_of(first, columns):
    return max(n for n in range(128, 769, 128) if columns % n == 0 and first % n == 0)


def held_product(left, blocks, first, columns):
    rows, depth = left.shape
    tile = tile_of(first, columns)

    def kernel(left_ref, *refs):
        whole = jnp.concatenate([one[...] for one in refs[:-1]], axis=0)
        refs[-1][...] = contract(left_ref[...], whole, 1, 0)

    return pl.pallas_call(
        kernel,
        grid=(columns // tile,),
        in_specs=[pl.BlockSpec((rows, depth), lambda n: (0, 0))]
        + [pl.BlockSpec((one.shape[0], tile), lambda n: (0, first // tile + n)) for one in blocks],
        out_specs=pl.BlockSpec((rows, tile), lambda n: (0, n)),
        out_shape=jax.ShapeDtypeStruct((rows, columns), F32),
        cost_estimate=BRIEF,
        name="held_product",
    )(left, *blocks)


def held_product_back(left, blocks, first):
    rows, columns = left.shape
    depth = sum(one.shape[0] for one in blocks)
    tile = tile_of(first, columns)

    def kernel(left_ref, *refs):
        whole = jnp.concatenate([one[...] for one in refs[:-1]], axis=0)
        product = contract(left_ref[...], whole, 1, 1)

        @pl.when(pl.program_id(0) == 0)
        def _():
            refs[-1][...] = product

        @pl.when(pl.program_id(0) > 0)
        def _():
            refs[-1][...] += product

    return pl.pallas_call(
        kernel,
        grid=(columns // tile,),
        in_specs=[pl.BlockSpec((rows, tile), lambda n: (0, n))]
        + [pl.BlockSpec((one.shape[0], tile), lambda n: (0, first // tile + n)) for one in blocks],
        out_specs=pl.BlockSpec((rows, depth), lambda n: (0, 0)),
        out_shape=jax.ShapeDtypeStruct((rows, depth), F32),
        cost_estimate=BRIEF,
        name="held_product_back",
    )(left, *blocks)


class Order:
    def __init__(self):
        self.last = ()

    def enter(self, *values):
        held = lax.optimization_barrier(values + self.last)[: len(values)]
        return held[0] if len(values) == 1 else held

    def done(self, *values):
        self.last = values


class Rounds:
    def __init__(self, grid):
        self.grid = grid
        self.before = ()
        self.now = []

    def send(self, value, *move):
        arrived = self.grid.shift(after(value, *self.before), *move)
        self.now.append(arrived)
        return arrived

    def close(self):
        self.before, self.now = tuple(self.now), []


class Gather:
    def __init__(self, grid, rounds, block, merged):
        self.grid, self.rounds, self.merged = grid, rounds, merged
        self.held = {(0, 0, 0): block}
        self.halves = {}
        self.count = grid.z + grid.y + (1 if merged else 0) - 1 if grid.size > 1 else 0

    def round(self, r):
        grid, held = self.grid, self.held
        if r < grid.z - 1:
            held[(r + 1, 0, 0)] = self.rounds.send(held[(r, 0, 0)], 1, 0, 0)
        for j in range(grid.y - 1):
            if 0 <= r - j < grid.z:
                held[(r - j, j + 1, 0)] = self.rounds.send(held[(r - j, j, 0)], 0, 1, 0)
        if not self.merged:
            for j in range(grid.y):
                if 0 <= r - j < grid.z:
                    for k in range(1, grid.c):
                        held[(r - j, j, k)] = self.rounds.send(held[(r - j, j, k - 1)], 0, 0, 1)
            return
        for n, half in enumerate(grid.halves):
            if r == half[-1] + grid.y:
                stacks = [jnp.stack([held[place] for place in grid.places(half, 0)])]
                for _ in range(1, grid.c):
                    stacks.append(self.rounds.send(stacks[-1], 0, 0, 1))
                self.halves[n] = stacks


class Scatter:
    def __init__(self, grid, stage, half, make):
        self.grid, self.stage, self.make = grid, stage, make
        self.rows = len(half)

    def core(self):
        grid = self.grid
        if grid.c == 1:
            return
        total = self.make(grid.y * self.rows, grid.y * self.rows).astype(BF)
        self.stage.done(total)
        self.arrived = grid.shift(total, 0, 0, 1)

    def term(self, j):
        here = self.make(j * self.rows, self.rows)
        if self.grid.c > 1:
            here = here + self.arrived[j * self.rows : (j + 1) * self.rows].astype(F32)
        return here

    def along_y(self):
        grid = self.grid
        if grid.y == 1:
            return
        total = self.term(1).astype(BF)
        self.stage.done(total)
        self.total = grid.shift(total, 0, 1, 0)
        for j in range(2, grid.y):
            total = (self.term(j) + self.total.astype(F32)).astype(BF)
            self.stage.done(total)
            self.total = grid.shift(total, 0, 1, 0)

    def own(self):
        total = self.term(0)
        if self.grid.y > 1:
            total = total + self.total.astype(F32)
        total = total.astype(BF)
        self.stage.done(total)
        return total


class Grid:
    def __init__(self):
        self.size = lax.axis_size("grp")
        self.reps = lax.axis_size("rep")
        self.c = 2 if self.size % 2 == 0 else 1
        self.z = 4 if self.size % (4 * self.c) == 0 else 1
        self.y = self.size // (self.c * self.z)
        me = lax.axis_index("grp")
        self.my_c = me % self.c
        self.my_y = me // self.c % self.y
        self.my_z = me // (self.c * self.y)
        self.halves = ((0, 1), (2, 3)) if self.z == 4 else ((0,),)

    def flat(self, z, y, c):
        return (z % self.z * self.y + y % self.y) * self.c + c % self.c

    def shift(self, value, dz, dy, dc):
        pairs = [
            (self.flat(z, y, c), self.flat(z + dz, y + dy, c + dc))
            for z in range(self.z)
            for y in range(self.y)
            for c in range(self.c)
        ]
        return lax.ppermute(value, "grp", pairs)

    def source(self, step):
        return self.flat(
            self.my_z - step[0] + self.z, self.my_y - step[1] + self.y, self.my_c - step[2] + self.c
        )

    def places(self, half, k):
        return [(i, j, k) for j in range(self.y) for i in half]

    def order(self):
        return [
            place for half in self.halves for k in range(self.c) for place in self.places(half, k)
        ]

    def other_rep(self, value):
        if self.reps == 2:
            return lax.ppermute(value, "rep", [(0, 1), (1, 0)])
        return lax.psum(value, "rep")

    def both_reps(self, mine, theirs):
        if self.reps == 2:
            return mine.astype(F32) + theirs.astype(F32)
        return theirs.astype(F32)


def local(
    tokens,
    segments,
    routes,
    gates,
    gain_attn,
    w_qkv,
    w_out,
    gain_ffn,
    shared_gate,
    shared_up,
    shared_down,
    route_gate,
    route_up,
    route_down,
    cotangent,
):
    grid = Grid()
    seq_len, model_width = tokens.shape
    top_count = routes.shape[1]
    groups = grid.size
    expert_count = groups * route_gate.shape[0]
    capacity = 9 * seq_len * top_count // (8 * expert_count)
    slots = -(-capacity // 16) * 16
    hidden = shared_gate.shape[1] // groups
    width = gain_attn.shape[0]

    chosen = routes[:, :, None] == jnp.arange(expert_count, dtype=jnp.int32)[None, None, :]
    gate_table = jnp.sum(jnp.where(chosen, gates[:, :, None], 0.0), axis=1)
    gate_table = jnp.where(jnp.any(chosen, axis=1), gate_table, -1.0).T
    both_gains = jnp.concatenate([gain_attn, gain_ffn]).astype(F32)
    small = jnp.concatenate(
        [gate_table, jnp.broadcast_to(both_gains, (groups, 2 * width))], axis=1
    )
    small = lax.all_to_all(small, "grp", split_axis=0, concat_axis=0, tiled=True)

    sources = jnp.stack([grid.source(place) for place in grid.order()])
    held_feature = (sources[:, None] * width + jnp.arange(width, dtype=jnp.int32)[None, :]).reshape(-1)
    shuffle = (held_feature[:, None] == jnp.arange(model_width, dtype=jnp.int32)[None, :]).astype(BF)
    count = len(grid.halves)
    near = groups // count

    def chunk(values, n):
        size = values.shape[0] // count
        return values[n * size : (n + 1) * size]

    def to_held(values):
        return contract(values, shuffle, 1, 1).astype(BF)

    def from_held(values):
        high = lax.reduce_precision(values, 8, 7)
        both = jnp.concatenate([high.astype(BF), (values - high).astype(BF)])
        both = jnp.dot(both, shuffle, preferred_element_type=F32)
        return both[: values.shape[0]] + both[values.shape[0] :]

    rounds = Rounds(grid)
    qkv_width, inner = w_qkv.shape[1], w_out.shape[0]
    weights = Gather(grid, rounds, jnp.concatenate([w_qkv, w_out.T], axis=1), False)
    others = Gather(grid, rounds, cotangent, True)
    lead = grid.z
    arrivals = []
    for r in range(lead + others.count):
        if r < weights.count:
            weights.round(r)
        if r >= lead:
            others.round(r - lead)
        rounds.close()
        arrivals.append(rounds.before)
    blocks = [weights.held[place] for place in grid.order()]
    early = arrivals[0]

    small = after(small, *early)
    attn_gain = small[:, seq_len : seq_len + width].reshape(-1)
    ffn_gain = small[:, seq_len + width :].reshape(-1)
    places = jnp.arange(seq_len, dtype=jnp.int32)
    gate_rows = small[:, :seq_len][sources]
    routed_here = gate_rows >= 0.0
    earlier = (places[:, None] < places[None, :]).astype(BF)
    position = jnp.dot(routed_here.astype(BF), earlier, preferred_element_type=F32)
    kept = routed_here & (position < capacity)
    gate_kept = jnp.where(kept, gate_rows, 0.0)
    hit = kept[:, None, :] & (
        position[:, None, :] == jnp.arange(slots, dtype=F32)[None, :, None]
    )
    slot_gate = jnp.sum(jnp.where(hit, gate_rows[:, None, :], 0.0), axis=-1)
    select = hit.astype(BF)
    expert_gate_w, expert_up_w, expert_down_w = route_gate[0], route_up[0], route_down[0]
    inside = expert_gate_w.shape[1]
    both_w = jnp.concatenate([after(expert_gate_w, *early), expert_up_w], axis=1)

    stage = Order()
    rows = after(tokens, *early).astype(F32)
    inverse_one = rms_scale(rows)
    normed_one = rows * inverse_one
    attn_in = (normed_one * attn_gain).astype(BF)
    attn_held, slot_gate, gate_kept, select, both_w = (
        lax.optimization_barrier(
            (to_held(attn_in), slot_gate, gate_kept, select, both_w)
        )
    )
    projected = held_product(attn_held, blocks, 0, qkv_width)
    table = jnp.asarray(rotary_tables(seq_len))
    query, key, value, probs, attn_rows = attention_forward(
        after(projected, *arrivals[weights.count]), table, segments
    )
    residual = rows + from_held(
        held_product_back(after(attn_rows, *arrivals[weights.count + 1]), blocks, qkv_width)
    )
    inverse_two = rms_scale(residual)
    normed_two = residual * inverse_two
    ffn_in = (normed_two * ffn_gain).astype(BF)
    shared_gate, shared_up, shared_down = (
        after(one, ffn_in) for one in (shared_gate, shared_up, shared_down)
    )
    pieces = jnp.concatenate(
        [
            shared_gate.reshape(width, groups, hidden).transpose(1, 0, 2),
            shared_up.reshape(width, groups, hidden).transpose(1, 0, 2),
            shared_down.reshape(groups, hidden, width).transpose(0, 2, 1),
        ],
        axis=2,
    )
    pieces = lax.all_to_all(pieces, "grp", split_axis=0, concat_axis=0, tiled=True)
    pieces = pieces.reshape(model_width, 3 * hidden)
    shared_in, shared_back = pieces[:, : 2 * hidden], pieces[:, 2 * hidden :]

    stage.done(ffn_in)
    rounds = Rounds(grid)
    ffn = Gather(grid, rounds, ffn_in, True)
    for r in range(ffn.count):
        ffn.round(r)
        rounds.close()

    def picked(selection, stacks):
        size = selection.shape[0] // len(stacks)
        return jnp.concatenate(
            [
                jnp.einsum(
                    "sct,std->scd",
                    selection[n * size : (n + 1) * size],
                    one,
                    preferred_element_type=F32,
                )
                for n, one in enumerate(stacks)
            ]
        )

    def each(stacks, right):
        return jnp.concatenate(
            [
                jnp.dot(one.reshape(-1, one.shape[2]), right, preferred_element_type=F32)
                for one in stacks
            ]
        )

    flat = (near * slots, model_width)

    def forward_part(n):
        selection = stage.enter(chunk(select, n))
        dy = others.halves[n]
        expert_in = picked(selection, ffn.halves[n]).astype(BF).reshape(flat)
        grad_out = picked(selection, dy) * chunk(slot_gate, n)[:, :, None]
        grad_out = grad_out.astype(BF).reshape(flat)
        both = jnp.dot(expert_in, both_w, preferred_element_type=F32)
        expert_hidden = (jax.nn.silu(both[:, :inside]) * both[:, inside:]).astype(BF)
        stage.done(both, expert_hidden, grad_out)
        return {"in": expert_in, "out": grad_out, "hidden": expert_hidden, "both": both}

    def backward_part(n, part):
        grad_out, both = stage.enter(part["out"], part["both"])
        gate_part, up_part = both[:, :inside], both[:, inside:]
        grad_hidden = contract(grad_out, expert_down_w, 1, 1)
        grad_both = jnp.concatenate(
            [
                (grad_hidden * up_part * silu_slope(gate_part)).astype(BF),
                (grad_hidden * jax.nn.silu(gate_part)).astype(BF),
            ],
            axis=1,
        )
        grad_both = after(grad_both)
        grad_in = contract(grad_both, both_w, 1, 1).astype(BF)
        shared_pre = each(ffn.halves[n], shared_in)
        gate_pre, up_pre = shared_pre[:, :hidden], shared_pre[:, hidden:]
        shared_silu = jax.nn.silu(gate_pre)
        grad_shared_hidden = each(others.halves[n], shared_back)
        grad_shared_pre = jnp.concatenate(
            [
                (grad_shared_hidden * up_pre * silu_slope(gate_pre)).astype(BF),
                (grad_shared_hidden * shared_silu).astype(BF),
            ],
            axis=1,
        )
        part["grad_both"] = grad_both
        part["shared"] = (shared_silu * up_pre).astype(BF)
        part["shared_pre"] = grad_shared_pre
        stage.done(grad_in, grad_shared_pre)
        return to_tokens(n, grad_in, None, grad_shared_pre, shared_in)

    def to_tokens(n, slot_rows, scale, shared_rows, shared_weight):
        slot_rows = slot_rows.reshape(near, slots, model_width)

        def make(first, size):
            mine = slice(first, first + size)
            selection = stage.enter(chunk(select, n)[mine])
            back = jnp.einsum(
                "sct,scd->std", selection, slot_rows[mine], preferred_element_type=F32
            )
            if scale is not None:
                back = back * scale[mine][:, :, None]
            shared_mine = shared_rows[first * seq_len : (first + size) * seq_len]
            return back + contract(shared_mine, shared_weight, 1, 1).reshape(back.shape)

        return Scatter(grid, stage, grid.halves[n], make)

    swap = grid.other_rep
    parts, backs = [], []
    for n in range(count):
        parts.append(forward_part(n))
        if n:
            backs[n - 1].along_y()
        backs.append(backward_part(n, parts[n]))
        backs[n].core()

    def joined(key):
        return jnp.concatenate([part[key] for part in parts])

    class AlongZ:
        def __init__(self, halves):
            self.halves = halves

        def far(self):
            if count == 2:
                far = self.halves[1].own()
                self.passed_on = grid.shift(far[0], 3, 0, 0)
                self.back_one = grid.shift(far[1], 1, 0, 0)

        def near(self):
            close = self.halves[0].own()
            self.mine = close[0]
            if count == 2:
                near = (close[1].astype(F32) + self.passed_on.astype(F32)).astype(BF)
                stage.done(near)
                self.near_one = grid.shift(near, 3, 0, 0)

        def total(self):
            mine = stage.enter(self.mine).astype(F32)
            if count == 2:
                mine = mine + self.back_one.astype(F32) + self.near_one.astype(F32)
            return mine

    down_left, down_right = stage.enter(joined("hidden"), joined("out"))
    down_mine = contract(down_left, down_right, 0, 0).astype(BF)
    stage.done(down_mine)
    down_theirs = swap(down_mine)
    backs[-1].along_y()
    both_left, both_right = stage.enter(joined("in"), joined("grad_both"))
    both_mine = contract(both_left, both_right, 0, 0).astype(BF)
    stage.done(both_mine)
    ffn_sum = AlongZ(backs)
    ffn_sum.far()

    outs = []
    for n in range(count):
        hidden_rows = stage.enter(parts[n]["hidden"])
        expert_out = jnp.dot(hidden_rows, expert_down_w, preferred_element_type=F32).astype(BF)
        stage.done(expert_out)
        outs.append(
            to_tokens(n, expert_out, chunk(gate_kept, n), parts[n]["shared"], shared_back)
        )
    ffn_sum.near()
    for out in outs[::-1]:
        out.core()
    grad_ffn_in = ffn_sum.total()

    grad_norm_two, grad_ffn_gain = norm_backward(grad_ffn_in, normed_two, inverse_two, ffn_gain)
    grad_residual = cotangent.astype(F32) + grad_norm_two
    grad_attn_low = grad_residual.astype(BF)
    low_turned = contract(shuffle, grad_attn_low, 1, 1).astype(BF)
    grad_heads = held_product(low_turned.T, blocks, qkv_width, inner).astype(BF)
    stage.done(grad_heads)
    for out in outs[::-1]:
        out.along_y()
    down_there = stage.enter(down_mine)
    grad_route_down = grid.both_reps(down_there, down_theirs)[None]
    stage.done(grad_route_down)
    both_theirs = swap(after(both_mine, down_theirs))
    grads = attention_backward(stage.enter(grad_heads), query, key, value, probs, table)
    grad_projected = jnp.concatenate(grads, axis=1)
    stage.done(grad_projected)

    def products(n, turned, right):
        def make(first, size):
            rows = chunk(turned, n)[first * width : (first + size) * width]
            product = jnp.dot(stage.enter(rows), right, preferred_element_type=F32)
            return product.reshape(size, width, right.shape[1])

        return Scatter(grid, stage, grid.halves[n], make)

    turned_in = contract(shuffle, attn_in, 1, 1).astype(BF)
    wides = [products(n, turned_in, grad_projected) for n in range(count)]
    talls = [products(n, low_turned, attn_rows) for n in range(count)]
    out_sum, wide_sum, tall_sum = AlongZ(outs), AlongZ(wides), AlongZ(talls)
    for wide in wides[::-1]:
        wide.core()
    out_sum.far()
    for wide in wides[::-1]:
        wide.along_y()
    out_sum.near()
    wide_sum.far()
    mixed = (residual + out_sum.total()).astype(BF)
    stage.done(mixed)
    shared_left, shared_right = stage.enter(joined("shared_pre"), joined("shared"))

    def rows_of(stacks):
        return jnp.concatenate([one.reshape(-1, model_width) for half in stacks.values() for one in half])

    grad_pieces = jnp.concatenate(
        [
            contract(shared_left, rows_of(ffn.halves), 0, 0),
            contract(shared_right, rows_of(others.halves), 0, 0),
        ]
    ).astype(BF).T.reshape(groups, width, 3 * hidden)
    stage.done(grad_pieces)
    grad_pieces = lax.all_to_all(grad_pieces, "grp", split_axis=0, concat_axis=0, tiled=True)
    for tall in talls[::-1]:
        tall.core()
    for tall in talls[::-1]:
        tall.along_y()
    wide_sum.near()
    grad_attn_in = from_held(held_product_back(stage.enter(grad_projected), blocks, 0))
    grad_norm_one, grad_attn_gain = norm_backward(grad_attn_in, normed_one, inverse_one, attn_gain)
    grad_tokens = (grad_residual + grad_norm_one).astype(BF)
    stage.done(grad_tokens)
    grad_pieces = stage.enter(grad_pieces)
    stage.done(grad_pieces)
    grad_pieces_there = swap(grad_pieces)
    tall_sum.far()
    grad_w_qkv = wide_sum.total().astype(BF)
    stage.done(grad_w_qkv)
    grad_w_qkv_there = swap(grad_w_qkv)
    tall_sum.near()
    both_there = stage.enter(both_mine)
    both_total = grid.both_reps(both_there, both_theirs)
    grad_route_gate, grad_route_up = both_total[None, :, :inside], both_total[None, :, inside:]
    stage.done(grad_route_gate, grad_route_up)

    grad_w_out = tall_sum.total().astype(BF)
    stage.done(grad_w_out)
    grad_w_out = grid.both_reps(grad_w_out, swap(grad_w_out)).T
    grad_pieces = grid.both_reps(grad_pieces, grad_pieces_there)
    grad_w_qkv = grid.both_reps(grad_w_qkv, grad_w_qkv_there)

    def join(part):
        return part.transpose(1, 0, 2).reshape(width, groups * hidden)

    grad_shared_gate = join(grad_pieces[:, :, :hidden])
    grad_shared_up = join(grad_pieces[:, :, hidden : 2 * hidden])
    grad_shared_down = join(grad_pieces[:, :, 2 * hidden :]).T

    gain_grads = jnp.concatenate(
        [grad_attn_gain.reshape(groups, width), grad_ffn_gain.reshape(groups, width)], axis=1
    )
    gain_grads = lax.all_to_all(gain_grads, "grp", split_axis=0, concat_axis=0, tiled=True)
    gain_grads = stage.enter(gain_grads).sum(axis=0, keepdims=True)
    gain_grads = grid.both_reps(gain_grads, swap(gain_grads))[0]
    return (
        mixed,
        grad_tokens,
        gain_grads[:width],
        grad_w_qkv,
        grad_w_out,
        gain_grads[width:],
        grad_shared_gate,
        grad_shared_up,
        grad_shared_down,
        grad_route_gate,
        grad_route_up,
        grad_route_down,
    )


def solution(mesh):
    in_specs = (
        P(("rep", "grp"), None),
        P(("rep", "grp"), None),
        P(("rep", "grp"), None),
        P(("rep", "grp"), None),
        P("grp"),
        P("grp", None),
        P(None, "grp"),
        P("grp"),
        P("grp", None),
        P("grp", None),
        P(None, "grp"),
        P("grp", None, None),
        P("grp", None, None),
        P("grp", None, None),
        P(("rep", "grp"), None),
    )
    out_specs = (
        P(("rep", "grp"), None),
        P(("rep", "grp"), None),
        P("grp"),
        P("grp", None),
        P(None, "grp"),
        P("grp"),
        P("grp", None),
        P("grp", None),
        P(None, "grp"),
        P("grp", None, None),
        P("grp", None, None),
        P("grp", None, None),
    )
    return jax.shard_map(local, mesh=mesh, in_specs=in_specs, out_specs=out_specs, check_vma=False)
```

```python
import math

import jax
import jax.numpy as jnp
import numpy as np
from jax import lax
from jax.experimental import pallas as pl
from jax.experimental.pallas import tpu as pltpu
from jax.sharding import PartitionSpec as P

H = 10
HD = 128

EPSILON = 1e-06
MASKED_SCORE = -1000000000.0
BF = jnp.bfloat16
F32 = jnp.float32
BRIEF = pl.CostEstimate(flops=1, bytes_accessed=1, transcendentals=0)


def rms_scale(values):
    return lax.rsqrt(jnp.mean(values * values, axis=-1, keepdims=True) + EPSILON)


def rotary_tables(seq_len):
    half = HD // 2
    frequency = np.power(np.float32(10000.0), -2.0 * np.arange(half, dtype=np.float32) / HD)
    angle = np.arange(seq_len, dtype=np.float32)[:, None] * frequency.astype(np.float32)[None, :]
    cosine, sine = np.cos(angle), np.sin(angle)
    return np.stack(
        [np.concatenate([cosine, cosine], axis=1), np.concatenate([-sine, sine], axis=1)]
    ).astype(np.float32)


def contract(left, right, left_dim, right_dim):
    return lax.dot_general(
        left, right, (((left_dim,), (right_dim,)), ((), ())), preferred_element_type=F32
    )


def silu_slope(values):
    sigma = jax.nn.sigmoid(values)
    return sigma * (1.0 + values * (1.0 - sigma))


def norm_backward(grad_scaled, normed, inverse, gain):
    grad_normed = grad_scaled * gain
    grad_gain = jnp.sum(grad_scaled * normed, axis=0)
    grad_rows = inverse * (
        grad_normed - normed * jnp.mean(grad_normed * normed, axis=-1, keepdims=True)
    )
    return (grad_rows, grad_gain)


def after(value, *others):
    return lax.optimization_barrier((value,) + others)[0]


def attention_forward_kernel(q_in, k_in, v_in, table, doc_col, doc_row, q_ref, k_ref, v_ref, p_ref, o_ref):
    def turned(values):
        return (values * table[0] + pltpu.roll(values, HD // 2, 1) * table[1]).astype(BF)

    query, key, value = turned(q_in[...]), turned(k_in[...]), v_in[...].astype(BF)
    q_ref[...], k_ref[...], v_ref[...] = query, key, value
    scores = contract(query, key, 1, 1) / math.sqrt(HD)
    at = lax.broadcasted_iota(jnp.int32, scores.shape, 0)
    to = lax.broadcasted_iota(jnp.int32, scores.shape, 1)
    scores = jnp.where((at >= to) & (doc_col[...] == doc_row[...]), scores, MASKED_SCORE)
    raised = jnp.exp(scores - jnp.max(scores, axis=-1, keepdims=True))
    probs = raised / jnp.sum(raised, axis=-1, keepdims=True)
    p_ref[0] = probs
    o_ref[...] = contract(probs.astype(BF), value, 1, 0).astype(BF)


def attention_backward_kernel(g_ref, q_ref, k_ref, v_ref, p_ref, table, dq_ref, dk_ref, dv_ref):
    def turned_back(values):
        return (values * table[0] - pltpu.roll(values, HD // 2, 1) * table[1]).astype(BF)

    grad, probs = g_ref[...], p_ref[0]
    grad_probs = contract(grad, v_ref[...], 1, 1)
    dv_ref[...] = contract(probs.astype(BF), grad, 0, 0).astype(BF)
    mean = jnp.sum(grad_probs * probs, axis=-1, keepdims=True)
    grad_scores = (probs * (grad_probs - mean)).astype(BF)
    dq_ref[...] = turned_back(contract(grad_scores, k_ref[...], 1, 0) / math.sqrt(HD))
    dk_ref[...] = turned_back(contract(grad_scores, q_ref[...], 0, 0) / math.sqrt(HD))


def head_block(seq_len, offset=0):
    return pl.BlockSpec((seq_len, HD), lambda h: (0, offset + h))


def attention_forward(projected, table, documents):
    seq_len = projected.shape[0]
    row = jax.ShapeDtypeStruct((seq_len, H * HD), BF)
    probs_block = pl.BlockSpec((1, seq_len, seq_len), lambda h: (h, 0, 0))
    return pl.pallas_call(
        attention_forward_kernel,
        grid=(H,),
        in_specs=[
            head_block(seq_len),
            head_block(seq_len, H),
            head_block(seq_len, 2 * H),
            pl.BlockSpec((2, seq_len, HD), lambda h: (0, 0, 0)),
            pl.BlockSpec((seq_len, 1), lambda h: (0, 0)),
            pl.BlockSpec((1, seq_len), lambda h: (0, 0)),
        ],
        out_specs=[head_block(seq_len)] * 3 + [probs_block, head_block(seq_len)],
        out_shape=[row] * 3 + [jax.ShapeDtypeStruct((H, seq_len, seq_len), F32), row],
        cost_estimate=BRIEF,
        name="attention_forward",
    )(projected, projected, projected, table, documents.reshape(seq_len, 1), documents.reshape(1, seq_len))


def attention_backward(grad_heads, query, key, value, probs, table):
    seq_len = grad_heads.shape[0]
    row = jax.ShapeDtypeStruct((seq_len, H * HD), BF)
    return pl.pallas_call(
        attention_backward_kernel,
        grid=(H,),
        in_specs=[head_block(seq_len)] * 4
        + [
            pl.BlockSpec((1, seq_len, seq_len), lambda h: (h, 0, 0)),
            pl.BlockSpec((2, seq_len, HD), lambda h: (0, 0, 0)),
        ],
        out_specs=[head_block(seq_len)] * 3,
        out_shape=[row] * 3,
        cost_estimate=BRIEF,
        name="attention_backward",
    )(grad_heads, query, key, value, probs, table)


def tile_of(first, columns):
    return max(n for n in range(128, 769, 128) if columns % n == 0 and first % n == 0)


def held_product(left, blocks, first, columns):
    rows, depth = left.shape
    tile = tile_of(first, columns)

    def kernel(left_ref, *refs):
        whole = jnp.concatenate([one[...] for one in refs[:-1]], axis=0)
        refs[-1][...] = contract(left_ref[...], whole, 1, 0)

    return pl.pallas_call(
        kernel,
        grid=(columns // tile,),
        in_specs=[pl.BlockSpec((rows, depth), lambda n: (0, 0))]
        + [pl.BlockSpec((one.shape[0], tile), lambda n: (0, first // tile + n)) for one in blocks],
        out_specs=pl.BlockSpec((rows, tile), lambda n: (0, n)),
        out_shape=jax.ShapeDtypeStruct((rows, columns), F32),
        cost_estimate=BRIEF,
        name="held_product",
    )(left, *blocks)


def held_product_back(left, blocks, first):
    rows, columns = left.shape
    depth = sum(one.shape[0] for one in blocks)
    tile = tile_of(first, columns)

    def kernel(left_ref, *refs):
        whole = jnp.concatenate([one[...] for one in refs[:-1]], axis=0)
        product = contract(left_ref[...], whole, 1, 1)

        @pl.when(pl.program_id(0) == 0)
        def _():
            refs[-1][...] = product

        @pl.when(pl.program_id(0) > 0)
        def _():
            refs[-1][...] += product

    return pl.pallas_call(
        kernel,
        grid=(columns // tile,),
        in_specs=[pl.BlockSpec((rows, tile), lambda n: (0, n))]
        + [pl.BlockSpec((one.shape[0], tile), lambda n: (0, first // tile + n)) for one in blocks],
        out_specs=pl.BlockSpec((rows, depth), lambda n: (0, 0)),
        out_shape=jax.ShapeDtypeStruct((rows, depth), F32),
        cost_estimate=BRIEF,
        name="held_product_back",
    )(left, *blocks)


class Order:
    def __init__(self):
        self.last = ()

    def enter(self, *values):
        held = lax.optimization_barrier(values + self.last)[: len(values)]
        return held[0] if len(values) == 1 else held

    def done(self, *values):
        self.last = values


class Rounds:
    def __init__(self, grid):
        self.grid = grid
        self.before = ()
        self.now = []

    def send(self, value, *move):
        arrived = self.grid.shift(after(value, *self.before), *move)
        self.now.append(arrived)
        return arrived

    def close(self):
        self.before, self.now = tuple(self.now), []


class Gather:
    def __init__(self, grid, rounds, block, merged):
        self.grid, self.rounds, self.merged = grid, rounds, merged
        self.held = {(0, 0, 0): block}
        self.halves = {}
        self.count = grid.z + grid.y + (1 if merged else 0) - 1 if grid.size > 1 else 0

    def round(self, r):
        grid, held = self.grid, self.held
        if r < grid.z - 1:
            held[(r + 1, 0, 0)] = self.rounds.send(held[(r, 0, 0)], 1, 0, 0)
        for j in range(grid.y - 1):
            if 0 <= r - j < grid.z:
                held[(r - j, j + 1, 0)] = self.rounds.send(held[(r - j, j, 0)], 0, 1, 0)
        if not self.merged:
            for j in range(grid.y):
                if 0 <= r - j < grid.z:
                    for k in range(1, grid.c):
                        held[(r - j, j, k)] = self.rounds.send(held[(r - j, j, k - 1)], 0, 0, 1)
            return
        for n, half in enumerate(grid.halves):
            if r == half[-1] + grid.y:
                stacks = [jnp.stack([held[place] for place in grid.places(half, 0)])]
                for _ in range(1, grid.c):
                    stacks.append(self.rounds.send(stacks[-1], 0, 0, 1))
                self.halves[n] = stacks


class Scatter:
    def __init__(self, grid, stage, half, make):
        self.grid, self.stage, self.make = grid, stage, make
        self.rows = len(half)

    def core(self):
        grid = self.grid
        if grid.c == 1:
            return
        total = self.make(grid.y * self.rows, grid.y * self.rows).astype(BF)
        self.stage.done(total)
        self.arrived = grid.shift(total, 0, 0, 1)

    def term(self, j):
        here = self.make(j * self.rows, self.rows)
        if self.grid.c > 1:
            here = here + self.arrived[j * self.rows : (j + 1) * self.rows].astype(F32)
        return here

    def along_y(self):
        grid = self.grid
        if grid.y == 1:
            return
        total = self.term(1).astype(BF)
        self.stage.done(total)
        self.total = grid.shift(total, 0, 1, 0)
        for j in range(2, grid.y):
            total = (self.term(j) + self.total.astype(F32)).astype(BF)
            self.stage.done(total)
            self.total = grid.shift(total, 0, 1, 0)

    def own(self):
        total = self.term(0)
        if self.grid.y > 1:
            total = total + self.total.astype(F32)
        total = total.astype(BF)
        self.stage.done(total)
        return total


class Grid:
    def __init__(self):
        self.size = lax.axis_size("grp")
        self.reps = lax.axis_size("rep")
        self.c = 2 if self.size % 2 == 0 else 1
        self.z = 4 if self.size % (4 * self.c) == 0 else 1
        self.y = self.size // (self.c * self.z)
        me = lax.axis_index("grp")
        self.my_c = me % self.c
        self.my_y = me // self.c % self.y
        self.my_z = me // (self.c * self.y)
        self.halves = ((0, 1), (2, 3)) if self.z == 4 else ((0,),)

    def flat(self, z, y, c):
        return (z % self.z * self.y + y % self.y) * self.c + c % self.c

    def shift(self, value, dz, dy, dc):
        pairs = [
            (self.flat(z, y, c), self.flat(z + dz, y + dy, c + dc))
            for z in range(self.z)
            for y in range(self.y)
            for c in range(self.c)
        ]
        return lax.ppermute(value, "grp", pairs)

    def source(self, step):
        return self.flat(
            self.my_z - step[0] + self.z, self.my_y - step[1] + self.y, self.my_c - step[2] + self.c
        )

    def places(self, half, k):
        return [(i, j, k) for j in range(self.y) for i in half]

    def order(self):
        return [
            place for half in self.halves for k in range(self.c) for place in self.places(half, k)
        ]

    def other_rep(self, value):
        if self.reps == 2:
            return lax.ppermute(value, "rep", [(0, 1), (1, 0)])
        return lax.psum(value, "rep")

    def both_reps(self, mine, theirs):
        if self.reps == 2:
            return mine.astype(F32) + theirs.astype(F32)
        return theirs.astype(F32)


def local(
    tokens,
    segments,
    routes,
    gates,
    gain_attn,
    w_qkv,
    w_out,
    gain_ffn,
    shared_gate,
    shared_up,
    shared_down,
    route_gate,
    route_up,
    route_down,
    cotangent,
):
    grid = Grid()
    seq_len, model_width = tokens.shape
    top_count = routes.shape[1]
    groups = grid.size
    expert_count = groups * route_gate.shape[0]
    capacity = 9 * seq_len * top_count // (8 * expert_count)
    slots = -(-capacity // 16) * 16
    hidden = shared_gate.shape[1] // groups
    width = gain_attn.shape[0]

    chosen = routes[:, :, None] == jnp.arange(expert_count, dtype=jnp.int32)[None, None, :]
    gate_table = jnp.sum(jnp.where(chosen, gates[:, :, None], 0.0), axis=1)
    gate_table = jnp.where(jnp.any(chosen, axis=1), gate_table, -1.0).T
    both_gains = jnp.concatenate([gain_attn, gain_ffn]).astype(F32)
    small = jnp.concatenate(
        [gate_table, jnp.broadcast_to(both_gains, (groups, 2 * width))], axis=1
    )
    small = lax.all_to_all(small, "grp", split_axis=0, concat_axis=0, tiled=True)

    sources = jnp.stack([grid.source(place) for place in grid.order()])
    held_feature = (sources[:, None] * width + jnp.arange(width, dtype=jnp.int32)[None, :]).reshape(-1)
    shuffle = (held_feature[:, None] == jnp.arange(model_width, dtype=jnp.int32)[None, :]).astype(BF)
    count = len(grid.halves)
    near = groups // count

    def chunk(values, n):
        size = values.shape[0] // count
        return values[n * size : (n + 1) * size]

    def to_held(values):
        return contract(values, shuffle, 1, 1).astype(BF)

    def from_held(values):
        high = lax.reduce_precision(values, 8, 7)
        both = jnp.concatenate([high.astype(BF), (values - high).astype(BF)])
        both = jnp.dot(both, shuffle, preferred_element_type=F32)
        return both[: values.shape[0]] + both[values.shape[0] :]

    rounds = Rounds(grid)
    qkv_width, inner = w_qkv.shape[1], w_out.shape[0]
    weights = Gather(grid, rounds, jnp.concatenate([w_qkv, w_out.T], axis=1), False)
    others = Gather(grid, rounds, cotangent, True)
    started = 0
    for r in range(weights.count):
        weights.round(r)
        if r >= grid.z:
            others.round(started)
            started += 1
        rounds.close()
        if r == 0:
            early = rounds.before
    blocks = [weights.held[place] for place in grid.order()]

    small = after(small, *early)
    attn_gain = small[:, seq_len : seq_len + width].reshape(-1)
    ffn_gain = small[:, seq_len + width :].reshape(-1)
    places = jnp.arange(seq_len, dtype=jnp.int32)
    gate_rows = small[:, :seq_len][sources]
    routed_here = gate_rows >= 0.0
    earlier = (places[:, None] < places[None, :]).astype(BF)
    position = jnp.dot(routed_here.astype(BF), earlier, preferred_element_type=F32)
    kept = routed_here & (position < capacity)
    gate_kept = jnp.where(kept, gate_rows, 0.0)
    hit = kept[:, None, :] & (
        position[:, None, :] == jnp.arange(slots, dtype=F32)[None, :, None]
    )
    slot_gate = jnp.sum(jnp.where(hit, gate_rows[:, None, :], 0.0), axis=-1)
    select = hit.astype(BF)
    expert_gate_w, expert_up_w, expert_down_w = route_gate[0], route_up[0], route_down[0]
    inside = expert_gate_w.shape[1]
    both_w = jnp.concatenate([after(expert_gate_w, *early), expert_up_w], axis=1)

    stage = Order()
    rows = after(tokens, *early).astype(F32)
    inverse_one = rms_scale(rows)
    normed_one = rows * inverse_one
    attn_in = (normed_one * attn_gain).astype(BF)
    attn_held, slot_gate, gate_kept, select, both_w = (
        lax.optimization_barrier(
            (to_held(attn_in), slot_gate, gate_kept, select, both_w)
        )
    )
    projected = held_product(attn_held, blocks, 0, qkv_width)
    table = jnp.asarray(rotary_tables(seq_len))

    def next_round(*held_back):
        nonlocal started
        if started < others.count:
            rounds.before += held_back
            others.round(started)
            started += 1
            rounds.close()

    next_round(projected)
    query, key, value, probs, attn_rows = attention_forward(projected, table, segments)
    next_round(attn_rows)
    residual = rows + from_held(held_product_back(attn_rows, blocks, qkv_width))
    inverse_two = rms_scale(residual)
    normed_two = residual * inverse_two
    ffn_in = (normed_two * ffn_gain).astype(BF)
    shared_gate, shared_up, shared_down = (
        after(one, ffn_in) for one in (shared_gate, shared_up, shared_down)
    )
    pieces = jnp.concatenate(
        [
            shared_gate.reshape(width, groups, hidden).transpose(1, 0, 2),
            shared_up.reshape(width, groups, hidden).transpose(1, 0, 2),
            shared_down.reshape(groups, hidden, width).transpose(0, 2, 1),
        ],
        axis=2,
    )
    pieces = lax.all_to_all(pieces, "grp", split_axis=0, concat_axis=0, tiled=True)
    pieces = pieces.reshape(model_width, 3 * hidden)

    stage.done(ffn_in)
    while started < others.count:
        next_round(ffn_in)
    rounds = Rounds(grid)
    ffn = Gather(grid, rounds, ffn_in, True)
    for r in range(ffn.count):
        ffn.round(r)
        rounds.close()

    def picked(selection, stacks):
        size = selection.shape[0] // len(stacks)
        return jnp.concatenate(
            [
                jnp.einsum(
                    "sct,std->scd",
                    selection[n * size : (n + 1) * size],
                    one,
                    preferred_element_type=F32,
                )
                for n, one in enumerate(stacks)
            ]
        )

    def each(stacks, right):
        return jnp.concatenate(
            [
                jnp.dot(one.reshape(-1, one.shape[2]), right, preferred_element_type=F32)
                for one in stacks
            ]
        )

    flat = (near * slots, model_width)

    def forward_part(n):
        selection = stage.enter(chunk(select, n))
        dy = others.halves[n]
        expert_in = picked(selection, ffn.halves[n]).astype(BF).reshape(flat)
        grad_out = picked(selection, dy) * chunk(slot_gate, n)[:, :, None]
        grad_out = grad_out.astype(BF).reshape(flat)
        both = jnp.dot(expert_in, both_w, preferred_element_type=F32)
        expert_hidden = (jax.nn.silu(both[:, :inside]) * both[:, inside:]).astype(BF)
        stage.done(both, expert_hidden, grad_out)
        return {"in": expert_in, "out": grad_out, "hidden": expert_hidden, "both": both}

    def backward_part(n, part):
        grad_out, both = stage.enter(part["out"], part["both"])
        gate_part, up_part = both[:, :inside], both[:, inside:]
        grad_hidden = contract(grad_out, expert_down_w, 1, 1)
        grad_both = jnp.concatenate(
            [
                (grad_hidden * up_part * silu_slope(gate_part)).astype(BF),
                (grad_hidden * jax.nn.silu(gate_part)).astype(BF),
            ],
            axis=1,
        )
        grad_both = after(grad_both)
        grad_in = contract(grad_both, both_w, 1, 1).astype(BF)
        if n == 0:
            held_pieces = after(pieces, grad_both)
            shared.extend([held_pieces[:, : 2 * hidden], held_pieces[:, 2 * hidden :]])
        shared_in, shared_back = shared
        shared_pre = each(ffn.halves[n], shared_in)
        gate_pre, up_pre = shared_pre[:, :hidden], shared_pre[:, hidden:]
        shared_silu = jax.nn.silu(gate_pre)
        grad_shared_hidden = each(others.halves[n], shared_back)
        grad_shared_pre = jnp.concatenate(
            [
                (grad_shared_hidden * up_pre * silu_slope(gate_pre)).astype(BF),
                (grad_shared_hidden * shared_silu).astype(BF),
            ],
            axis=1,
        )
        part["grad_both"] = grad_both
        part["shared"] = (shared_silu * up_pre).astype(BF)
        part["shared_pre"] = grad_shared_pre
        stage.done(grad_in, grad_shared_pre)
        return to_tokens(n, grad_in, None, grad_shared_pre, shared_in)

    def to_tokens(n, slot_rows, scale, shared_rows, shared_weight):
        slot_rows = slot_rows.reshape(near, slots, model_width)

        def make(first, size):
            mine = slice(first, first + size)
            selection = stage.enter(chunk(select, n)[mine])
            back = jnp.einsum(
                "sct,scd->std", selection, slot_rows[mine], preferred_element_type=F32
            )
            if scale is not None:
                back = back * scale[mine][:, :, None]
            shared_mine = shared_rows[first * seq_len : (first + size) * seq_len]
            return back + contract(shared_mine, shared_weight, 1, 1).reshape(back.shape)

        return Scatter(grid, stage, grid.halves[n], make)

    swap = grid.other_rep
    parts, backs, shared = [], [], []
    for n in range(count):
        parts.append(forward_part(n))
        if n:
            backs[n - 1].along_y()
        backs.append(backward_part(n, parts[n]))
        backs[n].core()

    def joined(key):
        return jnp.concatenate([part[key] for part in parts])

    class AlongZ:
        def __init__(self, halves):
            self.halves = halves

        def far(self):
            if grid.z == 4:
                far = self.halves[-1].own()
                self.whole = far
                self.passed_on = grid.shift(far[-2], 3, 0, 0)
                self.back_one = grid.shift(far[-1], 1, 0, 0)

        def near(self):
            close = self.whole if grid.z == 4 and len(self.halves) == 1 else self.halves[0].own()
            self.mine = close[0]
            if grid.z == 4:
                near = stage.enter(close[1]).astype(F32) + self.passed_on.astype(F32)
                near = near.astype(BF)
                stage.done(near)
                self.near_one = grid.shift(near, 3, 0, 0)

        def total(self):
            mine = stage.enter(self.mine).astype(F32)
            if grid.z == 4:
                mine = mine + self.back_one.astype(F32) + self.near_one.astype(F32)
            return mine

    down_left, down_right = stage.enter(joined("hidden"), joined("out"))
    down_mine = contract(down_left, down_right, 0, 0).astype(BF)
    stage.done(down_mine)
    down_theirs = swap(down_mine)
    backs[-1].along_y()
    both_left, both_right = stage.enter(joined("in"), joined("grad_both"))
    both_mine = contract(both_left, both_right, 0, 0).astype(BF)
    stage.done(both_mine)
    ffn_sum = AlongZ(backs)
    ffn_sum.far()

    outs = []
    for n in range(count):
        hidden_rows = stage.enter(parts[n]["hidden"])
        expert_out = jnp.dot(hidden_rows, expert_down_w, preferred_element_type=F32).astype(BF)
        stage.done(expert_out)
        outs.append(
            to_tokens(n, expert_out, chunk(gate_kept, n), parts[n]["shared"], shared[1])
        )
    for out in outs[::-1]:
        out.core()
    ffn_sum.near()
    for out in outs[::-1]:
        out.along_y()
    grad_ffn_in = ffn_sum.total()

    grad_norm_two, grad_ffn_gain = norm_backward(grad_ffn_in, normed_two, inverse_two, ffn_gain)
    grad_residual = cotangent.astype(F32) + grad_norm_two
    grad_attn_low = grad_residual.astype(BF)
    low_turned = contract(shuffle, grad_attn_low, 1, 1).astype(BF)
    grad_heads = held_product(low_turned.T, blocks, qkv_width, inner).astype(BF)
    stage.done(grad_heads)

    def products(half, turned, right):
        def make(first, size):
            rows = turned[first * width : (first + size) * width]
            product = jnp.dot(stage.enter(rows), right, preferred_element_type=F32)
            return product.reshape(size, width, right.shape[1])

        return Scatter(grid, stage, half, make)

    everywhere = sum(grid.halves, ())
    merged = low_turned.reshape(count, grid.c, grid.y, len(everywhere) // count, width, seq_len)
    merged = merged.transpose(1, 2, 0, 3, 4, 5).reshape(model_width, seq_len)
    tall = products(everywhere, merged, attn_rows)
    out_sum, tall_sum = AlongZ(outs), AlongZ([tall])
    tall.core()
    out_sum.far()
    tall.along_y()
    grad_route_down = grid.both_reps(stage.enter(down_mine), down_theirs)[None]
    stage.done(grad_route_down)
    both_theirs = swap(after(both_mine, down_theirs))
    grads = attention_backward(stage.enter(grad_heads), query, key, value, probs, table)
    grad_projected = jnp.concatenate(grads, axis=1)
    stage.done(grad_projected)
    turned_in = contract(shuffle, attn_in, 1, 1).astype(BF)
    wides = [products(half, chunk(turned_in, n), grad_projected) for n, half in enumerate(grid.halves)]
    wide_sum = AlongZ(wides)
    for wide in wides[::-1]:
        wide.core()
    out_sum.near()
    for wide in wides[::-1]:
        wide.along_y()
    tall_sum.far()
    grad_attn_held = held_product_back(stage.enter(grad_projected), blocks, 0)
    stage.done(grad_attn_held)
    wide_sum.far()
    grad_attn_in = from_held(stage.enter(grad_attn_held))
    grad_norm_one, grad_attn_gain = norm_backward(grad_attn_in, normed_one, inverse_one, attn_gain)
    grad_tokens = (grad_residual + grad_norm_one).astype(BF)
    stage.done(grad_tokens)
    tall_sum.near()
    mixed = (residual + out_sum.total()).astype(BF)
    stage.done(mixed)
    shared_left, shared_right = stage.enter(joined("shared_pre"), joined("shared"))

    def rows_of(stacks):
        return jnp.concatenate([one.reshape(-1, model_width) for half in stacks.values() for one in half])

    grad_pieces = jnp.concatenate(
        [
            contract(shared_left, rows_of(ffn.halves), 0, 0),
            contract(shared_right, rows_of(others.halves), 0, 0),
            grad_attn_gain[None],
            grad_ffn_gain[None],
        ]
    )
    grad_pieces = grad_pieces.astype(BF).T.reshape(groups, width, 3 * hidden + 2)
    stage.done(grad_pieces)
    grad_pieces = lax.all_to_all(grad_pieces, "grp", split_axis=0, concat_axis=0, tiled=True)
    wide_sum.near()
    grad_w_out = tall_sum.total().astype(BF)
    stage.done(grad_w_out)
    grad_w_out_there = swap(grad_w_out)
    grad_pieces = stage.enter(grad_pieces)
    stage.done(grad_pieces)
    grad_pieces_there = swap(grad_pieces)
    both_total = grid.both_reps(stage.enter(both_mine), both_theirs)
    grad_route_gate, grad_route_up = both_total[None, :, :inside], both_total[None, :, inside:]
    stage.done(grad_route_gate, grad_route_up)
    grad_w_qkv = wide_sum.total().astype(BF)
    stage.done(grad_w_qkv)
    grad_w_qkv_there = swap(grad_w_qkv)

    grad_w_out = grid.both_reps(grad_w_out, grad_w_out_there).T
    grad_pieces = grid.both_reps(grad_pieces, grad_pieces_there)
    grad_w_qkv = grid.both_reps(grad_w_qkv, grad_w_qkv_there)
    gain_grads = grad_pieces[:, :, 3 * hidden :].sum(axis=0)

    def join(part):
        return part.transpose(1, 0, 2).reshape(width, groups * hidden)

    grad_shared_gate = join(grad_pieces[:, :, :hidden])
    grad_shared_up = join(grad_pieces[:, :, hidden : 2 * hidden])
    grad_shared_down = join(grad_pieces[:, :, 2 * hidden : 3 * hidden]).T

    return (
        mixed,
        grad_tokens,
        gain_grads[:, 0],
        grad_w_qkv,
        grad_w_out,
        gain_grads[:, 1],
        grad_shared_gate,
        grad_shared_up,
        grad_shared_down,
        grad_route_gate,
        grad_route_up,
        grad_route_down,
    )


def solution(mesh):
    in_specs = (
        P(("rep", "grp"), None),
        P(("rep", "grp"), None),
        P(("rep", "grp"), None),
        P(("rep", "grp"), None),
        P("grp"),
        P("grp", None),
        P(None, "grp"),
        P("grp"),
        P("grp", None),
        P("grp", None),
        P(None, "grp"),
        P("grp", None, None),
        P("grp", None, None),
        P("grp", None, None),
        P(("rep", "grp"), None),
    )
    out_specs = (
        P(("rep", "grp"), None),
        P(("rep", "grp"), None),
        P("grp"),
        P("grp", None),
        P(None, "grp"),
        P("grp"),
        P("grp", None),
        P("grp", None),
        P(None, "grp"),
        P("grp", None, None),
        P("grp", None, None),
        P("grp", None, None),
    )
    return jax.shard_map(local, mesh=mesh, in_specs=in_specs, out_specs=out_specs, check_vma=False)
```

```python
import math

import jax
import jax.numpy as jnp
import numpy as np
from jax import lax
from jax.experimental import pallas as pl
from jax.experimental.pallas import tpu as pltpu
from jax.sharding import PartitionSpec as P

H = 10
HD = 128

EPSILON = 1e-06
MASKED_SCORE = -1000000000.0
BF = jnp.bfloat16
F32 = jnp.float32
BRIEF = pl.CostEstimate(flops=1, bytes_accessed=1, transcendentals=0)


def rms_scale(values):
    return lax.rsqrt(jnp.mean(values * values, axis=-1, keepdims=True) + EPSILON)


def rotary_tables(seq_len):
    half = HD // 2
    frequency = np.power(np.float32(10000.0), -2.0 * np.arange(half, dtype=np.float32) / HD)
    angle = np.arange(seq_len, dtype=np.float32)[:, None] * frequency.astype(np.float32)[None, :]
    cosine, sine = np.cos(angle), np.sin(angle)
    return np.stack(
        [np.concatenate([cosine, cosine], axis=1), np.concatenate([-sine, sine], axis=1)]
    ).astype(np.float32)


def contract(left, right, left_dim, right_dim):
    return lax.dot_general(
        left, right, (((left_dim,), (right_dim,)), ((), ())), preferred_element_type=F32
    )


def silu_slope(values):
    sigma = jax.nn.sigmoid(values)
    return sigma * (1.0 + values * (1.0 - sigma))


def norm_backward(grad_scaled, normed, inverse, gain):
    grad_normed = grad_scaled * gain
    grad_gain = jnp.sum(grad_scaled * normed, axis=0)
    grad_rows = inverse * (
        grad_normed - normed * jnp.mean(grad_normed * normed, axis=-1, keepdims=True)
    )
    return (grad_rows, grad_gain)


def after(value, *others):
    return lax.optimization_barrier((value,) + others)[0]


def attention_forward_kernel(q_in, k_in, v_in, table, doc_col, doc_row, q_ref, k_ref, v_ref, p_ref, o_ref):
    def turned(values):
        return (values * table[0] + pltpu.roll(values, HD // 2, 1) * table[1]).astype(BF)

    query, key, value = turned(q_in[...]), turned(k_in[...]), v_in[...].astype(BF)
    q_ref[...], k_ref[...], v_ref[...] = query, key, value
    scores = contract(query, key, 1, 1) / math.sqrt(HD)
    at = lax.broadcasted_iota(jnp.int32, scores.shape, 0)
    to = lax.broadcasted_iota(jnp.int32, scores.shape, 1)
    scores = jnp.where((at >= to) & (doc_col[...] == doc_row[...]), scores, MASKED_SCORE)
    raised = jnp.exp(scores - jnp.max(scores, axis=-1, keepdims=True))
    probs = raised / jnp.sum(raised, axis=-1, keepdims=True)
    p_ref[0] = probs
    o_ref[...] = contract(probs.astype(BF), value, 1, 0).astype(BF)


def attention_backward_kernel(g_ref, q_ref, k_ref, v_ref, p_ref, table, dq_ref, dk_ref, dv_ref):
    def turned_back(values):
        return (values * table[0] - pltpu.roll(values, HD // 2, 1) * table[1]).astype(BF)

    grad, probs = g_ref[...], p_ref[0]
    grad_probs = contract(grad, v_ref[...], 1, 1)
    dv_ref[...] = contract(probs.astype(BF), grad, 0, 0).astype(BF)
    mean = jnp.sum(grad_probs * probs, axis=-1, keepdims=True)
    grad_scores = (probs * (grad_probs - mean)).astype(BF)
    dq_ref[...] = turned_back(contract(grad_scores, k_ref[...], 1, 0) / math.sqrt(HD))
    dk_ref[...] = turned_back(contract(grad_scores, q_ref[...], 0, 0) / math.sqrt(HD))


def head_block(seq_len, offset=0):
    return pl.BlockSpec((seq_len, HD), lambda h: (0, offset + h))


def attention_forward(projected, table, documents):
    seq_len = projected.shape[0]
    row = jax.ShapeDtypeStruct((seq_len, H * HD), BF)
    probs_block = pl.BlockSpec((1, seq_len, seq_len), lambda h: (h, 0, 0))
    return pl.pallas_call(
        attention_forward_kernel,
        grid=(H,),
        in_specs=[
            head_block(seq_len),
            head_block(seq_len, H),
            head_block(seq_len, 2 * H),
            pl.BlockSpec((2, seq_len, HD), lambda h: (0, 0, 0)),
            pl.BlockSpec((seq_len, 1), lambda h: (0, 0)),
            pl.BlockSpec((1, seq_len), lambda h: (0, 0)),
        ],
        out_specs=[head_block(seq_len)] * 3 + [probs_block, head_block(seq_len)],
        out_shape=[row] * 3 + [jax.ShapeDtypeStruct((H, seq_len, seq_len), F32), row],
        cost_estimate=BRIEF,
        name="attention_forward",
    )(projected, projected, projected, table, documents.reshape(seq_len, 1), documents.reshape(1, seq_len))


def attention_backward(grad_heads, query, key, value, probs, table):
    seq_len = grad_heads.shape[0]
    row = jax.ShapeDtypeStruct((seq_len, H * HD), BF)
    return pl.pallas_call(
        attention_backward_kernel,
        grid=(H,),
        in_specs=[head_block(seq_len)] * 4
        + [
            pl.BlockSpec((1, seq_len, seq_len), lambda h: (h, 0, 0)),
            pl.BlockSpec((2, seq_len, HD), lambda h: (0, 0, 0)),
        ],
        out_specs=[head_block(seq_len)] * 3,
        out_shape=[row] * 3,
        cost_estimate=BRIEF,
        name="attention_backward",
    )(grad_heads, query, key, value, probs, table)


def tile_of(first, columns):
    return max(n for n in range(128, 769, 128) if columns % n == 0 and first % n == 0)


def held_product(left, blocks, first, columns):
    rows, depth = left.shape
    tile = tile_of(first, columns)

    def kernel(left_ref, *refs):
        whole = jnp.concatenate([one[...] for one in refs[:-1]], axis=0)
        refs[-1][...] = contract(left_ref[...], whole, 1, 0)

    return pl.pallas_call(
        kernel,
        grid=(columns // tile,),
        in_specs=[pl.BlockSpec((rows, depth), lambda n: (0, 0))]
        + [pl.BlockSpec((one.shape[0], tile), lambda n: (0, first // tile + n)) for one in blocks],
        out_specs=pl.BlockSpec((rows, tile), lambda n: (0, n)),
        out_shape=jax.ShapeDtypeStruct((rows, columns), F32),
        cost_estimate=BRIEF,
        name="held_product",
    )(left, *blocks)


def held_product_back(left, blocks, first):
    rows, columns = left.shape
    depth = sum(one.shape[0] for one in blocks)
    tile = tile_of(first, columns)

    def kernel(left_ref, *refs):
        whole = jnp.concatenate([one[...] for one in refs[:-1]], axis=0)
        product = contract(left_ref[...], whole, 1, 1)

        @pl.when(pl.program_id(0) == 0)
        def _():
            refs[-1][...] = product

        @pl.when(pl.program_id(0) > 0)
        def _():
            refs[-1][...] += product

    return pl.pallas_call(
        kernel,
        grid=(columns // tile,),
        in_specs=[pl.BlockSpec((rows, tile), lambda n: (0, n))]
        + [pl.BlockSpec((one.shape[0], tile), lambda n: (0, first // tile + n)) for one in blocks],
        out_specs=pl.BlockSpec((rows, depth), lambda n: (0, 0)),
        out_shape=jax.ShapeDtypeStruct((rows, depth), F32),
        cost_estimate=BRIEF,
        name="held_product_back",
    )(left, *blocks)


def token_grad(grad_held, shuffle, normed, inverse, gain, grad_rows):
    rows, width = normed.shape

    def kernel(held_ref, shuffle_ref, normed_ref, inverse_ref, gain_ref, rows_ref, out_ref, gain_grad_ref):
        held, unit = held_ref[...], normed_ref[...]
        high = held.astype(BF)
        low = (held - high.astype(F32)).astype(BF)
        grad = contract(high, shuffle_ref[...], 1, 0) + contract(low, shuffle_ref[...], 1, 0)
        gain_grad_ref[...] = jnp.sum(grad * unit, axis=0, keepdims=True)
        grad = grad * gain_ref[...]
        mean = jnp.sum(grad * unit, axis=-1, keepdims=True) / width
        out_ref[...] = (rows_ref[...] + inverse_ref[...] * (grad - unit * mean)).astype(BF)

    return pl.pallas_call(
        kernel,
        out_shape=[
            jax.ShapeDtypeStruct((rows, width), BF),
            jax.ShapeDtypeStruct((1, width), F32),
        ],
        cost_estimate=BRIEF,
        name="token_grad",
    )(grad_held, shuffle, normed, inverse, gain.reshape(1, width), grad_rows)


def sum_of_reps(mine, theirs, parts):
    rows, width = mine.shape
    size = width // parts
    tile = max(n for n in range(16, 257, 16) if rows % n == 0)

    def kernel(mine_ref, theirs_ref, *out_refs):
        for n, out_ref in enumerate(out_refs):
            at = slice(n * size, (n + 1) * size)
            out_ref[...] = mine_ref[:, at].astype(F32) + theirs_ref[:, at].astype(F32)

    return pl.pallas_call(
        kernel,
        grid=(rows // tile,),
        in_specs=[pl.BlockSpec((tile, width), lambda n: (n, 0))] * 2,
        out_specs=[pl.BlockSpec((tile, size), lambda n: (n, 0))] * parts,
        out_shape=[jax.ShapeDtypeStruct((rows, size), F32)] * parts,
        cost_estimate=BRIEF,
        name="sum_of_reps",
    )(mine, theirs)


class Order:
    def __init__(self):
        self.last = ()

    def enter(self, *values):
        held = lax.optimization_barrier(values + self.last)[: len(values)]
        return held[0] if len(values) == 1 else held

    def done(self, *values):
        self.last = values


class Rounds:
    def __init__(self, grid):
        self.grid = grid
        self.before = ()
        self.now = []

    def send(self, value, *move):
        arrived = self.grid.shift(after(value, *self.before), *move)
        self.now.append(arrived)
        return arrived

    def close(self):
        self.before, self.now = tuple(self.now), []


class Gather:
    def __init__(self, grid, rounds, block, merged):
        self.grid, self.rounds, self.merged = grid, rounds, merged
        self.held = {(0, 0, 0): block}
        self.halves = {}
        self.count = grid.z + grid.y + (1 if merged else 0) - 1 if grid.size > 1 else 0

    def round(self, r):
        grid, held = self.grid, self.held
        if r < grid.z - 1:
            held[(r + 1, 0, 0)] = self.rounds.send(held[(r, 0, 0)], 1, 0, 0)
        for j in range(grid.y - 1):
            if 0 <= r - j < grid.z:
                held[(r - j, j + 1, 0)] = self.rounds.send(held[(r - j, j, 0)], 0, 1, 0)
        if not self.merged:
            for j in range(grid.y):
                if 0 <= r - j < grid.z:
                    for k in range(1, grid.c):
                        held[(r - j, j, k)] = self.rounds.send(held[(r - j, j, k - 1)], 0, 0, 1)
            return
        for n, half in enumerate(grid.halves):
            if r == half[-1] + grid.y:
                stacks = [jnp.stack([held[place] for place in grid.places(half, 0)])]
                for _ in range(1, grid.c):
                    stacks.append(self.rounds.send(stacks[-1], 0, 0, 1))
                self.halves[n] = stacks


class Scatter:
    def __init__(self, grid, stage, half, make):
        self.grid, self.stage, self.make = grid, stage, make
        self.rows = len(half)

    def core(self):
        grid = self.grid
        if grid.c == 1:
            return
        total = self.make(grid.y * self.rows, grid.y * self.rows).astype(BF)
        self.stage.done(total)
        self.arrived = grid.shift(total, 0, 0, 1)

    def term(self, j):
        here = self.make(j * self.rows, self.rows)
        if self.grid.c > 1:
            here = here + self.arrived[j * self.rows : (j + 1) * self.rows].astype(F32)
        return here

    def along_y(self):
        grid = self.grid
        if grid.y == 1:
            return
        total = self.term(1).astype(BF)
        self.stage.done(total)
        self.total = grid.shift(total, 0, 1, 0)
        for j in range(2, grid.y):
            total = (self.term(j) + self.total.astype(F32)).astype(BF)
            self.stage.done(total)
            self.total = grid.shift(total, 0, 1, 0)

    def own(self):
        total = self.term(0)
        if self.grid.y > 1:
            total = total + self.total.astype(F32)
        total = total.astype(BF)
        self.stage.done(total)
        return total


class Grid:
    def __init__(self):
        self.size = lax.axis_size("grp")
        self.reps = lax.axis_size("rep")
        self.c = 2 if self.size % 2 == 0 else 1
        self.z = 4 if self.size % (4 * self.c) == 0 else 1
        self.y = self.size // (self.c * self.z)
        me = lax.axis_index("grp")
        self.my_c = me % self.c
        self.my_y = me // self.c % self.y
        self.my_z = me // (self.c * self.y)
        self.halves = ((0, 1), (2, 3)) if self.z == 4 else ((0,),)

    def flat(self, z, y, c):
        return (z % self.z * self.y + y % self.y) * self.c + c % self.c

    def shift(self, value, dz, dy, dc):
        pairs = [
            (self.flat(z, y, c), self.flat(z + dz, y + dy, c + dc))
            for z in range(self.z)
            for y in range(self.y)
            for c in range(self.c)
        ]
        return lax.ppermute(value, "grp", pairs)

    def source(self, step):
        return self.flat(
            self.my_z - step[0] + self.z, self.my_y - step[1] + self.y, self.my_c - step[2] + self.c
        )

    def places(self, half, k):
        return [(i, j, k) for j in range(self.y) for i in half]

    def order(self):
        return [
            place for half in self.halves for k in range(self.c) for place in self.places(half, k)
        ]

    def other_rep(self, value):
        if self.reps == 2:
            return lax.ppermute(value, "rep", [(0, 1), (1, 0)])
        return lax.psum(value, "rep")

    def parts_of_both(self, mine, theirs, parts):
        if self.reps == 2:
            return sum_of_reps(mine, theirs, parts)
        return [one.astype(F32) for one in jnp.split(theirs, parts, axis=1)]

    def both_reps(self, mine, theirs):
        if self.reps == 2:
            return mine.astype(F32) + theirs.astype(F32)
        return theirs.astype(F32)


def local(
    tokens,
    segments,
    routes,
    gates,
    gain_attn,
    w_qkv,
    w_out,
    gain_ffn,
    shared_gate,
    shared_up,
    shared_down,
    route_gate,
    route_up,
    route_down,
    cotangent,
):
    grid = Grid()
    seq_len, model_width = tokens.shape
    top_count = routes.shape[1]
    groups = grid.size
    expert_count = groups * route_gate.shape[0]
    capacity = 9 * seq_len * top_count // (8 * expert_count)
    slots = -(-capacity // 16) * 16
    hidden = shared_gate.shape[1] // groups
    width = gain_attn.shape[0]

    chosen = routes[:, :, None] == jnp.arange(expert_count, dtype=jnp.int32)[None, None, :]
    gate_table = jnp.sum(jnp.where(chosen, gates[:, :, None], 0.0), axis=1)
    gate_table = jnp.where(jnp.any(chosen, axis=1), gate_table, -1.0).T
    both_gains = jnp.concatenate([gain_attn, gain_ffn]).astype(F32)
    small = jnp.concatenate(
        [gate_table, jnp.broadcast_to(both_gains, (groups, 2 * width))], axis=1
    )
    small = lax.all_to_all(small, "grp", split_axis=0, concat_axis=0, tiled=True)

    sources = jnp.stack([grid.source(place) for place in grid.order()])
    held_feature = (sources[:, None] * width + jnp.arange(width, dtype=jnp.int32)[None, :]).reshape(-1)
    shuffle = (held_feature[:, None] == jnp.arange(model_width, dtype=jnp.int32)[None, :]).astype(BF)
    count = len(grid.halves)
    near = groups // count

    def chunk(values, n):
        size = values.shape[0] // count
        return values[n * size : (n + 1) * size]

    def to_held(values):
        return contract(values, shuffle, 1, 1).astype(BF)

    def from_held(values):
        high = lax.reduce_precision(values, 8, 7)
        both = jnp.concatenate([high.astype(BF), (values - high).astype(BF)])
        both = jnp.dot(both, shuffle, preferred_element_type=F32)
        return both[: values.shape[0]] + both[values.shape[0] :]

    rounds = Rounds(grid)
    qkv_width, inner = w_qkv.shape[1], w_out.shape[0]
    weights = Gather(grid, rounds, jnp.concatenate([w_qkv, w_out.T], axis=1), False)
    others = Gather(grid, rounds, cotangent, True)
    started = 0
    for r in range(weights.count):
        weights.round(r)
        if r >= grid.z:
            others.round(started)
            started += 1
        rounds.close()
        if r == 0:
            early = rounds.before
    blocks = [weights.held[place] for place in grid.order()]

    small = after(small, *early)
    attn_gain = small[:, seq_len : seq_len + width].reshape(-1)
    ffn_gain = small[:, seq_len + width :].reshape(-1)
    places = jnp.arange(seq_len, dtype=jnp.int32)
    gate_rows = small[:, :seq_len][sources]
    routed_here = gate_rows >= 0.0
    earlier = (places[:, None] < places[None, :]).astype(BF)
    position = jnp.dot(routed_here.astype(BF), earlier, preferred_element_type=F32)
    kept = routed_here & (position < capacity)
    gate_kept = jnp.where(kept, gate_rows, 0.0)
    hit = kept[:, None, :] & (
        position[:, None, :] == jnp.arange(slots, dtype=F32)[None, :, None]
    )
    slot_gate = jnp.sum(jnp.where(hit, gate_rows[:, None, :], 0.0), axis=-1)
    select = hit.astype(BF)
    expert_gate_w, expert_up_w, expert_down_w = route_gate[0], route_up[0], route_down[0]
    inside = expert_gate_w.shape[1]
    both_w = jnp.concatenate([after(expert_gate_w, *early), expert_up_w], axis=1)

    stage = Order()
    rows = after(tokens, *early).astype(F32)
    inverse_one = rms_scale(rows)
    normed_one = rows * inverse_one
    attn_in = (normed_one * attn_gain).astype(BF)
    attn_held, slot_gate, gate_kept, select, both_w = (
        lax.optimization_barrier(
            (to_held(attn_in), slot_gate, gate_kept, select, both_w)
        )
    )
    projected = held_product(attn_held, blocks, 0, qkv_width)
    table = jnp.asarray(rotary_tables(seq_len))

    def next_round(*held_back):
        nonlocal started
        if started < others.count:
            rounds.before += held_back
            others.round(started)
            started += 1
            rounds.close()

    next_round(projected)
    query, key, value, probs, attn_rows = attention_forward(projected, table, segments)
    next_round(attn_rows)
    residual = rows + from_held(held_product_back(attn_rows, blocks, qkv_width))
    inverse_two = rms_scale(residual)
    normed_two = residual * inverse_two
    ffn_in = (normed_two * ffn_gain).astype(BF)
    shared_gate, shared_up, shared_down = (
        after(one, ffn_in) for one in (shared_gate, shared_up, shared_down)
    )
    pieces = jnp.concatenate(
        [
            shared_gate.reshape(width, groups, hidden).transpose(1, 0, 2),
            shared_up.reshape(width, groups, hidden).transpose(1, 0, 2),
            shared_down.reshape(groups, hidden, width).transpose(0, 2, 1),
        ],
        axis=2,
    )
    pieces = lax.all_to_all(pieces, "grp", split_axis=0, concat_axis=0, tiled=True)
    pieces = pieces.reshape(model_width, 3 * hidden)

    stage.done(ffn_in)
    while started < others.count:
        next_round(ffn_in)
    rounds = Rounds(grid)
    ffn = Gather(grid, rounds, ffn_in, True)
    for r in range(ffn.count):
        ffn.round(r)
        rounds.close()

    def picked(selection, stacks):
        size = selection.shape[0] // len(stacks)
        return jnp.concatenate(
            [
                jnp.einsum(
                    "sct,std->scd",
                    selection[n * size : (n + 1) * size],
                    one,
                    preferred_element_type=F32,
                )
                for n, one in enumerate(stacks)
            ]
        )

    def each(stacks, right):
        return jnp.concatenate(
            [
                jnp.dot(one.reshape(-1, one.shape[2]), right, preferred_element_type=F32)
                for one in stacks
            ]
        )

    flat = (near * slots, model_width)

    def forward_part(n):
        selection = stage.enter(chunk(select, n))
        dy = others.halves[n]
        expert_in = picked(selection, ffn.halves[n]).astype(BF).reshape(flat)
        grad_out = picked(selection, dy) * chunk(slot_gate, n)[:, :, None]
        grad_out = grad_out.astype(BF).reshape(flat)
        both = jnp.dot(expert_in, both_w, preferred_element_type=F32)
        expert_hidden = (jax.nn.silu(both[:, :inside]) * both[:, inside:]).astype(BF)
        stage.done(both, expert_hidden, grad_out)
        return {"in": expert_in, "out": grad_out, "hidden": expert_hidden, "both": both}

    def backward_part(n, part):
        grad_out, both = stage.enter(part["out"], part["both"])
        gate_part, up_part = both[:, :inside], both[:, inside:]
        grad_hidden = contract(grad_out, expert_down_w, 1, 1)
        grad_both = jnp.concatenate(
            [
                (grad_hidden * up_part * silu_slope(gate_part)).astype(BF),
                (grad_hidden * jax.nn.silu(gate_part)).astype(BF),
            ],
            axis=1,
        )
        grad_both = after(grad_both)
        grad_in = contract(grad_both, both_w, 1, 1).astype(BF)
        if n == 0:
            held_pieces = after(pieces, grad_both)
            shared.extend([held_pieces[:, : 2 * hidden], held_pieces[:, 2 * hidden :]])
        shared_in, shared_back = shared
        shared_pre = each(ffn.halves[n], shared_in)
        gate_pre, up_pre = shared_pre[:, :hidden], shared_pre[:, hidden:]
        shared_silu = jax.nn.silu(gate_pre)
        grad_shared_hidden = each(others.halves[n], shared_back)
        grad_shared_pre = jnp.concatenate(
            [
                (grad_shared_hidden * up_pre * silu_slope(gate_pre)).astype(BF),
                (grad_shared_hidden * shared_silu).astype(BF),
            ],
            axis=1,
        )
        part["grad_both"] = grad_both
        part["shared"] = (shared_silu * up_pre).astype(BF)
        part["shared_pre"] = grad_shared_pre
        stage.done(grad_in, grad_shared_pre)
        return to_tokens(n, grad_in, None, grad_shared_pre, shared_in)

    def to_tokens(n, slot_rows, scale, shared_rows, shared_weight):
        slot_rows = slot_rows.reshape(near, slots, model_width)

        def make(first, size):
            mine = slice(first, first + size)
            selection = stage.enter(chunk(select, n)[mine])
            back = jnp.einsum(
                "sct,scd->std", selection, slot_rows[mine], preferred_element_type=F32
            )
            if scale is not None:
                back = back * scale[mine][:, :, None]
            shared_mine = shared_rows[first * seq_len : (first + size) * seq_len]
            return back + contract(shared_mine, shared_weight, 1, 1).reshape(back.shape)

        return Scatter(grid, stage, grid.halves[n], make)

    swap = grid.other_rep
    parts, backs, shared = [], [], []
    for n in range(count):
        parts.append(forward_part(n))
        if n:
            backs[n - 1].along_y()
        backs.append(backward_part(n, parts[n]))
        backs[n].core()

    def joined(key):
        return jnp.concatenate([part[key] for part in parts])

    class AlongZ:
        def __init__(self, halves):
            self.halves = halves

        def far(self):
            if grid.z == 4:
                far = self.halves[-1].own()
                self.whole = far
                self.passed_on = grid.shift(far[-2], 3, 0, 0)
                self.back_one = grid.shift(far[-1], 1, 0, 0)

        def near(self):
            if grid.z != 4:
                self.mine = self.halves[0].own()[0]
                return
            if len(self.halves) == 1:
                near = stage.enter(self.whole[1]).astype(F32) + self.passed_on.astype(F32)
                self.mine = self.whole[0].astype(F32) + self.back_one.astype(F32)
                self.back_one = None
                stage.done(self.mine)
                near = stage.enter(near)
            else:
                half = self.halves[0]
                total = half.term(0)
                near = after(stage.enter(total[1]) + self.passed_on.astype(F32))
                stage.done(near)
                self.mine = total[0]
                if grid.y > 1:
                    near = near + half.total[1].astype(F32)
                    self.mine = total[0] + half.total[0].astype(F32)
            near = near.astype(BF)
            stage.done(near)
            self.near_one = grid.shift(near, 3, 0, 0)

        def total(self):
            mine = stage.enter(self.mine).astype(F32)
            if grid.z == 4:
                if self.back_one is not None:
                    mine = mine + self.back_one.astype(F32)
                mine = mine + self.near_one.astype(F32)
            return mine

    down_left, down_right = stage.enter(joined("hidden"), joined("out"))
    down_mine = contract(down_left, down_right, 0, 0).astype(BF)
    stage.done(down_mine)
    down_theirs = swap(down_mine)
    backs[-1].along_y()
    both_left, both_right = stage.enter(joined("in"), joined("grad_both"))
    both_mine = contract(both_left, both_right, 0, 0).astype(BF)
    stage.done(both_mine)
    ffn_sum = AlongZ(backs)
    ffn_sum.far()

    outs = []
    for n in range(count):
        hidden_rows = stage.enter(parts[n]["hidden"])
        expert_out = jnp.dot(hidden_rows, expert_down_w, preferred_element_type=F32).astype(BF)
        stage.done(expert_out)
        outs.append(
            to_tokens(n, expert_out, chunk(gate_kept, n), parts[n]["shared"], shared[1])
        )
    for out in outs[::-1]:
        out.core()
    ffn_sum.near()
    for out in outs[::-1]:
        out.along_y()
    grad_ffn_in = ffn_sum.total()

    grad_norm_two, grad_ffn_gain = norm_backward(grad_ffn_in, normed_two, inverse_two, ffn_gain)
    grad_residual = cotangent.astype(F32) + grad_norm_two
    grad_attn_low = grad_residual.astype(BF)
    low_turned = contract(shuffle, grad_attn_low, 1, 1).astype(BF)
    grad_heads = held_product(low_turned.T, blocks, qkv_width, inner).astype(BF)
    stage.done(grad_heads)

    def products(half, turned, right):
        def make(first, size):
            rows = turned[first * width : (first + size) * width]
            product = jnp.dot(stage.enter(rows), right, preferred_element_type=F32)
            return product.reshape(size, width, right.shape[1])

        return Scatter(grid, stage, half, make)

    everywhere = sum(grid.halves, ())
    merged = low_turned.reshape(count, grid.c, grid.y, len(everywhere) // count, width, seq_len)
    merged = merged.transpose(1, 2, 0, 3, 4, 5).reshape(model_width, seq_len)
    tall = products(everywhere, merged, attn_rows)
    out_sum, tall_sum = AlongZ(outs), AlongZ([tall])
    tall.core()
    both_theirs = swap(after(both_mine, down_theirs))
    grads = attention_backward(stage.enter(grad_heads), query, key, value, probs, table)
    grad_projected = jnp.concatenate(grads, axis=1)
    stage.done(grad_projected)
    turned_in = contract(shuffle, attn_in, 1, 1).astype(BF)
    wides = [products(half, chunk(turned_in, n), grad_projected) for n, half in enumerate(grid.halves)]
    wide_sum = AlongZ(wides)
    out_sum.far()
    tall.along_y()
    for wide in wides[::-1]:
        wide.core()
    out_sum.near()
    for wide in wides[::-1]:
        wide.along_y()
    grad_attn_held = held_product_back(stage.enter(grad_projected), blocks, 0)
    stage.done(grad_attn_held)
    tall_sum.far()
    grad_tokens, grad_attn_gain = token_grad(
        stage.enter(grad_attn_held), shuffle, normed_one, inverse_one, attn_gain, grad_residual
    )
    stage.done(grad_tokens)
    mixed = (residual + out_sum.total()).astype(BF)
    stage.done(mixed)
    tall_sum.near()
    (grad_route_down,) = grid.parts_of_both(stage.enter(down_mine), down_theirs, 1)
    stage.done(grad_route_down)
    wide_sum.far()
    shared_left, shared_right = stage.enter(joined("shared_pre"), joined("shared"))

    def rows_of(stacks):
        return jnp.concatenate([one.reshape(-1, model_width) for half in stacks.values() for one in half])

    grad_pieces = jnp.concatenate(
        [
            contract(shared_left, rows_of(ffn.halves), 0, 0),
            contract(shared_right, rows_of(others.halves), 0, 0),
            grad_attn_gain,
            grad_ffn_gain[None],
        ]
    )
    grad_pieces = grad_pieces.astype(BF)
    stage.done(grad_pieces)
    grad_pieces_there = swap(grad_pieces)
    grad_route_gate, grad_route_up = grid.parts_of_both(stage.enter(both_mine), both_theirs, 2)
    stage.done(grad_route_gate, grad_route_up)
    grad_pieces = grid.both_reps(stage.enter(grad_pieces), grad_pieces_there).astype(BF)
    grad_pieces = grad_pieces.T.reshape(groups, width, 3 * hidden + 2)
    stage.done(grad_pieces)
    grad_pieces = lax.all_to_all(grad_pieces, "grp", split_axis=0, concat_axis=0, tiled=True)
    wide_sum.near()
    grad_w_out = tall_sum.total().astype(BF)
    stage.done(grad_w_out)
    grad_w_out_there = swap(grad_w_out)
    grad_w_qkv = wide_sum.total().astype(BF)
    stage.done(grad_w_qkv)
    grad_w_qkv_there = swap(grad_w_qkv)
    grad_route_down, grad_route_gate, grad_route_up = (
        one[None] for one in (grad_route_down, grad_route_gate, grad_route_up)
    )

    grad_w_out = grid.both_reps(grad_w_out, grad_w_out_there).T
    grad_pieces = stage.enter(grad_pieces).astype(F32)
    grad_w_qkv = grid.both_reps(grad_w_qkv, grad_w_qkv_there)
    gain_grads = grad_pieces[:, :, 3 * hidden :].sum(axis=0)

    def join(part):
        return part.transpose(1, 0, 2).reshape(width, groups * hidden)

    grad_shared_gate = join(grad_pieces[:, :, :hidden])
    grad_shared_up = join(grad_pieces[:, :, hidden : 2 * hidden])
    grad_shared_down = join(grad_pieces[:, :, 2 * hidden : 3 * hidden]).T

    return (
        mixed,
        grad_tokens,
        gain_grads[:, 0],
        grad_w_qkv,
        grad_w_out,
        gain_grads[:, 1],
        grad_shared_gate,
        grad_shared_up,
        grad_shared_down,
        grad_route_gate,
        grad_route_up,
        grad_route_down,
    )


def solution(mesh):
    in_specs = (
        P(("rep", "grp"), None),
        P(("rep", "grp"), None),
        P(("rep", "grp"), None),
        P(("rep", "grp"), None),
        P("grp"),
        P("grp", None),
        P(None, "grp"),
        P("grp"),
        P("grp", None),
        P("grp", None),
        P(None, "grp"),
        P("grp", None, None),
        P("grp", None, None),
        P("grp", None, None),
        P(("rep", "grp"), None),
    )
    out_specs = (
        P(("rep", "grp"), None),
        P(("rep", "grp"), None),
        P("grp"),
        P("grp", None),
        P(None, "grp"),
        P("grp"),
        P("grp", None),
        P("grp", None),
        P(None, "grp"),
        P("grp", None, None),
        P("grp", None, None),
        P("grp", None, None),
    )
    return jax.shard_map(local, mesh=mesh, in_specs=in_specs, out_specs=out_specs, check_vma=False)
```

```python
import math

import jax
import jax.numpy as jnp
import numpy as np
from jax import lax
from jax.experimental import pallas as pl
from jax.experimental.pallas import tpu as pltpu
from jax.sharding import PartitionSpec as P

H = 10
HD = 128
HEADS_AT_ONCE = 5

EPSILON = 1e-06
MASKED_SCORE = -1000000000.0
BF = jnp.bfloat16
F32 = jnp.float32
BRIEF = pl.CostEstimate(flops=1, bytes_accessed=1, transcendentals=0)


def rms_scale(values):
    return lax.rsqrt(jnp.mean(values * values, axis=-1, keepdims=True) + EPSILON)


def rotary_tables(seq_len):
    half = HD // 2
    frequency = np.power(np.float32(10000.0), -2.0 * np.arange(half, dtype=np.float32) / HD)
    angle = np.arange(seq_len, dtype=np.float32)[:, None] * frequency.astype(np.float32)[None, :]
    cosine, sine = np.cos(angle), np.sin(angle)
    return np.stack(
        [np.concatenate([cosine, cosine], axis=1), np.concatenate([-sine, sine], axis=1)]
    ).astype(np.float32)


def contract(left, right, left_dim, right_dim):
    return lax.dot_general(
        left, right, (((left_dim,), (right_dim,)), ((), ())), preferred_element_type=F32
    )


def silu_slope(values):
    sigma = jax.nn.sigmoid(values)
    return sigma * (1.0 + values * (1.0 - sigma))


def norm_backward(grad_scaled, normed, inverse, gain):
    grad_normed = grad_scaled * gain
    grad_gain = jnp.sum(grad_scaled * normed, axis=0)
    grad_rows = inverse * (
        grad_normed - normed * jnp.mean(grad_normed * normed, axis=-1, keepdims=True)
    )
    return (grad_rows, grad_gain)


def after(value, *others):
    return lax.optimization_barrier((value,) + others)[0]


def attention_forward_kernel(q_in, k_in, v_in, table, doc_col, doc_row, q_ref, k_ref, v_ref, p_ref, o_ref):
    def turned(values):
        return (values * table[0] + pltpu.roll(values, HD // 2, 1) * table[1]).astype(BF)

    for n in range(HEADS_AT_ONCE):
        at = slice(n * HD, (n + 1) * HD)
        query, key, value = turned(q_in[:, at]), turned(k_in[:, at]), v_in[:, at].astype(BF)
        q_ref[:, at], k_ref[:, at], v_ref[:, at] = query, key, value
        scores = contract(query, key, 1, 1) / math.sqrt(HD)
        row = lax.broadcasted_iota(jnp.int32, scores.shape, 0)
        column = lax.broadcasted_iota(jnp.int32, scores.shape, 1)
        allowed = (row >= column) & (doc_col[...] == doc_row[...])
        scores = jnp.where(allowed, scores, MASKED_SCORE)
        raised = jnp.exp(scores - jnp.max(scores, axis=-1, keepdims=True))
        probs = raised / jnp.sum(raised, axis=-1, keepdims=True)
        p_ref[n] = probs
        o_ref[:, at] = contract(probs.astype(BF), value, 1, 0).astype(BF)


def attention_backward_kernel(g_ref, q_ref, k_ref, v_ref, p_ref, table, dq_ref, dk_ref, dv_ref):
    def turned_back(values):
        return (values * table[0] - pltpu.roll(values, HD // 2, 1) * table[1]).astype(BF)

    for n in range(HEADS_AT_ONCE):
        at = slice(n * HD, (n + 1) * HD)
        grad, probs = g_ref[:, at], p_ref[n]
        grad_probs = contract(grad, v_ref[:, at], 1, 1)
        dv_ref[:, at] = contract(probs.astype(BF), grad, 0, 0).astype(BF)
        mean = jnp.sum(grad_probs * probs, axis=-1, keepdims=True)
        grad_scores = (probs * (grad_probs - mean)).astype(BF)
        dq_ref[:, at] = turned_back(contract(grad_scores, k_ref[:, at], 1, 0) / math.sqrt(HD))
        dk_ref[:, at] = turned_back(contract(grad_scores, q_ref[:, at], 0, 0) / math.sqrt(HD))


def head_block(seq_len, offset=0):
    return pl.BlockSpec((seq_len, HEADS_AT_ONCE * HD), lambda h: (0, offset // HEADS_AT_ONCE + h))


def attention_forward(projected, table, documents):
    seq_len = projected.shape[0]
    row = jax.ShapeDtypeStruct((seq_len, H * HD), BF)
    probs_block = pl.BlockSpec((HEADS_AT_ONCE, seq_len, seq_len), lambda h: (h, 0, 0))
    return pl.pallas_call(
        attention_forward_kernel,
        grid=(H // HEADS_AT_ONCE,),
        in_specs=[
            head_block(seq_len),
            head_block(seq_len, H),
            head_block(seq_len, 2 * H),
            pl.BlockSpec((2, seq_len, HD), lambda h: (0, 0, 0)),
            pl.BlockSpec((seq_len, 1), lambda h: (0, 0)),
            pl.BlockSpec((1, seq_len), lambda h: (0, 0)),
        ],
        out_specs=[head_block(seq_len)] * 3 + [probs_block, head_block(seq_len)],
        out_shape=[row] * 3 + [jax.ShapeDtypeStruct((H, seq_len, seq_len), F32), row],
        cost_estimate=BRIEF,
        name="attention_forward",
    )(projected, projected, projected, table, documents.reshape(seq_len, 1), documents.reshape(1, seq_len))


def attention_backward(grad_heads, query, key, value, probs, table):
    seq_len = grad_heads.shape[0]
    row = jax.ShapeDtypeStruct((seq_len, H * HD), BF)
    return pl.pallas_call(
        attention_backward_kernel,
        grid=(H // HEADS_AT_ONCE,),
        in_specs=[head_block(seq_len)] * 4
        + [
            pl.BlockSpec((HEADS_AT_ONCE, seq_len, seq_len), lambda h: (h, 0, 0)),
            pl.BlockSpec((2, seq_len, HD), lambda h: (0, 0, 0)),
        ],
        out_specs=[head_block(seq_len)] * 3,
        out_shape=[row] * 3,
        cost_estimate=BRIEF,
        name="attention_backward",
    )(grad_heads, query, key, value, probs, table)


def tile_of(first, columns):
    most = max(columns // 3, 640)
    return max(n for n in range(128, most + 1, 128) if columns % n == 0 and first % n == 0)


def held_product(left, blocks, first, columns):
    rows, depth = left.shape
    tile = tile_of(first, columns)

    def kernel(left_ref, *refs):
        whole = jnp.concatenate([one[...] for one in refs[:-1]], axis=0)
        refs[-1][...] = contract(left_ref[...], whole, 1, 0)

    return pl.pallas_call(
        kernel,
        grid=(columns // tile,),
        in_specs=[pl.BlockSpec((rows, depth), lambda n: (0, 0))]
        + [pl.BlockSpec((one.shape[0], tile), lambda n: (0, first // tile + n)) for one in blocks],
        out_specs=pl.BlockSpec((rows, tile), lambda n: (0, n)),
        out_shape=jax.ShapeDtypeStruct((rows, columns), F32),
        cost_estimate=BRIEF,
        name="held_product",
    )(left, *blocks)


def held_product_back(left, blocks, first):
    rows, columns = left.shape
    depth = sum(one.shape[0] for one in blocks)
    tile = tile_of(first, columns)

    def kernel(left_ref, *refs):
        whole = jnp.concatenate([one[...] for one in refs[:-1]], axis=0)
        product = contract(left_ref[...], whole, 1, 1)

        @pl.when(pl.program_id(0) == 0)
        def _():
            refs[-1][...] = product

        @pl.when(pl.program_id(0) > 0)
        def _():
            refs[-1][...] += product

    return pl.pallas_call(
        kernel,
        grid=(columns // tile,),
        in_specs=[pl.BlockSpec((rows, tile), lambda n: (0, n))]
        + [pl.BlockSpec((one.shape[0], tile), lambda n: (0, first // tile + n)) for one in blocks],
        out_specs=pl.BlockSpec((rows, depth), lambda n: (0, 0)),
        out_shape=jax.ShapeDtypeStruct((rows, depth), F32),
        cost_estimate=BRIEF,
        name="held_product_back",
    )(left, *blocks)


def token_grad(grad_held, shuffle, normed, inverse, gain, grad_rows):
    rows, width = normed.shape

    def kernel(held_ref, shuffle_ref, normed_ref, inverse_ref, gain_ref, rows_ref, out_ref, gain_grad_ref):
        held, unit = held_ref[...], normed_ref[...]
        high = held.astype(BF)
        low = (held - high.astype(F32)).astype(BF)
        grad = contract(high, shuffle_ref[...], 1, 0) + contract(low, shuffle_ref[...], 1, 0)
        gain_grad_ref[...] = jnp.sum(grad * unit, axis=0, keepdims=True)
        grad = grad * gain_ref[...]
        mean = jnp.sum(grad * unit, axis=-1, keepdims=True) / width
        out_ref[...] = (rows_ref[...] + inverse_ref[...] * (grad - unit * mean)).astype(BF)

    return pl.pallas_call(
        kernel,
        out_shape=[
            jax.ShapeDtypeStruct((rows, width), BF),
            jax.ShapeDtypeStruct((1, width), F32),
        ],
        cost_estimate=BRIEF,
        name="token_grad",
    )(grad_held, shuffle, normed, inverse, gain.reshape(1, width), grad_rows)


def sum_of_reps(mine, theirs, parts):
    rows, width = mine.shape
    size = width // parts
    tile = max(n for n in range(16, 257, 16) if rows % n == 0)

    def kernel(mine_ref, theirs_ref, *out_refs):
        for n, out_ref in enumerate(out_refs):
            at = slice(n * size, (n + 1) * size)
            out_ref[...] = mine_ref[:, at].astype(F32) + theirs_ref[:, at].astype(F32)

    return pl.pallas_call(
        kernel,
        grid=(rows // tile,),
        in_specs=[pl.BlockSpec((tile, width), lambda n: (n, 0))] * 2,
        out_specs=[pl.BlockSpec((tile, size), lambda n: (n, 0))] * parts,
        out_shape=[jax.ShapeDtypeStruct((rows, size), F32)] * parts,
        cost_estimate=BRIEF,
        name="sum_of_reps",
    )(mine, theirs)


class Order:
    def __init__(self):
        self.last = ()

    def enter(self, *values):
        held = lax.optimization_barrier(values + self.last)[: len(values)]
        return held[0] if len(values) == 1 else held

    def done(self, *values):
        self.last = values


class Rounds:
    def __init__(self, grid):
        self.grid = grid
        self.before = ()
        self.now = []

    def send(self, value, *move):
        arrived = self.grid.shift(after(value, *self.before), *move)
        self.now.append(arrived)
        return arrived

    def close(self):
        self.before, self.now = tuple(self.now), []


class Gather:
    def __init__(self, grid, rounds, block, merged):
        self.grid, self.rounds, self.merged = grid, rounds, merged
        self.held = {(0, 0, 0): block}
        self.halves = {}
        self.count = grid.z + grid.y + (1 if merged else 0) - 1 if grid.size > 1 else 0

    def round(self, r):
        grid, held = self.grid, self.held
        if r < grid.z - 1:
            held[(r + 1, 0, 0)] = self.rounds.send(held[(r, 0, 0)], 1, 0, 0)
        for j in range(grid.y - 1):
            if 0 <= r - j < grid.z:
                held[(r - j, j + 1, 0)] = self.rounds.send(held[(r - j, j, 0)], 0, 1, 0)
        if not self.merged:
            for j in range(grid.y):
                if 0 <= r - j < grid.z:
                    for k in range(1, grid.c):
                        held[(r - j, j, k)] = self.rounds.send(held[(r - j, j, k - 1)], 0, 0, 1)
            return
        for n, half in enumerate(grid.halves):
            if r == half[-1] + grid.y:
                stacks = [jnp.stack([held[place] for place in grid.places(half, 0)])]
                for _ in range(1, grid.c):
                    stacks.append(self.rounds.send(stacks[-1], 0, 0, 1))
                self.halves[n] = stacks


class Scatter:
    def __init__(self, grid, stage, half, make):
        self.grid, self.stage, self.make = grid, stage, make
        self.rows = len(half)

    def core(self):
        grid = self.grid
        if grid.c == 1:
            return
        total = self.make(grid.y * self.rows, grid.y * self.rows).astype(BF)
        self.stage.done(total)
        self.arrived = grid.shift(total, 0, 0, 1)

    def term(self, j):
        here = self.make(j * self.rows, self.rows)
        if self.grid.c > 1:
            here = here + self.arrived[j * self.rows : (j + 1) * self.rows].astype(F32)
        return here

    def along_y(self):
        grid = self.grid
        if grid.y == 1:
            return
        total = self.term(1).astype(BF)
        self.stage.done(total)
        self.total = grid.shift(total, 0, 1, 0)
        for j in range(2, grid.y):
            total = (self.term(j) + self.total.astype(F32)).astype(BF)
            self.stage.done(total)
            self.total = grid.shift(total, 0, 1, 0)

    def own(self):
        total = self.term(0)
        if self.grid.y > 1:
            total = total + self.total.astype(F32)
        total = total.astype(BF)
        self.stage.done(total)
        return total


class Grid:
    def __init__(self):
        self.size = lax.axis_size("grp")
        self.reps = lax.axis_size("rep")
        self.c = 2 if self.size % 2 == 0 else 1
        self.z = 4 if self.size % (4 * self.c) == 0 else 1
        self.y = self.size // (self.c * self.z)
        me = lax.axis_index("grp")
        self.my_c = me % self.c
        self.my_y = me // self.c % self.y
        self.my_z = me // (self.c * self.y)
        self.halves = ((0, 1), (2, 3)) if self.z == 4 else ((0,),)

    def flat(self, z, y, c):
        return (z % self.z * self.y + y % self.y) * self.c + c % self.c

    def shift(self, value, dz, dy, dc):
        pairs = [
            (self.flat(z, y, c), self.flat(z + dz, y + dy, c + dc))
            for z in range(self.z)
            for y in range(self.y)
            for c in range(self.c)
        ]
        return lax.ppermute(value, "grp", pairs)

    def source(self, step):
        return self.flat(
            self.my_z - step[0] + self.z, self.my_y - step[1] + self.y, self.my_c - step[2] + self.c
        )

    def places(self, half, k):
        return [(i, j, k) for j in range(self.y) for i in half]

    def order(self):
        return [
            place for half in self.halves for k in range(self.c) for place in self.places(half, k)
        ]

    def other_rep(self, value):
        if self.reps == 2:
            return lax.ppermute(value, "rep", [(0, 1), (1, 0)])
        return lax.psum(value, "rep")

    def parts_of_both(self, mine, theirs, parts):
        if self.reps == 2:
            return sum_of_reps(mine, theirs, parts)
        return [one.astype(F32) for one in jnp.split(theirs, parts, axis=1)]

    def both_reps(self, mine, theirs):
        if self.reps == 2:
            return mine.astype(F32) + theirs.astype(F32)
        return theirs.astype(F32)


def local(
    tokens,
    segments,
    routes,
    gates,
    gain_attn,
    w_qkv,
    w_out,
    gain_ffn,
    shared_gate,
    shared_up,
    shared_down,
    route_gate,
    route_up,
    route_down,
    cotangent,
):
    grid = Grid()
    seq_len, model_width = tokens.shape
    top_count = routes.shape[1]
    groups = grid.size
    expert_count = groups * route_gate.shape[0]
    capacity = 9 * seq_len * top_count // (8 * expert_count)
    slots = -(-capacity // 16) * 16
    hidden = shared_gate.shape[1] // groups
    width = gain_attn.shape[0]

    chosen = routes[:, :, None] == jnp.arange(expert_count, dtype=jnp.int32)[None, None, :]
    gate_table = jnp.sum(jnp.where(chosen, gates[:, :, None], 0.0), axis=1)
    gate_table = jnp.where(jnp.any(chosen, axis=1), gate_table, -1.0).T
    both_gains = jnp.concatenate([gain_attn, gain_ffn]).astype(F32)
    small = jnp.concatenate(
        [gate_table, jnp.broadcast_to(both_gains, (groups, 2 * width))], axis=1
    )
    small = lax.all_to_all(small, "grp", split_axis=0, concat_axis=0, tiled=True)

    sources = jnp.stack([grid.source(place) for place in grid.order()])
    held_feature = (sources[:, None] * width + jnp.arange(width, dtype=jnp.int32)[None, :]).reshape(-1)
    shuffle = (held_feature[:, None] == jnp.arange(model_width, dtype=jnp.int32)[None, :]).astype(BF)
    count = len(grid.halves)
    near = groups // count

    def chunk(values, n):
        size = values.shape[0] // count
        return values[n * size : (n + 1) * size]

    def to_held(values):
        return contract(values, shuffle, 1, 1).astype(BF)

    def from_held(values):
        high = lax.reduce_precision(values, 8, 7)
        both = jnp.concatenate([high.astype(BF), (values - high).astype(BF)])
        both = jnp.dot(both, shuffle, preferred_element_type=F32)
        return both[: values.shape[0]] + both[values.shape[0] :]

    rounds = Rounds(grid)
    qkv_width, inner = w_qkv.shape[1], w_out.shape[0]
    weights = Gather(grid, rounds, jnp.concatenate([w_qkv, w_out.T], axis=1), False)
    others = Gather(grid, rounds, cotangent, True)
    started = 0
    for r in range(weights.count):
        weights.round(r)
        if r >= grid.z:
            others.round(started)
            started += 1
        rounds.close()
        if r == 0:
            early = rounds.before
    blocks = [weights.held[place] for place in grid.order()]

    small = after(small, *early)
    attn_gain = small[:, seq_len : seq_len + width].reshape(-1)
    ffn_gain = small[:, seq_len + width :].reshape(-1)
    places = jnp.arange(seq_len, dtype=jnp.int32)
    gate_rows = small[:, :seq_len][sources]
    routed_here = gate_rows >= 0.0
    earlier = (places[:, None] < places[None, :]).astype(BF)
    position = jnp.dot(routed_here.astype(BF), earlier, preferred_element_type=F32)
    kept = routed_here & (position < capacity)
    gate_kept = jnp.where(kept, gate_rows, 0.0)
    hit = kept[:, None, :] & (
        position[:, None, :] == jnp.arange(slots, dtype=F32)[None, :, None]
    )
    slot_gate = jnp.sum(jnp.where(hit, gate_rows[:, None, :], 0.0), axis=-1)
    select = hit.astype(BF)
    expert_gate_w, expert_up_w, expert_down_w = route_gate[0], route_up[0], route_down[0]
    inside = expert_gate_w.shape[1]
    both_w = jnp.concatenate([after(expert_gate_w, *early), expert_up_w], axis=1)

    stage = Order()
    rows = after(tokens, *early).astype(F32)
    inverse_one = rms_scale(rows)
    normed_one = rows * inverse_one
    attn_in = (normed_one * attn_gain).astype(BF)
    attn_held, slot_gate, gate_kept, select, both_w = (
        lax.optimization_barrier(
            (to_held(attn_in), slot_gate, gate_kept, select, both_w)
        )
    )
    projected = held_product(attn_held, blocks, 0, qkv_width)
    table = jnp.asarray(rotary_tables(seq_len))

    def next_round(*held_back):
        nonlocal started
        if started < others.count:
            rounds.before += held_back
            others.round(started)
            started += 1
            rounds.close()

    next_round(projected)
    query, key, value, probs, attn_rows = attention_forward(projected, table, segments)
    next_round(attn_rows)
    residual = rows + from_held(held_product_back(attn_rows, blocks, qkv_width))
    inverse_two = rms_scale(residual)
    normed_two = residual * inverse_two
    ffn_in = (normed_two * ffn_gain).astype(BF)
    shared_gate, shared_up, shared_down = (
        after(one, ffn_in) for one in (shared_gate, shared_up, shared_down)
    )
    pieces = jnp.concatenate(
        [
            shared_gate.reshape(width, groups, hidden).transpose(1, 0, 2),
            shared_up.reshape(width, groups, hidden).transpose(1, 0, 2),
            shared_down.reshape(groups, hidden, width).transpose(0, 2, 1),
        ],
        axis=2,
    )
    pieces = lax.all_to_all(pieces, "grp", split_axis=0, concat_axis=0, tiled=True)
    pieces = pieces.reshape(model_width, 3 * hidden)

    stage.done(ffn_in)
    while started < others.count:
        next_round(ffn_in)
    rounds = Rounds(grid)
    ffn = Gather(grid, rounds, ffn_in, True)
    for r in range(ffn.count):
        ffn.round(r)
        rounds.close()

    def picked(selection, stacks):
        size = selection.shape[0] // len(stacks)
        return jnp.concatenate(
            [
                jnp.einsum(
                    "sct,std->scd",
                    selection[n * size : (n + 1) * size],
                    one,
                    preferred_element_type=F32,
                )
                for n, one in enumerate(stacks)
            ]
        )

    def each(stacks, right):
        return jnp.concatenate(
            [
                jnp.dot(one.reshape(-1, one.shape[2]), right, preferred_element_type=F32)
                for one in stacks
            ]
        )

    flat = (near * slots, model_width)

    def forward_part(n):
        selection = stage.enter(chunk(select, n))
        dy = others.halves[n]
        expert_in = picked(selection, ffn.halves[n]).astype(BF).reshape(flat)
        grad_out = picked(selection, dy) * chunk(slot_gate, n)[:, :, None]
        grad_out = grad_out.astype(BF).reshape(flat)
        both = jnp.dot(expert_in, both_w, preferred_element_type=F32)
        expert_hidden = (jax.nn.silu(both[:, :inside]) * both[:, inside:]).astype(BF)
        stage.done(both, expert_hidden, grad_out)
        return {"in": expert_in, "out": grad_out, "hidden": expert_hidden, "both": both}

    def backward_part(n, part):
        grad_out, both = stage.enter(part["out"], part["both"])
        gate_part, up_part = both[:, :inside], both[:, inside:]
        grad_hidden = contract(grad_out, expert_down_w, 1, 1)
        grad_both = jnp.concatenate(
            [
                (grad_hidden * up_part * silu_slope(gate_part)).astype(BF),
                (grad_hidden * jax.nn.silu(gate_part)).astype(BF),
            ],
            axis=1,
        )
        grad_both = after(grad_both)
        grad_in = contract(grad_both, both_w, 1, 1).astype(BF)
        if n == 0:
            held_pieces = after(pieces, grad_both)
            shared.extend([held_pieces[:, : 2 * hidden], held_pieces[:, 2 * hidden :]])
        shared_in, shared_back = shared
        shared_pre = each(ffn.halves[n], shared_in)
        gate_pre, up_pre = shared_pre[:, :hidden], shared_pre[:, hidden:]
        shared_silu = jax.nn.silu(gate_pre)
        grad_shared_hidden = each(others.halves[n], shared_back)
        grad_shared_pre = jnp.concatenate(
            [
                (grad_shared_hidden * up_pre * silu_slope(gate_pre)).astype(BF),
                (grad_shared_hidden * shared_silu).astype(BF),
            ],
            axis=1,
        )
        part["grad_both"] = grad_both
        part["shared"] = (shared_silu * up_pre).astype(BF)
        part["shared_pre"] = grad_shared_pre
        stage.done(grad_in, grad_shared_pre)
        return to_tokens(n, grad_in, None, grad_shared_pre, shared_in)

    def to_tokens(n, slot_rows, scale, shared_rows, shared_weight):
        slot_rows = slot_rows.reshape(near, slots, model_width)

        def make(first, size):
            mine = slice(first, first + size)
            selection = stage.enter(chunk(select, n)[mine])
            back = jnp.einsum(
                "sct,scd->std", selection, slot_rows[mine], preferred_element_type=F32
            )
            if scale is not None:
                back = back * scale[mine][:, :, None]
            shared_mine = shared_rows[first * seq_len : (first + size) * seq_len]
            return back + contract(shared_mine, shared_weight, 1, 1).reshape(back.shape)

        return Scatter(grid, stage, grid.halves[n], make)

    swap = grid.other_rep
    parts, backs, shared = [], [], []
    for n in range(count):
        parts.append(forward_part(n))
        if n:
            backs[n - 1].along_y()
        backs.append(backward_part(n, parts[n]))
        backs[n].core()

    def joined(key):
        return jnp.concatenate([part[key] for part in parts])

    class AlongZ:
        def __init__(self, halves):
            self.halves = halves

        def far(self):
            if grid.z == 4:
                far = self.halves[-1].own()
                self.whole = far
                self.passed_on = grid.shift(far[-2], 3, 0, 0)
                self.back_one = grid.shift(far[-1], 1, 0, 0)

        def near(self):
            if grid.z != 4:
                self.mine = self.halves[0].own()[0]
                return
            if len(self.halves) == 1:
                near = stage.enter(self.whole[1]).astype(F32) + self.passed_on.astype(F32)
                self.mine = self.whole[0].astype(F32) + self.back_one.astype(F32)
                self.back_one = None
                stage.done(self.mine)
                near = stage.enter(near)
            else:
                half = self.halves[0]
                total = half.term(0)
                near = after(stage.enter(total[1]) + self.passed_on.astype(F32))
                stage.done(near)
                self.mine = total[0]
                if grid.y > 1:
                    near = near + half.total[1].astype(F32)
                    self.mine = total[0] + half.total[0].astype(F32)
            near = near.astype(BF)
            stage.done(near)
            self.near_one = grid.shift(near, 3, 0, 0)

        def total(self):
            mine = stage.enter(self.mine).astype(F32)
            if grid.z == 4:
                if self.back_one is not None:
                    mine = mine + self.back_one.astype(F32)
                mine = mine + self.near_one.astype(F32)
            return mine

    down_left, down_right = stage.enter(joined("hidden"), joined("out"))
    down_mine = contract(down_left, down_right, 0, 0).astype(BF)
    stage.done(down_mine)
    down_theirs = swap(down_mine)
    backs[-1].along_y()
    both_left, both_right = stage.enter(joined("in"), joined("grad_both"))
    both_mine = contract(both_left, both_right, 0, 0).astype(BF)
    stage.done(both_mine)
    ffn_sum = AlongZ(backs)
    ffn_sum.far()

    outs = []
    for n in range(count):
        hidden_rows = stage.enter(parts[n]["hidden"])
        expert_out = jnp.dot(hidden_rows, expert_down_w, preferred_element_type=F32).astype(BF)
        stage.done(expert_out)
        outs.append(
            to_tokens(n, expert_out, chunk(gate_kept, n), parts[n]["shared"], shared[1])
        )
    for out in outs[::-1]:
        out.core()
    ffn_sum.near()
    for out in outs[::-1]:
        out.along_y()
    grad_ffn_in = ffn_sum.total()

    grad_norm_two, grad_ffn_gain = norm_backward(grad_ffn_in, normed_two, inverse_two, ffn_gain)
    grad_residual = cotangent.astype(F32) + grad_norm_two
    grad_attn_low = grad_residual.astype(BF)
    low_turned = contract(shuffle, grad_attn_low, 1, 1).astype(BF)
    grad_heads = held_product(low_turned.T, blocks, qkv_width, inner).astype(BF)
    stage.done(grad_heads)

    def products(half, turned, right):
        def make(first, size):
            rows = turned[first * width : (first + size) * width]
            product = jnp.dot(stage.enter(rows), right, preferred_element_type=F32)
            return product.reshape(size, width, right.shape[1])

        return Scatter(grid, stage, half, make)

    everywhere = sum(grid.halves, ())
    merged = low_turned.reshape(count, grid.c, grid.y, len(everywhere) // count, width, seq_len)
    merged = merged.transpose(1, 2, 0, 3, 4, 5).reshape(model_width, seq_len)
    tall = products(everywhere, merged, attn_rows)
    out_sum, tall_sum = AlongZ(outs), AlongZ([tall])
    tall.core()
    both_theirs = swap(after(both_mine, down_theirs))
    grads = attention_backward(stage.enter(grad_heads), query, key, value, probs, table)
    grad_projected = jnp.concatenate(grads, axis=1)
    stage.done(grad_projected)
    turned_in = contract(shuffle, attn_in, 1, 1).astype(BF)
    wides = [products(half, chunk(turned_in, n), grad_projected) for n, half in enumerate(grid.halves)]
    wide_sum = AlongZ(wides)
    out_sum.far()
    tall.along_y()
    for wide in wides[::-1]:
        wide.core()
    out_sum.near()
    for wide in wides[::-1]:
        wide.along_y()
    grad_attn_held = held_product_back(stage.enter(grad_projected), blocks, 0)
    stage.done(grad_attn_held)
    tall_sum.far()
    grad_tokens, grad_attn_gain = token_grad(
        stage.enter(grad_attn_held), shuffle, normed_one, inverse_one, attn_gain, grad_residual
    )
    stage.done(grad_tokens)
    mixed = (residual + out_sum.total()).astype(BF)
    stage.done(mixed)
    tall_sum.near()
    (grad_route_down,) = grid.parts_of_both(stage.enter(down_mine), down_theirs, 1)
    stage.done(grad_route_down)
    wide_sum.far()
    shared_left, shared_right = stage.enter(joined("shared_pre"), joined("shared"))

    def rows_of(stacks):
        return jnp.concatenate([one.reshape(-1, model_width) for half in stacks.values() for one in half])

    grad_pieces = jnp.concatenate(
        [
            contract(shared_left, rows_of(ffn.halves), 0, 0),
            contract(shared_right, rows_of(others.halves), 0, 0),
            grad_attn_gain,
            grad_ffn_gain[None],
        ]
    )
    grad_pieces = grad_pieces.astype(BF)
    stage.done(grad_pieces)
    grad_pieces_there = swap(grad_pieces)
    grad_route_gate, grad_route_up = grid.parts_of_both(stage.enter(both_mine), both_theirs, 2)
    stage.done(grad_route_gate, grad_route_up)
    grad_pieces = grid.both_reps(stage.enter(grad_pieces), grad_pieces_there).astype(BF)
    grad_pieces = grad_pieces.T.reshape(groups, width, 3 * hidden + 2)
    stage.done(grad_pieces)
    grad_pieces = lax.all_to_all(grad_pieces, "grp", split_axis=0, concat_axis=0, tiled=True)
    wide_sum.near()
    grad_w_out = tall_sum.total().astype(BF)
    stage.done(grad_w_out)
    grad_w_out_there = swap(grad_w_out)
    grad_w_qkv = wide_sum.total().astype(BF)
    stage.done(grad_w_qkv)
    grad_w_qkv_there = swap(grad_w_qkv)
    grad_route_down, grad_route_gate, grad_route_up = (
        one[None] for one in (grad_route_down, grad_route_gate, grad_route_up)
    )

    grad_w_out = grid.both_reps(grad_w_out, grad_w_out_there).T
    grad_pieces = stage.enter(grad_pieces).astype(F32)
    grad_w_qkv = grid.both_reps(grad_w_qkv, grad_w_qkv_there)
    gain_grads = grad_pieces[:, :, 3 * hidden :].sum(axis=0)

    def join(part):
        return part.transpose(1, 0, 2).reshape(width, groups * hidden)

    grad_shared_gate = join(grad_pieces[:, :, :hidden])
    grad_shared_up = join(grad_pieces[:, :, hidden : 2 * hidden])
    grad_shared_down = join(grad_pieces[:, :, 2 * hidden : 3 * hidden]).T

    return (
        mixed,
        grad_tokens,
        gain_grads[:, 0],
        grad_w_qkv,
        grad_w_out,
        gain_grads[:, 1],
        grad_shared_gate,
        grad_shared_up,
        grad_shared_down,
        grad_route_gate,
        grad_route_up,
        grad_route_down,
    )


def solution(mesh):
    in_specs = (
        P(("rep", "grp"), None),
        P(("rep", "grp"), None),
        P(("rep", "grp"), None),
        P(("rep", "grp"), None),
        P("grp"),
        P("grp", None),
        P(None, "grp"),
        P("grp"),
        P("grp", None),
        P("grp", None),
        P(None, "grp"),
        P("grp", None, None),
        P("grp", None, None),
        P("grp", None, None),
        P(("rep", "grp"), None),
    )
    out_specs = (
        P(("rep", "grp"), None),
        P(("rep", "grp"), None),
        P("grp"),
        P("grp", None),
        P(None, "grp"),
        P("grp"),
        P("grp", None),
        P("grp", None),
        P(None, "grp"),
        P("grp", None, None),
        P("grp", None, None),
        P("grp", None, None),
    )
    return jax.shard_map(local, mesh=mesh, in_specs=in_specs, out_specs=out_specs, check_vma=False)
```

```python
import math

import jax
import jax.numpy as jnp
import numpy as np
from jax import lax
from jax.experimental import pallas as pl
from jax.experimental.pallas import tpu as pltpu
from jax.sharding import PartitionSpec as P

H = 10
HD = 128
HEADS_AT_ONCE = 5

EPSILON = 1e-06
MASKED_SCORE = -1000000000.0
BF = jnp.bfloat16
F32 = jnp.float32
BRIEF = pl.CostEstimate(flops=1, bytes_accessed=1, transcendentals=0)


def rms_scale(values):
    return lax.rsqrt(jnp.mean(values * values, axis=-1, keepdims=True) + EPSILON)


def rotary_tables(seq_len):
    half = HD // 2
    frequency = np.power(np.float32(10000.0), -2.0 * np.arange(half, dtype=np.float32) / HD)
    angle = np.arange(seq_len, dtype=np.float32)[:, None] * frequency.astype(np.float32)[None, :]
    cosine, sine = np.cos(angle), np.sin(angle)
    return np.stack(
        [np.concatenate([cosine, cosine], axis=1), np.concatenate([-sine, sine], axis=1)]
    ).astype(np.float32)


def contract(left, right, left_dim, right_dim):
    return lax.dot_general(
        left, right, (((left_dim,), (right_dim,)), ((), ())), preferred_element_type=F32
    )


def silu_slope(values):
    sigma = jax.nn.sigmoid(values)
    return sigma * (1.0 + values * (1.0 - sigma))


def norm_backward(grad_scaled, normed, inverse, gain):
    grad_normed = grad_scaled * gain
    grad_gain = jnp.sum(grad_scaled * normed, axis=0)
    grad_rows = inverse * (
        grad_normed - normed * jnp.mean(grad_normed * normed, axis=-1, keepdims=True)
    )
    return (grad_rows, grad_gain)


def after(value, *others):
    return lax.optimization_barrier((value,) + others)[0]


def attention_forward_kernel(q_in, k_in, v_in, table, doc_col, doc_row, q_ref, k_ref, v_ref, p_ref, o_ref):
    def turned(values):
        return (values * table[0] + pltpu.roll(values, HD // 2, 1) * table[1]).astype(BF)

    for n in range(HEADS_AT_ONCE):
        at = slice(n * HD, (n + 1) * HD)
        query, key, value = turned(q_in[:, at]), turned(k_in[:, at]), v_in[:, at].astype(BF)
        q_ref[:, at], k_ref[:, at], v_ref[:, at] = query, key, value
        scores = contract(query, key, 1, 1) / math.sqrt(HD)
        row = lax.broadcasted_iota(jnp.int32, scores.shape, 0)
        column = lax.broadcasted_iota(jnp.int32, scores.shape, 1)
        allowed = (row >= column) & (doc_col[...] == doc_row[...])
        scores = jnp.where(allowed, scores, MASKED_SCORE)
        raised = jnp.exp(scores - jnp.max(scores, axis=-1, keepdims=True))
        probs = raised / jnp.sum(raised, axis=-1, keepdims=True)
        p_ref[n] = probs
        o_ref[:, at] = contract(probs.astype(BF), value, 1, 0).astype(BF)


def attention_backward_kernel(g_ref, q_ref, k_ref, v_ref, p_ref, table, out_ref):
    def turned_back(values):
        return (values * table[0] - pltpu.roll(values, HD // 2, 1) * table[1]).astype(BF)

    def place(part, n):
        return slice((part * H + n) * HD, (part * H + n + 1) * HD)

    for n in range(H):
        at = place(0, n)
        grad, probs = g_ref[:, at], p_ref[n]
        grad_probs = contract(grad, v_ref[:, at], 1, 1)
        out_ref[:, place(2, n)] = contract(probs.astype(BF), grad, 0, 0).astype(BF)
        mean = jnp.sum(grad_probs * probs, axis=-1, keepdims=True)
        grad_scores = (probs * (grad_probs - mean)).astype(BF)
        out_ref[:, at] = turned_back(contract(grad_scores, k_ref[:, at], 1, 0) / math.sqrt(HD))
        out_ref[:, place(1, n)] = turned_back(contract(grad_scores, q_ref[:, at], 0, 0) / math.sqrt(HD))


def head_block(seq_len, offset=0):
    return pl.BlockSpec((seq_len, HEADS_AT_ONCE * HD), lambda h: (0, offset // HEADS_AT_ONCE + h))


def attention_forward(projected, table, documents):
    seq_len = projected.shape[0]
    row = jax.ShapeDtypeStruct((seq_len, H * HD), BF)
    probs_block = pl.BlockSpec((HEADS_AT_ONCE, seq_len, seq_len), lambda h: (h, 0, 0))
    return pl.pallas_call(
        attention_forward_kernel,
        grid=(H // HEADS_AT_ONCE,),
        in_specs=[
            head_block(seq_len),
            head_block(seq_len, H),
            head_block(seq_len, 2 * H),
            pl.BlockSpec((2, seq_len, HD), lambda h: (0, 0, 0)),
            pl.BlockSpec((seq_len, 1), lambda h: (0, 0)),
            pl.BlockSpec((1, seq_len), lambda h: (0, 0)),
        ],
        out_specs=[head_block(seq_len)] * 3 + [probs_block, head_block(seq_len)],
        out_shape=[row] * 3 + [jax.ShapeDtypeStruct((H, seq_len, seq_len), F32), row],
        cost_estimate=BRIEF,
        name="attention_forward",
    )(projected, projected, projected, table, documents.reshape(seq_len, 1), documents.reshape(1, seq_len))


def attention_backward(grad_heads, query, key, value, probs, table):
    seq_len = grad_heads.shape[0]
    return pl.pallas_call(
        attention_backward_kernel,
        out_shape=jax.ShapeDtypeStruct((seq_len, 3 * H * HD), BF),
        cost_estimate=BRIEF,
        name="attention_backward",
    )(grad_heads, query, key, value, probs, table)


def tile_of(first, columns):
    most = max(columns // 3, 640)
    return max(n for n in range(128, most + 1, 128) if columns % n == 0 and first % n == 0)


def held_product(left, blocks, first, columns, kind=F32):
    rows, depth = left.shape
    tile = tile_of(first, columns)

    def kernel(left_ref, *refs):
        whole = jnp.concatenate([one[...] for one in refs[:-1]], axis=0)
        refs[-1][...] = contract(left_ref[...], whole, 1, 0).astype(kind)

    return pl.pallas_call(
        kernel,
        grid=(columns // tile,),
        in_specs=[pl.BlockSpec((rows, depth), lambda n: (0, 0))]
        + [pl.BlockSpec((one.shape[0], tile), lambda n: (0, first // tile + n)) for one in blocks],
        out_specs=pl.BlockSpec((rows, tile), lambda n: (0, n)),
        out_shape=jax.ShapeDtypeStruct((rows, columns), kind),
        cost_estimate=BRIEF,
        name="held_product",
    )(left, *blocks)


def held_product_back(left, blocks, first):
    rows, columns = left.shape
    depth = sum(one.shape[0] for one in blocks)
    tile = tile_of(first, columns)

    def kernel(left_ref, *refs):
        whole = jnp.concatenate([one[...] for one in refs[:-1]], axis=0)
        product = contract(left_ref[...], whole, 1, 1)

        @pl.when(pl.program_id(0) == 0)
        def _():
            refs[-1][...] = product

        @pl.when(pl.program_id(0) > 0)
        def _():
            refs[-1][...] += product

    return pl.pallas_call(
        kernel,
        grid=(columns // tile,),
        in_specs=[pl.BlockSpec((rows, tile), lambda n: (0, n))]
        + [pl.BlockSpec((one.shape[0], tile), lambda n: (0, first // tile + n)) for one in blocks],
        out_specs=pl.BlockSpec((rows, depth), lambda n: (0, 0)),
        out_shape=jax.ShapeDtypeStruct((rows, depth), F32),
        cost_estimate=BRIEF,
        name="held_product_back",
    )(left, *blocks)


def token_grad(grad_held, shuffle, normed, inverse, gain, grad_rows):
    rows, width = normed.shape

    def kernel(held_ref, shuffle_ref, normed_ref, inverse_ref, gain_ref, rows_ref, out_ref, gain_grad_ref):
        held, unit = held_ref[...], normed_ref[...]
        high = held.astype(BF)
        low = (held - high.astype(F32)).astype(BF)
        grad = contract(high, shuffle_ref[...], 1, 0) + contract(low, shuffle_ref[...], 1, 0)
        gain_grad_ref[...] = jnp.sum(grad * unit, axis=0, keepdims=True)
        grad = grad * gain_ref[...]
        mean = jnp.sum(grad * unit, axis=-1, keepdims=True) / width
        out_ref[...] = (rows_ref[...] + inverse_ref[...] * (grad - unit * mean)).astype(BF)

    return pl.pallas_call(
        kernel,
        out_shape=[
            jax.ShapeDtypeStruct((rows, width), BF),
            jax.ShapeDtypeStruct((1, width), F32),
        ],
        cost_estimate=BRIEF,
        name="token_grad",
    )(grad_held, shuffle, normed, inverse, gain.reshape(1, width), grad_rows)


def sum_of_reps(mine, theirs, parts):
    rows, width = mine.shape
    size = width // parts
    tile = max(n for n in range(16, 257, 16) if rows % n == 0)

    def kernel(mine_ref, theirs_ref, *out_refs):
        for n, out_ref in enumerate(out_refs):
            at = slice(n * size, (n + 1) * size)
            out_ref[...] = mine_ref[:, at].astype(F32) + theirs_ref[:, at].astype(F32)

    return pl.pallas_call(
        kernel,
        grid=(rows // tile,),
        in_specs=[pl.BlockSpec((tile, width), lambda n: (n, 0))] * 2,
        out_specs=[pl.BlockSpec((tile, size), lambda n: (n, 0))] * parts,
        out_shape=[jax.ShapeDtypeStruct((rows, size), F32)] * parts,
        cost_estimate=BRIEF,
        name="sum_of_reps",
    )(mine, theirs)


class Order:
    def __init__(self):
        self.last = ()

    def enter(self, *values):
        held = lax.optimization_barrier(values + self.last)[: len(values)]
        return held[0] if len(values) == 1 else held

    def done(self, *values):
        self.last = values


class Rounds:
    def __init__(self, grid):
        self.grid = grid
        self.before = ()
        self.now = []

    def send(self, value, *move):
        arrived = self.grid.shift(after(value, *self.before), *move)
        self.now.append(arrived)
        return arrived

    def close(self):
        self.before, self.now = tuple(self.now), []


class Gather:
    def __init__(self, grid, rounds, block, merged):
        self.grid, self.rounds, self.merged = grid, rounds, merged
        self.held = {(0, 0, 0): block}
        self.halves = {}
        self.count = grid.z + grid.y + (1 if merged else 0) - 1 if grid.size > 1 else 0

    def round(self, r):
        grid, held = self.grid, self.held
        if r < grid.z - 1:
            held[(r + 1, 0, 0)] = self.rounds.send(held[(r, 0, 0)], 1, 0, 0)
        for j in range(grid.y - 1):
            if 0 <= r - j < grid.z:
                held[(r - j, j + 1, 0)] = self.rounds.send(held[(r - j, j, 0)], 0, 1, 0)
        if not self.merged:
            for j in range(grid.y):
                if 0 <= r - j < grid.z:
                    for k in range(1, grid.c):
                        held[(r - j, j, k)] = self.rounds.send(held[(r - j, j, k - 1)], 0, 0, 1)
            return
        for n, half in enumerate(grid.halves):
            if r == half[-1] + grid.y:
                stacks = [jnp.stack([held[place] for place in grid.places(half, 0)])]
                for _ in range(1, grid.c):
                    stacks.append(self.rounds.send(stacks[-1], 0, 0, 1))
                self.halves[n] = stacks


class Scatter:
    def __init__(self, grid, stage, half, make):
        self.grid, self.stage, self.make = grid, stage, make
        self.rows = len(half)

    def core(self):
        grid = self.grid
        if grid.c == 1:
            return
        total = self.make(grid.y * self.rows, grid.y * self.rows).astype(BF)
        self.stage.done(total)
        self.arrived = grid.shift(total, 0, 0, 1)

    def term(self, j):
        here = self.make(j * self.rows, self.rows)
        if self.grid.c > 1:
            here = here + self.arrived[j * self.rows : (j + 1) * self.rows].astype(F32)
        return here

    def along_y(self):
        grid = self.grid
        if grid.y == 1:
            return
        total = self.term(1).astype(BF)
        self.stage.done(total)
        self.total = grid.shift(total, 0, 1, 0)
        for j in range(2, grid.y):
            total = (self.term(j) + self.total.astype(F32)).astype(BF)
            self.stage.done(total)
            self.total = grid.shift(total, 0, 1, 0)

    def own(self):
        total = self.term(0)
        if self.grid.y > 1:
            total = total + self.total.astype(F32)
        total = total.astype(BF)
        self.stage.done(total)
        return total


class Grid:
    def __init__(self):
        self.size = lax.axis_size("grp")
        self.reps = lax.axis_size("rep")
        self.c = 2 if self.size % 2 == 0 else 1
        self.z = 4 if self.size % (4 * self.c) == 0 else 1
        self.y = self.size // (self.c * self.z)
        me = lax.axis_index("grp")
        self.my_c = me % self.c
        self.my_y = me // self.c % self.y
        self.my_z = me // (self.c * self.y)
        self.halves = ((0, 1), (2, 3)) if self.z == 4 else ((0,),)

    def flat(self, z, y, c):
        return (z % self.z * self.y + y % self.y) * self.c + c % self.c

    def shift(self, value, dz, dy, dc):
        pairs = [
            (self.flat(z, y, c), self.flat(z + dz, y + dy, c + dc))
            for z in range(self.z)
            for y in range(self.y)
            for c in range(self.c)
        ]
        return lax.ppermute(value, "grp", pairs)

    def source(self, step):
        return self.flat(
            self.my_z - step[0] + self.z, self.my_y - step[1] + self.y, self.my_c - step[2] + self.c
        )

    def places(self, half, k):
        return [(i, j, k) for j in range(self.y) for i in half]

    def order(self):
        return [
            place for half in self.halves for k in range(self.c) for place in self.places(half, k)
        ]

    def other_rep(self, value):
        if self.reps == 2:
            return lax.ppermute(value, "rep", [(0, 1), (1, 0)])
        return lax.psum(value, "rep")

    def parts_of_both(self, mine, theirs, parts):
        if self.reps == 2:
            return sum_of_reps(mine, theirs, parts)
        return [one.astype(F32) for one in jnp.split(theirs, parts, axis=1)]

    def both_reps(self, mine, theirs):
        if self.reps == 2:
            return mine.astype(F32) + theirs.astype(F32)
        return theirs.astype(F32)


def local(
    tokens,
    segments,
    routes,
    gates,
    gain_attn,
    w_qkv,
    w_out,
    gain_ffn,
    shared_gate,
    shared_up,
    shared_down,
    route_gate,
    route_up,
    route_down,
    cotangent,
):
    grid = Grid()
    seq_len, model_width = tokens.shape
    top_count = routes.shape[1]
    groups = grid.size
    expert_count = groups * route_gate.shape[0]
    capacity = 9 * seq_len * top_count // (8 * expert_count)
    slots = -(-capacity // 16) * 16
    hidden = shared_gate.shape[1] // groups
    width = gain_attn.shape[0]

    chosen = routes[:, :, None] == jnp.arange(expert_count, dtype=jnp.int32)[None, None, :]
    gate_table = jnp.sum(jnp.where(chosen, gates[:, :, None], 0.0), axis=1)
    gate_table = jnp.where(jnp.any(chosen, axis=1), gate_table, -1.0).T
    both_gains = jnp.concatenate([gain_attn, gain_ffn]).astype(F32)
    small = jnp.concatenate(
        [gate_table, jnp.broadcast_to(both_gains, (groups, 2 * width))], axis=1
    )
    small = lax.all_to_all(small, "grp", split_axis=0, concat_axis=0, tiled=True)

    sources = jnp.stack([grid.source(place) for place in grid.order()])
    held_feature = (sources[:, None] * width + jnp.arange(width, dtype=jnp.int32)[None, :]).reshape(-1)
    shuffle = (held_feature[:, None] == jnp.arange(model_width, dtype=jnp.int32)[None, :]).astype(BF)
    count = len(grid.halves)
    near = groups // count

    def chunk(values, n):
        size = values.shape[0] // count
        return values[n * size : (n + 1) * size]

    def to_held(values):
        return contract(values, shuffle, 1, 1).astype(BF)

    def from_held(values):
        high = lax.reduce_precision(values, 8, 7)
        both = jnp.concatenate([high.astype(BF), (values - high).astype(BF)])
        both = jnp.dot(both, shuffle, preferred_element_type=F32)
        return both[: values.shape[0]] + both[values.shape[0] :]

    rounds = Rounds(grid)
    qkv_width, inner = w_qkv.shape[1], w_out.shape[0]
    weights = Gather(grid, rounds, jnp.concatenate([w_qkv, w_out.T], axis=1), False)
    others = Gather(grid, rounds, cotangent, True)
    started = 0
    for r in range(weights.count):
        weights.round(r)
        if r >= grid.z:
            others.round(started)
            started += 1
        rounds.close()
        if r == 0:
            early = rounds.before
    blocks = [weights.held[place] for place in grid.order()]

    small = after(small, *early)
    attn_gain = small[:, seq_len : seq_len + width].reshape(-1)
    ffn_gain = small[:, seq_len + width :].reshape(-1)
    places = jnp.arange(seq_len, dtype=jnp.int32)
    gate_rows = small[:, :seq_len][sources]
    routed_here = gate_rows >= 0.0
    earlier = (places[:, None] < places[None, :]).astype(BF)
    position = jnp.dot(routed_here.astype(BF), earlier, preferred_element_type=F32)
    kept = routed_here & (position < capacity)
    gate_kept = jnp.where(kept, gate_rows, 0.0)
    hit = kept[:, None, :] & (
        position[:, None, :] == jnp.arange(slots, dtype=F32)[None, :, None]
    )
    slot_gate = jnp.sum(jnp.where(hit, gate_rows[:, None, :], 0.0), axis=-1)
    select = hit.astype(BF)
    expert_gate_w, expert_up_w, expert_down_w = route_gate[0], route_up[0], route_down[0]
    inside = expert_gate_w.shape[1]
    both_w = jnp.concatenate([after(expert_gate_w, *early), expert_up_w], axis=1)

    stage = Order()
    rows = after(tokens, *early).astype(F32)
    inverse_one = rms_scale(rows)
    normed_one = rows * inverse_one
    attn_in = (normed_one * attn_gain).astype(BF)
    attn_held, slot_gate, gate_kept, select, both_w = (
        lax.optimization_barrier(
            (to_held(attn_in), slot_gate, gate_kept, select, both_w)
        )
    )
    projected = held_product(attn_held, blocks, 0, qkv_width)
    table = jnp.asarray(rotary_tables(seq_len))

    def next_round(*held_back):
        nonlocal started
        if started < others.count:
            rounds.before += held_back
            others.round(started)
            started += 1
            rounds.close()

    next_round(projected)
    query, key, value, probs, attn_rows = attention_forward(projected, table, segments)
    next_round(attn_rows)
    residual = rows + from_held(held_product_back(attn_rows, blocks, qkv_width))
    inverse_two = rms_scale(residual)
    normed_two = residual * inverse_two
    ffn_in = (normed_two * ffn_gain).astype(BF)
    shared_gate, shared_up, shared_down = (
        after(one, ffn_in) for one in (shared_gate, shared_up, shared_down)
    )
    pieces = jnp.concatenate(
        [
            shared_gate.reshape(width, groups, hidden).transpose(1, 0, 2),
            shared_up.reshape(width, groups, hidden).transpose(1, 0, 2),
            shared_down.reshape(groups, hidden, width).transpose(0, 2, 1),
        ],
        axis=2,
    )
    pieces = lax.all_to_all(pieces, "grp", split_axis=0, concat_axis=0, tiled=True)
    pieces = pieces.reshape(model_width, 3 * hidden)

    stage.done(ffn_in)
    while started < others.count:
        next_round(ffn_in)
    rounds = Rounds(grid)
    ffn = Gather(grid, rounds, ffn_in, True)
    for r in range(ffn.count):
        ffn.round(r)
        rounds.close()

    def picked(selection, stacks):
        size = selection.shape[0] // len(stacks)
        return jnp.concatenate(
            [
                jnp.einsum(
                    "sct,std->scd",
                    selection[n * size : (n + 1) * size],
                    one,
                    preferred_element_type=F32,
                )
                for n, one in enumerate(stacks)
            ]
        )

    def each(stacks, right):
        return jnp.concatenate(
            [
                jnp.dot(one.reshape(-1, one.shape[2]), right, preferred_element_type=F32)
                for one in stacks
            ]
        )

    flat = (near * slots, model_width)

    def forward_part(n):
        selection = stage.enter(chunk(select, n))
        dy = others.halves[n]
        expert_in = picked(selection, ffn.halves[n]).astype(BF).reshape(flat)
        grad_out = picked(selection, dy) * chunk(slot_gate, n)[:, :, None]
        grad_out = grad_out.astype(BF).reshape(flat)
        both = jnp.dot(expert_in, both_w, preferred_element_type=F32)
        expert_hidden = (jax.nn.silu(both[:, :inside]) * both[:, inside:]).astype(BF)
        stage.done(both, expert_hidden, grad_out)
        return {"in": expert_in, "out": grad_out, "hidden": expert_hidden, "both": both}

    def backward_part(n, part):
        grad_out, both = stage.enter(part["out"], part["both"])
        gate_part, up_part = both[:, :inside], both[:, inside:]
        grad_hidden = contract(grad_out, expert_down_w, 1, 1)
        grad_both = jnp.concatenate(
            [
                (grad_hidden * up_part * silu_slope(gate_part)).astype(BF),
                (grad_hidden * jax.nn.silu(gate_part)).astype(BF),
            ],
            axis=1,
        )
        grad_both = after(grad_both)
        grad_in = contract(grad_both, both_w, 1, 1).astype(BF)
        if n == 0:
            held_pieces = after(pieces, grad_both)
            shared.extend([held_pieces[:, : 2 * hidden], held_pieces[:, 2 * hidden :]])
        shared_in, shared_back = shared
        shared_pre = each(ffn.halves[n], shared_in)
        gate_pre, up_pre = shared_pre[:, :hidden], shared_pre[:, hidden:]
        shared_silu = jax.nn.silu(gate_pre)
        grad_shared_hidden = each(others.halves[n], shared_back)
        grad_shared_pre = jnp.concatenate(
            [
                (grad_shared_hidden * up_pre * silu_slope(gate_pre)).astype(BF),
                (grad_shared_hidden * shared_silu).astype(BF),
            ],
            axis=1,
        )
        part["grad_both"] = grad_both
        part["shared"] = (shared_silu * up_pre).astype(BF)
        part["shared_pre"] = grad_shared_pre
        stage.done(grad_in, grad_shared_pre)
        return to_tokens(n, grad_in, None, grad_shared_pre, shared_in)

    def to_tokens(n, slot_rows, scale, shared_rows, shared_weight):
        slot_rows = slot_rows.reshape(near, slots, model_width)

        def make(first, size):
            mine = slice(first, first + size)
            selection = stage.enter(chunk(select, n)[mine])
            back = jnp.einsum(
                "sct,scd->std", selection, slot_rows[mine], preferred_element_type=F32
            )
            if scale is not None:
                back = back * scale[mine][:, :, None]
            shared_mine = shared_rows[first * seq_len : (first + size) * seq_len]
            return back + contract(shared_mine, shared_weight, 1, 1).reshape(back.shape)

        return Scatter(grid, stage, grid.halves[n], make)

    swap = grid.other_rep
    parts, backs, shared = [], [], []
    for n in range(count):
        parts.append(forward_part(n))
        if n:
            backs[n - 1].along_y()
        backs.append(backward_part(n, parts[n]))
        backs[n].core()

    def joined(key):
        return jnp.concatenate([part[key] for part in parts])

    class AlongZ:
        def __init__(self, halves):
            self.halves = halves

        def far(self):
            if grid.z == 4:
                far = self.halves[-1].own()
                self.whole = far
                self.passed_on = grid.shift(far[-2], 3, 0, 0)
                self.back_one = grid.shift(far[-1], 1, 0, 0)

        def near(self):
            if grid.z != 4:
                self.mine = self.halves[0].own()[0]
                return
            if len(self.halves) == 1:
                near = stage.enter(self.whole[1]).astype(F32) + self.passed_on.astype(F32)
                self.mine = self.whole[0].astype(F32) + self.back_one.astype(F32)
                self.back_one = None
                stage.done(self.mine)
                near = stage.enter(near)
            else:
                half = self.halves[0]
                total = half.term(0)
                near = after(stage.enter(total[1]) + self.passed_on.astype(F32))
                stage.done(near)
                self.mine = total[0]
                if grid.y > 1:
                    near = near + half.total[1].astype(F32)
                    self.mine = total[0] + half.total[0].astype(F32)
            near = near.astype(BF)
            stage.done(near)
            self.near_one = grid.shift(near, 3, 0, 0)

        def total(self):
            mine = stage.enter(self.mine).astype(F32)
            if grid.z == 4:
                if self.back_one is not None:
                    mine = mine + self.back_one.astype(F32)
                mine = mine + self.near_one.astype(F32)
            return mine

    down_left, down_right = stage.enter(joined("hidden"), joined("out"))
    down_mine = contract(down_left, down_right, 0, 0).astype(BF)
    stage.done(down_mine)
    down_theirs = swap(down_mine)
    backs[-1].along_y()
    both_left, both_right = stage.enter(joined("in"), joined("grad_both"))
    both_mine = contract(both_left, both_right, 0, 0).astype(BF)
    stage.done(both_mine)
    ffn_sum = AlongZ(backs)
    ffn_sum.far()

    outs = []
    for n in range(count):
        hidden_rows = stage.enter(parts[n]["hidden"])
        expert_out = jnp.dot(hidden_rows, expert_down_w, preferred_element_type=F32).astype(BF)
        stage.done(expert_out)
        outs.append(
            to_tokens(n, expert_out, chunk(gate_kept, n), parts[n]["shared"], shared[1])
        )
    for out in outs[::-1]:
        out.core()
    ffn_sum.near()
    for out in outs[::-1]:
        out.along_y()
    grad_ffn_in = ffn_sum.total()

    grad_norm_two, grad_ffn_gain = norm_backward(grad_ffn_in, normed_two, inverse_two, ffn_gain)
    grad_residual = cotangent.astype(F32) + grad_norm_two
    grad_attn_low = grad_residual.astype(BF)
    low_turned = contract(shuffle, grad_attn_low, 1, 1).astype(BF)
    grad_heads = held_product(low_turned.T, blocks, qkv_width, inner, BF)
    stage.done(grad_heads)

    def products(half, turned, right):
        def make(first, size):
            rows = turned[first * width : (first + size) * width]
            product = jnp.dot(stage.enter(rows), right, preferred_element_type=F32)
            return product.reshape(size, width, right.shape[1])

        return Scatter(grid, stage, half, make)

    everywhere = sum(grid.halves, ())
    merged = low_turned.reshape(count, grid.c, grid.y, len(everywhere) // count, width, seq_len)
    merged = merged.transpose(1, 2, 0, 3, 4, 5).reshape(model_width, seq_len)
    tall = products(everywhere, merged, attn_rows)
    out_sum, tall_sum = AlongZ(outs), AlongZ([tall])
    tall.core()
    both_theirs = swap(after(both_mine, down_theirs))
    grad_projected = attention_backward(stage.enter(grad_heads), query, key, value, probs, table)
    stage.done(grad_projected)
    turned_in = contract(shuffle, attn_in, 1, 1).astype(BF)
    wides = [products(half, chunk(turned_in, n), grad_projected) for n, half in enumerate(grid.halves)]
    wide_sum = AlongZ(wides)
    out_sum.far()
    tall.along_y()
    for wide in wides[::-1]:
        wide.core()
    out_sum.near()
    for wide in wides[::-1]:
        wide.along_y()
    grad_attn_held = held_product_back(stage.enter(grad_projected), blocks, 0)
    stage.done(grad_attn_held)
    tall_sum.far()
    grad_tokens, grad_attn_gain = token_grad(
        stage.enter(grad_attn_held), shuffle, normed_one, inverse_one, attn_gain, grad_residual
    )
    stage.done(grad_tokens)
    mixed = (residual + out_sum.total()).astype(BF)
    stage.done(mixed)
    tall_sum.near()
    (grad_route_down,) = grid.parts_of_both(stage.enter(down_mine), down_theirs, 1)
    stage.done(grad_route_down)
    wide_sum.far()
    shared_left, shared_right = stage.enter(joined("shared_pre"), joined("shared"))

    def rows_of(stacks):
        return jnp.concatenate([one.reshape(-1, model_width) for half in stacks.values() for one in half])

    grad_pieces = jnp.concatenate(
        [
            contract(shared_left, rows_of(ffn.halves), 0, 0),
            contract(shared_right, rows_of(others.halves), 0, 0),
            grad_attn_gain,
            grad_ffn_gain[None],
        ]
    )
    grad_pieces = grad_pieces.astype(BF)
    stage.done(grad_pieces)
    grad_pieces_there = swap(grad_pieces)
    grad_route_gate, grad_route_up = grid.parts_of_both(stage.enter(both_mine), both_theirs, 2)
    stage.done(grad_route_gate, grad_route_up)
    grad_pieces = grid.both_reps(stage.enter(grad_pieces), grad_pieces_there).astype(BF)
    grad_pieces = grad_pieces.T.reshape(groups, width, 3 * hidden + 2)
    stage.done(grad_pieces)
    grad_pieces = lax.all_to_all(grad_pieces, "grp", split_axis=0, concat_axis=0, tiled=True)
    wide_sum.near()
    grad_w_out = tall_sum.total().astype(BF)
    stage.done(grad_w_out)
    grad_w_out_there = swap(grad_w_out)
    grad_w_qkv = wide_sum.total().astype(BF)
    stage.done(grad_w_qkv)
    grad_w_qkv_there = swap(grad_w_qkv)
    grad_route_down, grad_route_gate, grad_route_up = (
        one[None] for one in (grad_route_down, grad_route_gate, grad_route_up)
    )

    grad_w_out = grid.both_reps(grad_w_out, grad_w_out_there).T
    grad_pieces = stage.enter(grad_pieces).astype(F32)
    grad_w_qkv = grid.both_reps(grad_w_qkv, grad_w_qkv_there)
    gain_grads = grad_pieces[:, :, 3 * hidden :].sum(axis=0)

    def join(part):
        return part.transpose(1, 0, 2).reshape(width, groups * hidden)

    grad_shared_gate = join(grad_pieces[:, :, :hidden])
    grad_shared_up = join(grad_pieces[:, :, hidden : 2 * hidden])
    grad_shared_down = join(grad_pieces[:, :, 2 * hidden : 3 * hidden]).T

    return (
        mixed,
        grad_tokens,
        gain_grads[:, 0],
        grad_w_qkv,
        grad_w_out,
        gain_grads[:, 1],
        grad_shared_gate,
        grad_shared_up,
        grad_shared_down,
        grad_route_gate,
        grad_route_up,
        grad_route_down,
    )


def solution(mesh):
    in_specs = (
        P(("rep", "grp"), None),
        P(("rep", "grp"), None),
        P(("rep", "grp"), None),
        P(("rep", "grp"), None),
        P("grp"),
        P("grp", None),
        P(None, "grp"),
        P("grp"),
        P("grp", None),
        P("grp", None),
        P(None, "grp"),
        P("grp", None, None),
        P("grp", None, None),
        P("grp", None, None),
        P(("rep", "grp"), None),
    )
    out_specs = (
        P(("rep", "grp"), None),
        P(("rep", "grp"), None),
        P("grp"),
        P("grp", None),
        P(None, "grp"),
        P("grp"),
        P("grp", None),
        P("grp", None),
        P(None, "grp"),
        P("grp", None, None),
        P("grp", None, None),
        P("grp", None, None),
    )
    return jax.shard_map(local, mesh=mesh, in_specs=in_specs, out_specs=out_specs, check_vma=False)
```

```python
import math

import jax
import jax.numpy as jnp
import numpy as np
from jax import lax
from jax.experimental import pallas as pl
from jax.experimental.pallas import tpu as pltpu
from jax.sharding import PartitionSpec as P

H = 10
HD = 128
HEADS_AT_ONCE = 10

EPSILON = 1e-06
MASKED_SCORE = -1000000000.0
BF = jnp.bfloat16
F32 = jnp.float32
BRIEF = pl.CostEstimate(flops=1, bytes_accessed=1, transcendentals=0)


def rms_scale(values):
    return lax.rsqrt(jnp.mean(values * values, axis=-1, keepdims=True) + EPSILON)


def rotary_tables(seq_len):
    half = HD // 2
    frequency = np.power(np.float32(10000.0), -2.0 * np.arange(half, dtype=np.float32) / HD)
    angle = np.arange(seq_len, dtype=np.float32)[:, None] * frequency.astype(np.float32)[None, :]
    cosine, sine = np.cos(angle), np.sin(angle)
    return np.stack(
        [np.concatenate([cosine, cosine], axis=1), np.concatenate([-sine, sine], axis=1)]
    ).astype(np.float32)


def contract(left, right, left_dim, right_dim):
    return lax.dot_general(
        left, right, (((left_dim,), (right_dim,)), ((), ())), preferred_element_type=F32
    )


def silu_slope(values):
    sigma = jax.nn.sigmoid(values)
    return sigma * (1.0 + values * (1.0 - sigma))


def norm_backward(grad_scaled, normed, inverse, gain):
    grad_normed = grad_scaled * gain
    grad_gain = jnp.sum(grad_scaled * normed, axis=0)
    grad_rows = inverse * (
        grad_normed - normed * jnp.mean(grad_normed * normed, axis=-1, keepdims=True)
    )
    return (grad_rows, grad_gain)


def after(value, *others):
    return lax.optimization_barrier((value,) + others)[0]


def attention_forward_kernel(q_in, k_in, v_in, table, doc_col, doc_row, q_ref, k_ref, v_ref, p_ref, o_ref):
    def turned(values):
        return (values * table[0] + pltpu.roll(values, HD // 2, 1) * table[1]).astype(BF)

    for n in range(HEADS_AT_ONCE):
        at = slice(n * HD, (n + 1) * HD)
        query, key, value = turned(q_in[:, at]), turned(k_in[:, at]), v_in[:, at].astype(BF)
        q_ref[:, at], k_ref[:, at], v_ref[:, at] = query, key, value
        scores = contract(query, key, 1, 1) / math.sqrt(HD)
        row = lax.broadcasted_iota(jnp.int32, scores.shape, 0)
        column = lax.broadcasted_iota(jnp.int32, scores.shape, 1)
        allowed = (row >= column) & (doc_col[...] == doc_row[...])
        scores = jnp.where(allowed, scores, MASKED_SCORE)
        raised = jnp.exp(scores - jnp.max(scores, axis=-1, keepdims=True))
        probs = raised / jnp.sum(raised, axis=-1, keepdims=True)
        p_ref[n] = probs
        o_ref[:, at] = contract(probs.astype(BF), value, 1, 0).astype(BF)


def attention_backward_kernel(g_ref, q_ref, k_ref, v_ref, p_ref, table, out_ref):
    def turned_back(values):
        return (values * table[0] - pltpu.roll(values, HD // 2, 1) * table[1]).astype(BF)

    def place(part, n):
        return slice((part * H + n) * HD, (part * H + n + 1) * HD)

    for n in range(H):
        at = place(0, n)
        grad, probs = g_ref[:, at], p_ref[n]
        grad_probs = contract(grad, v_ref[:, at], 1, 1)
        out_ref[:, place(2, n)] = contract(probs.astype(BF), grad, 0, 0).astype(BF)
        mean = jnp.sum(grad_probs * probs, axis=-1, keepdims=True)
        grad_scores = (probs * (grad_probs - mean)).astype(BF)
        out_ref[:, at] = turned_back(contract(grad_scores, k_ref[:, at], 1, 0) / math.sqrt(HD))
        out_ref[:, place(1, n)] = turned_back(contract(grad_scores, q_ref[:, at], 0, 0) / math.sqrt(HD))


def head_block(seq_len, offset=0):
    return pl.BlockSpec((seq_len, HEADS_AT_ONCE * HD), lambda h: (0, offset // HEADS_AT_ONCE + h))


def attention_forward(projected, table, documents):
    seq_len = projected.shape[0]
    row = jax.ShapeDtypeStruct((seq_len, H * HD), BF)
    probs_block = pl.BlockSpec((HEADS_AT_ONCE, seq_len, seq_len), lambda h: (h, 0, 0))
    return pl.pallas_call(
        attention_forward_kernel,
        grid=(H // HEADS_AT_ONCE,),
        in_specs=[
            head_block(seq_len),
            head_block(seq_len, H),
            head_block(seq_len, 2 * H),
            pl.BlockSpec((2, seq_len, HD), lambda h: (0, 0, 0)),
            pl.BlockSpec((seq_len, 1), lambda h: (0, 0)),
            pl.BlockSpec((1, seq_len), lambda h: (0, 0)),
        ],
        out_specs=[head_block(seq_len)] * 3 + [probs_block, head_block(seq_len)],
        out_shape=[row] * 3 + [jax.ShapeDtypeStruct((H, seq_len, seq_len), F32), row],
        cost_estimate=BRIEF,
        name="attention_forward",
    )(projected, projected, projected, table, documents.reshape(seq_len, 1), documents.reshape(1, seq_len))


def attention_backward(grad_heads, query, key, value, probs, table):
    seq_len = grad_heads.shape[0]
    return pl.pallas_call(
        attention_backward_kernel,
        out_shape=jax.ShapeDtypeStruct((seq_len, 3 * H * HD), BF),
        cost_estimate=BRIEF,
        name="attention_backward",
    )(grad_heads, query, key, value, probs, table)


def tile_of(first, columns):
    most = max(columns // 3, 640)
    return max(n for n in range(128, most + 1, 128) if columns % n == 0 and first % n == 0)


def held_product(left, blocks, first, columns, kind=F32):
    rows, depth = left.shape
    tile = tile_of(first, columns)

    def kernel(left_ref, *refs):
        whole = jnp.concatenate([one[...] for one in refs[:-1]], axis=0)
        refs[-1][...] = contract(left_ref[...], whole, 1, 0).astype(kind)

    return pl.pallas_call(
        kernel,
        grid=(columns // tile,),
        in_specs=[pl.BlockSpec((rows, depth), lambda n: (0, 0))]
        + [pl.BlockSpec((one.shape[0], tile), lambda n: (0, first // tile + n)) for one in blocks],
        out_specs=pl.BlockSpec((rows, tile), lambda n: (0, n)),
        out_shape=jax.ShapeDtypeStruct((rows, columns), kind),
        cost_estimate=BRIEF,
        name="held_product",
    )(left, *blocks)


def held_product_back(left, blocks, first):
    rows, columns = left.shape
    depth = sum(one.shape[0] for one in blocks)
    tile = tile_of(first, columns)

    def kernel(left_ref, *refs):
        whole = jnp.concatenate([one[...] for one in refs[:-1]], axis=0)
        product = contract(left_ref[...], whole, 1, 1)

        @pl.when(pl.program_id(0) == 0)
        def _():
            refs[-1][...] = product

        @pl.when(pl.program_id(0) > 0)
        def _():
            refs[-1][...] += product

    return pl.pallas_call(
        kernel,
        grid=(columns // tile,),
        in_specs=[pl.BlockSpec((rows, tile), lambda n: (0, n))]
        + [pl.BlockSpec((one.shape[0], tile), lambda n: (0, first // tile + n)) for one in blocks],
        out_specs=pl.BlockSpec((rows, depth), lambda n: (0, 0)),
        out_shape=jax.ShapeDtypeStruct((rows, depth), F32),
        cost_estimate=BRIEF,
        name="held_product_back",
    )(left, *blocks)


def token_grad(grad_held, shuffle, normed, inverse, gain, grad_rows):
    rows, width = normed.shape

    def kernel(held_ref, shuffle_ref, normed_ref, inverse_ref, gain_ref, rows_ref, out_ref, gain_grad_ref):
        held, unit = held_ref[...], normed_ref[...]
        high = held.astype(BF)
        low = (held - high.astype(F32)).astype(BF)
        grad = contract(high, shuffle_ref[...], 1, 0) + contract(low, shuffle_ref[...], 1, 0)
        gain_grad_ref[...] = jnp.sum(grad * unit, axis=0, keepdims=True)
        grad = grad * gain_ref[...]
        mean = jnp.sum(grad * unit, axis=-1, keepdims=True) / width
        out_ref[...] = (rows_ref[...] + inverse_ref[...] * (grad - unit * mean)).astype(BF)

    return pl.pallas_call(
        kernel,
        out_shape=[
            jax.ShapeDtypeStruct((rows, width), BF),
            jax.ShapeDtypeStruct((1, width), F32),
        ],
        cost_estimate=BRIEF,
        name="token_grad",
    )(grad_held, shuffle, normed, inverse, gain.reshape(1, width), grad_rows)


def sum_of_reps(mine, theirs, parts):
    rows, width = mine.shape
    size = width // parts
    tile = max(n for n in range(16, 257, 16) if rows % n == 0)

    def kernel(mine_ref, theirs_ref, *out_refs):
        for n, out_ref in enumerate(out_refs):
            at = slice(n * size, (n + 1) * size)
            out_ref[...] = mine_ref[:, at].astype(F32) + theirs_ref[:, at].astype(F32)

    return pl.pallas_call(
        kernel,
        grid=(rows // tile,),
        in_specs=[pl.BlockSpec((tile, width), lambda n: (n, 0))] * 2,
        out_specs=[pl.BlockSpec((tile, size), lambda n: (n, 0))] * parts,
        out_shape=[jax.ShapeDtypeStruct((rows, size), F32)] * parts,
        cost_estimate=BRIEF,
        name="sum_of_reps",
    )(mine, theirs)


class Order:
    def __init__(self):
        self.last = ()

    def enter(self, *values):
        held = lax.optimization_barrier(values + self.last)[: len(values)]
        return held[0] if len(values) == 1 else held

    def done(self, *values):
        self.last = values


class Rounds:
    def __init__(self, grid):
        self.grid = grid
        self.before = ()
        self.now = []

    def send(self, value, *move):
        arrived = self.grid.shift(after(value, *self.before), *move)
        self.now.append(arrived)
        return arrived

    def close(self):
        self.before, self.now = tuple(self.now), []


class Gather:
    def __init__(self, grid, rounds, block, merged):
        self.grid, self.rounds, self.merged = grid, rounds, merged
        self.held = {(0, 0, 0): block}
        self.halves = {}
        self.count = grid.z + grid.y + (1 if merged else 0) - 1 if grid.size > 1 else 0

    def round(self, r):
        grid, held = self.grid, self.held
        if r < grid.z - 1:
            held[(r + 1, 0, 0)] = self.rounds.send(held[(r, 0, 0)], 1, 0, 0)
        for j in range(grid.y - 1):
            if 0 <= r - j < grid.z:
                held[(r - j, j + 1, 0)] = self.rounds.send(held[(r - j, j, 0)], 0, 1, 0)
        if not self.merged:
            for j in range(grid.y):
                if 0 <= r - j < grid.z:
                    for k in range(1, grid.c):
                        held[(r - j, j, k)] = self.rounds.send(held[(r - j, j, k - 1)], 0, 0, 1)
            return
        for n, half in enumerate(grid.halves):
            if r == half[-1] + grid.y:
                stacks = [jnp.stack([held[place] for place in grid.places(half, 0)])]
                for _ in range(1, grid.c):
                    stacks.append(self.rounds.send(stacks[-1], 0, 0, 1))
                self.halves[n] = stacks


class Scatter:
    def __init__(self, grid, stage, half, make):
        self.grid, self.stage, self.make = grid, stage, make
        self.rows = len(half)

    def core(self):
        grid = self.grid
        if grid.c == 1:
            return
        total = self.make(grid.y * self.rows, grid.y * self.rows).astype(BF)
        self.stage.done(total)
        self.arrived = grid.shift(total, 0, 0, 1)

    def term(self, j):
        here = self.make(j * self.rows, self.rows)
        if self.grid.c > 1:
            here = here + self.arrived[j * self.rows : (j + 1) * self.rows].astype(F32)
        return here

    def along_y(self):
        grid = self.grid
        if grid.y == 1:
            return
        total = self.term(1).astype(BF)
        self.stage.done(total)
        self.total = grid.shift(total, 0, 1, 0)
        for j in range(2, grid.y):
            total = (self.term(j) + self.total.astype(F32)).astype(BF)
            self.stage.done(total)
            self.total = grid.shift(total, 0, 1, 0)

    def own(self):
        total = self.term(0)
        if self.grid.y > 1:
            total = total + self.total.astype(F32)
        total = total.astype(BF)
        self.stage.done(total)
        return total


class Grid:
    def __init__(self):
        self.size = lax.axis_size("grp")
        self.reps = lax.axis_size("rep")
        self.c = 2 if self.size % 2 == 0 else 1
        self.z = 4 if self.size % (4 * self.c) == 0 else 1
        self.y = self.size // (self.c * self.z)
        me = lax.axis_index("grp")
        self.my_c = me % self.c
        self.my_y = me // self.c % self.y
        self.my_z = me // (self.c * self.y)
        self.halves = ((0, 1), (2, 3)) if self.z == 4 else ((0,),)

    def flat(self, z, y, c):
        return (z % self.z * self.y + y % self.y) * self.c + c % self.c

    def shift(self, value, dz, dy, dc):
        pairs = [
            (self.flat(z, y, c), self.flat(z + dz, y + dy, c + dc))
            for z in range(self.z)
            for y in range(self.y)
            for c in range(self.c)
        ]
        return lax.ppermute(value, "grp", pairs)

    def source(self, step):
        return self.flat(
            self.my_z - step[0] + self.z, self.my_y - step[1] + self.y, self.my_c - step[2] + self.c
        )

    def places(self, half, k):
        return [(i, j, k) for j in range(self.y) for i in half]

    def order(self):
        return [
            place for half in self.halves for k in range(self.c) for place in self.places(half, k)
        ]

    def other_rep(self, value):
        if self.reps == 2:
            return lax.ppermute(value, "rep", [(0, 1), (1, 0)])
        return lax.psum(value, "rep")

    def parts_of_both(self, mine, theirs, parts):
        if self.reps == 2:
            return sum_of_reps(mine, theirs, parts)
        return [one.astype(F32) for one in jnp.split(theirs, parts, axis=1)]

    def both_reps(self, mine, theirs):
        if self.reps == 2:
            return mine.astype(F32) + theirs.astype(F32)
        return theirs.astype(F32)


def local(
    tokens,
    segments,
    routes,
    gates,
    gain_attn,
    w_qkv,
    w_out,
    gain_ffn,
    shared_gate,
    shared_up,
    shared_down,
    route_gate,
    route_up,
    route_down,
    cotangent,
):
    grid = Grid()
    seq_len, model_width = tokens.shape
    top_count = routes.shape[1]
    groups = grid.size
    expert_count = groups * route_gate.shape[0]
    capacity = 9 * seq_len * top_count // (8 * expert_count)
    slots = -(-capacity // 16) * 16
    hidden = shared_gate.shape[1] // groups
    width = gain_attn.shape[0]

    chosen = routes[:, :, None] == jnp.arange(expert_count, dtype=jnp.int32)[None, None, :]
    gate_table = jnp.sum(jnp.where(chosen, gates[:, :, None], 0.0), axis=1)
    gate_table = jnp.where(jnp.any(chosen, axis=1), gate_table, -1.0).T
    both_gains = jnp.concatenate([gain_attn, gain_ffn]).astype(F32)
    small = jnp.concatenate(
        [gate_table, jnp.broadcast_to(both_gains, (groups, 2 * width))], axis=1
    )
    small = lax.all_to_all(small, "grp", split_axis=0, concat_axis=0, tiled=True)

    sources = jnp.stack([grid.source(place) for place in grid.order()])
    held_feature = (sources[:, None] * width + jnp.arange(width, dtype=jnp.int32)[None, :]).reshape(-1)
    shuffle = (held_feature[:, None] == jnp.arange(model_width, dtype=jnp.int32)[None, :]).astype(BF)
    count = len(grid.halves)
    near = groups // count

    def chunk(values, n):
        size = values.shape[0] // count
        return values[n * size : (n + 1) * size]

    def to_held(values):
        return contract(values, shuffle, 1, 1).astype(BF)

    def from_held(values):
        high = lax.reduce_precision(values, 8, 7)
        both = jnp.concatenate([high.astype(BF), (values - high).astype(BF)])
        both = jnp.dot(both, shuffle, preferred_element_type=F32)
        return both[: values.shape[0]] + both[values.shape[0] :]

    rounds = Rounds(grid)
    qkv_width, inner = w_qkv.shape[1], w_out.shape[0]
    weights = Gather(grid, rounds, jnp.concatenate([w_qkv, w_out.T], axis=1), False)
    others = Gather(grid, rounds, cotangent, True)
    started = 0
    for r in range(weights.count):
        weights.round(r)
        if r >= grid.z:
            others.round(started)
            started += 1
        rounds.close()
        if r == 0:
            early = rounds.before
    blocks = [weights.held[place] for place in grid.order()]

    small = after(small, *early)
    attn_gain = small[:, seq_len : seq_len + width].reshape(-1)
    ffn_gain = small[:, seq_len + width :].reshape(-1)
    places = jnp.arange(seq_len, dtype=jnp.int32)
    gate_rows = small[:, :seq_len][sources]
    routed_here = gate_rows >= 0.0
    earlier = (places[:, None] < places[None, :]).astype(BF)
    position = jnp.dot(routed_here.astype(BF), earlier, preferred_element_type=F32)
    kept = routed_here & (position < capacity)
    gate_kept = jnp.where(kept, gate_rows, 0.0)
    hit = kept[:, None, :] & (
        position[:, None, :] == jnp.arange(slots, dtype=F32)[None, :, None]
    )
    slot_gate = jnp.sum(jnp.where(hit, gate_rows[:, None, :], 0.0), axis=-1)
    select = hit.astype(BF)
    expert_gate_w, expert_up_w, expert_down_w = route_gate[0], route_up[0], route_down[0]
    inside = expert_gate_w.shape[1]
    both_w = jnp.concatenate([after(expert_gate_w, *early), expert_up_w], axis=1)

    stage = Order()
    rows = after(tokens, *early).astype(F32)
    inverse_one = rms_scale(rows)
    normed_one = rows * inverse_one
    attn_in = (normed_one * attn_gain).astype(BF)
    attn_held, slot_gate, gate_kept, select, both_w = (
        lax.optimization_barrier(
            (to_held(attn_in), slot_gate, gate_kept, select, both_w)
        )
    )
    projected = held_product(attn_held, blocks, 0, qkv_width)
    table = jnp.asarray(rotary_tables(seq_len))

    def next_round(*held_back):
        nonlocal started
        if started < others.count:
            rounds.before += held_back
            others.round(started)
            started += 1
            rounds.close()

    next_round(projected)
    query, key, value, probs, attn_rows = attention_forward(projected, table, segments)
    next_round(attn_rows)
    residual = rows + from_held(held_product_back(attn_rows, blocks, qkv_width))
    inverse_two = rms_scale(residual)
    normed_two = residual * inverse_two
    ffn_in = (normed_two * ffn_gain).astype(BF)
    shared_gate, shared_up, shared_down = (
        after(one, ffn_in) for one in (shared_gate, shared_up, shared_down)
    )
    pieces = jnp.concatenate(
        [
            shared_gate.reshape(width, groups, hidden).transpose(1, 0, 2),
            shared_up.reshape(width, groups, hidden).transpose(1, 0, 2),
            shared_down.reshape(groups, hidden, width).transpose(0, 2, 1),
        ],
        axis=2,
    )
    pieces = lax.all_to_all(pieces, "grp", split_axis=0, concat_axis=0, tiled=True)
    pieces = pieces.reshape(model_width, 3 * hidden)

    stage.done(ffn_in)
    while started < others.count:
        next_round(ffn_in)
    rounds = Rounds(grid)
    ffn = Gather(grid, rounds, ffn_in, True)
    for r in range(ffn.count):
        ffn.round(r)
        rounds.close()

    def picked(selection, stacks):
        size = selection.shape[0] // len(stacks)
        return jnp.concatenate(
            [
                jnp.einsum(
                    "sct,std->scd",
                    selection[n * size : (n + 1) * size],
                    one,
                    preferred_element_type=F32,
                )
                for n, one in enumerate(stacks)
            ]
        )

    def each(stacks, right):
        return jnp.concatenate(
            [
                jnp.dot(one.reshape(-1, one.shape[2]), right, preferred_element_type=F32)
                for one in stacks
            ]
        )

    flat = (near * slots, model_width)

    def forward_part(n):
        selection = stage.enter(chunk(select, n))
        dy = others.halves[n]
        expert_in = picked(selection, ffn.halves[n]).astype(BF).reshape(flat)
        grad_out = picked(selection, dy) * chunk(slot_gate, n)[:, :, None]
        grad_out = grad_out.astype(BF).reshape(flat)
        both = jnp.dot(expert_in, both_w, preferred_element_type=F32)
        expert_hidden = (jax.nn.silu(both[:, :inside]) * both[:, inside:]).astype(BF)
        stage.done(both, expert_hidden, grad_out)
        return {"in": expert_in, "out": grad_out, "hidden": expert_hidden, "both": both}

    def backward_part(n, part):
        grad_out, both = stage.enter(part["out"], part["both"])
        gate_part, up_part = both[:, :inside], both[:, inside:]
        grad_hidden = contract(grad_out, expert_down_w, 1, 1)
        grad_both = jnp.concatenate(
            [
                (grad_hidden * up_part * silu_slope(gate_part)).astype(BF),
                (grad_hidden * jax.nn.silu(gate_part)).astype(BF),
            ],
            axis=1,
        )
        grad_both = after(grad_both)
        grad_in = contract(grad_both, both_w, 1, 1).astype(BF)
        if n == 0:
            held_pieces = after(pieces, grad_both)
            shared.extend([held_pieces[:, : 2 * hidden], held_pieces[:, 2 * hidden :]])
        shared_in, shared_back = shared
        shared_pre = each(ffn.halves[n], shared_in)
        gate_pre, up_pre = shared_pre[:, :hidden], shared_pre[:, hidden:]
        shared_silu = jax.nn.silu(gate_pre)
        grad_shared_hidden = each(others.halves[n], shared_back)
        grad_shared_pre = jnp.concatenate(
            [
                (grad_shared_hidden * up_pre * silu_slope(gate_pre)).astype(BF),
                (grad_shared_hidden * shared_silu).astype(BF),
            ],
            axis=1,
        )
        part["grad_both"] = grad_both
        part["shared"] = (shared_silu * up_pre).astype(BF)
        part["shared_pre"] = grad_shared_pre
        stage.done(grad_in, grad_shared_pre)
        return to_tokens(n, grad_in, None, grad_shared_pre, shared_in)

    def to_tokens(n, slot_rows, scale, shared_rows, shared_weight):
        slot_rows = slot_rows.reshape(near, slots, model_width)

        def make(first, size):
            mine = slice(first, first + size)
            selection = stage.enter(chunk(select, n)[mine])
            back = jnp.einsum(
                "sct,scd->std", selection, slot_rows[mine], preferred_element_type=F32
            )
            if scale is not None:
                back = back * scale[mine][:, :, None]
            shared_mine = shared_rows[first * seq_len : (first + size) * seq_len]
            return back + contract(shared_mine, shared_weight, 1, 1).reshape(back.shape)

        return Scatter(grid, stage, grid.halves[n], make)

    swap = grid.other_rep
    parts, backs, shared = [], [], []
    for n in range(count):
        parts.append(forward_part(n))
        if n:
            backs[n - 1].along_y()
        backs.append(backward_part(n, parts[n]))
        backs[n].core()

    def joined(key):
        return jnp.concatenate([part[key] for part in parts])

    class AlongZ:
        def __init__(self, halves):
            self.halves = halves

        def far(self):
            if grid.z == 4:
                far = self.halves[-1].own()
                self.whole = far
                self.passed_on = grid.shift(far[-2], 3, 0, 0)
                self.back_one = grid.shift(far[-1], 1, 0, 0)

        def near(self):
            if grid.z != 4:
                self.mine = self.halves[0].own()[0]
                return
            if len(self.halves) == 1:
                near = stage.enter(self.whole[1]).astype(F32) + self.passed_on.astype(F32)
                self.mine = self.whole[0].astype(F32) + self.back_one.astype(F32)
                self.back_one = None
                stage.done(self.mine)
                near = stage.enter(near)
            else:
                half = self.halves[0]
                total = half.term(0)
                near = after(stage.enter(total[1]) + self.passed_on.astype(F32))
                stage.done(near)
                self.mine = total[0]
                if grid.y > 1:
                    near = near + half.total[1].astype(F32)
                    self.mine = total[0] + half.total[0].astype(F32)
            near = near.astype(BF)
            stage.done(near)
            self.near_one = grid.shift(near, 3, 0, 0)

        def total(self):
            mine = stage.enter(self.mine).astype(F32)
            if grid.z == 4:
                if self.back_one is not None:
                    mine = mine + self.back_one.astype(F32)
                mine = mine + self.near_one.astype(F32)
            return mine

    down_left, down_right = stage.enter(joined("hidden"), joined("out"))
    down_mine = contract(down_left, down_right, 0, 0).astype(BF)
    stage.done(down_mine)
    down_theirs = swap(down_mine)
    backs[-1].along_y()
    both_left, both_right = stage.enter(joined("in"), joined("grad_both"))
    both_mine = contract(both_left, both_right, 0, 0).astype(BF)
    stage.done(both_mine)
    ffn_sum = AlongZ(backs)
    ffn_sum.far()

    outs = []
    for n in range(count):
        hidden_rows = stage.enter(parts[n]["hidden"])
        expert_out = jnp.dot(hidden_rows, expert_down_w, preferred_element_type=F32).astype(BF)
        stage.done(expert_out)
        outs.append(
            to_tokens(n, expert_out, chunk(gate_kept, n), parts[n]["shared"], shared[1])
        )
    for out in outs[::-1]:
        out.core()
    ffn_sum.near()
    for out in outs[::-1]:
        out.along_y()
    grad_ffn_in = ffn_sum.total()

    grad_norm_two, grad_ffn_gain = norm_backward(grad_ffn_in, normed_two, inverse_two, ffn_gain)
    grad_residual = cotangent.astype(F32) + grad_norm_two
    grad_attn_low = grad_residual.astype(BF)
    low_turned = contract(shuffle, grad_attn_low, 1, 1).astype(BF)
    grad_heads = held_product(low_turned.T, blocks, qkv_width, inner, BF)
    stage.done(grad_heads)

    def products(half, turned, right):
        def make(first, size):
            rows = turned[first * width : (first + size) * width]
            product = jnp.dot(stage.enter(rows), right, preferred_element_type=F32)
            return product.reshape(size, width, right.shape[1])

        return Scatter(grid, stage, half, make)

    everywhere = sum(grid.halves, ())
    merged = low_turned.reshape(count, grid.c, grid.y, len(everywhere) // count, width, seq_len)
    merged = merged.transpose(1, 2, 0, 3, 4, 5).reshape(model_width, seq_len)
    tall = products(everywhere, merged, attn_rows)
    out_sum, tall_sum = AlongZ(outs), AlongZ([tall])
    tall.core()
    both_theirs = swap(after(both_mine, down_theirs))
    grad_projected = attention_backward(stage.enter(grad_heads), query, key, value, probs, table)
    stage.done(grad_projected)
    turned_in = contract(shuffle, attn_in, 1, 1).astype(BF)
    wides = [products(half, chunk(turned_in, n), grad_projected) for n, half in enumerate(grid.halves)]
    wide_sum = AlongZ(wides)
    out_sum.far()
    tall.along_y()
    for wide in wides[::-1]:
        wide.core()
    out_sum.near()
    for wide in wides[::-1]:
        wide.along_y()
    grad_attn_held = held_product_back(stage.enter(grad_projected), blocks, 0)
    stage.done(grad_attn_held)
    tall_sum.far()
    grad_tokens, grad_attn_gain = token_grad(
        stage.enter(grad_attn_held), shuffle, normed_one, inverse_one, attn_gain, grad_residual
    )
    stage.done(grad_tokens)
    mixed = (residual + out_sum.total()).astype(BF)
    stage.done(mixed)
    tall_sum.near()
    (grad_route_down,) = grid.parts_of_both(stage.enter(down_mine), down_theirs, 1)
    stage.done(grad_route_down)
    wide_sum.far()
    shared_left, shared_right = stage.enter(joined("shared_pre"), joined("shared"))

    def rows_of(stacks):
        return jnp.concatenate([one.reshape(-1, model_width) for half in stacks.values() for one in half])

    grad_pieces = jnp.concatenate(
        [
            contract(shared_left, rows_of(ffn.halves), 0, 0),
            contract(shared_right, rows_of(others.halves), 0, 0),
            grad_attn_gain,
            grad_ffn_gain[None],
        ]
    )
    grad_pieces = grad_pieces.astype(BF)
    stage.done(grad_pieces)
    grad_pieces_there = swap(grad_pieces)
    grad_route_gate, grad_route_up = grid.parts_of_both(stage.enter(both_mine), both_theirs, 2)
    stage.done(grad_route_gate, grad_route_up)
    grad_pieces = grid.both_reps(stage.enter(grad_pieces), grad_pieces_there).astype(BF)
    grad_pieces = grad_pieces.T.reshape(groups, width, 3 * hidden + 2)
    stage.done(grad_pieces)
    grad_pieces = lax.all_to_all(grad_pieces, "grp", split_axis=0, concat_axis=0, tiled=True)
    wide_sum.near()
    grad_w_out = tall_sum.total().astype(BF)
    stage.done(grad_w_out)
    grad_w_out_there = swap(grad_w_out)
    grad_w_qkv = wide_sum.total().astype(BF)
    stage.done(grad_w_qkv)
    grad_w_qkv_there = swap(grad_w_qkv)
    grad_route_down, grad_route_gate, grad_route_up = (
        one[None] for one in (grad_route_down, grad_route_gate, grad_route_up)
    )

    grad_w_out = grid.both_reps(grad_w_out, grad_w_out_there).T
    grad_pieces = stage.enter(grad_pieces).astype(F32)
    grad_w_qkv = grid.both_reps(grad_w_qkv, grad_w_qkv_there)
    gain_grads = grad_pieces[:, :, 3 * hidden :].sum(axis=0)

    def join(part):
        return part.transpose(1, 0, 2).reshape(width, groups * hidden)

    grad_shared_gate = join(grad_pieces[:, :, :hidden])
    grad_shared_up = join(grad_pieces[:, :, hidden : 2 * hidden])
    grad_shared_down = join(grad_pieces[:, :, 2 * hidden : 3 * hidden]).T

    return (
        mixed,
        grad_tokens,
        gain_grads[:, 0],
        grad_w_qkv,
        grad_w_out,
        gain_grads[:, 1],
        grad_shared_gate,
        grad_shared_up,
        grad_shared_down,
        grad_route_gate,
        grad_route_up,
        grad_route_down,
    )


def solution(mesh):
    in_specs = (
        P(("rep", "grp"), None),
        P(("rep", "grp"), None),
        P(("rep", "grp"), None),
        P(("rep", "grp"), None),
        P("grp"),
        P("grp", None),
        P(None, "grp"),
        P("grp"),
        P("grp", None),
        P("grp", None),
        P(None, "grp"),
        P("grp", None, None),
        P("grp", None, None),
        P("grp", None, None),
        P(("rep", "grp"), None),
    )
    out_specs = (
        P(("rep", "grp"), None),
        P(("rep", "grp"), None),
        P("grp"),
        P("grp", None),
        P(None, "grp"),
        P("grp"),
        P("grp", None),
        P("grp", None),
        P(None, "grp"),
        P("grp", None, None),
        P("grp", None, None),
        P("grp", None, None),
    )
    return jax.shard_map(local, mesh=mesh, in_specs=in_specs, out_specs=out_specs, check_vma=False)
```
